512 devices in a mesh: sta: 64 (over y, x, z_hi), win: 8 (over z_lo, core).
Axes of the slice: x: 4, y: 8, z: 8 (z_hi: 2, z_lo: 4; z = z_hi * 4 + z_lo), core: 2. Of those that a mesh axis runs over, the one named last changes fastest.
Arguments:
- spectra: float32 [16, 256, 2, 3, 1664], P('win', 'sta')
- flags: int32 [16, 256], P('win', 'sta'), may hold values 0 or 1
- owners: int32 [4], replicated, may hold values from 0 to 63, as said below
- source_slots: int32 [4, 4], replicated, may hold values from 0 to 3, as said below
Outputs:
- correlations: float32 [4, 4, 3, 256, 3, 768], P(None, None, None, 'sta')
The draws below stay inside these ranges and needn't reach their ends.
Inputs may be any that keep to these rules, and one draw needn't show every extreme that they name: `owners`: the index of a block of 4 stations along sta. `source_slots`: distinct within a step.
All inputs are finite; a program needn't handle non-finite values. No bound on the sum of `flags` on one device may be relied on, other than what follows from the above.
Results may differ from the reference program's by a relative error of at most 0.0037.
Values sent between devices are 32-bit elements; how exact they have to be, the bound alone decides.
A program may use at most 64 MiB of HBM per device.

```python
import math
import jax
import jax.numpy as jnp
from jax import lax

NF = 1664
NLAG = 768
SRC = 4
STEPS = 4
WIN_DEV = 2
REC_DEV = 4
STATIONS = 256
WINDOWS = 16
N_WIN = 8


def draw_spectra(key, part):
    first, second, third = jax.random.split(key, 3)
    shape = (WINDOWS, STATIONS, 2, 3, NF)
    station_scale = jnp.exp(jax.random.uniform(first, (1, STATIONS, 1, 1, 1), jnp.float32, 0.0, math.log(10.0)))
    bin_scale = jnp.exp(jax.random.uniform(second, (WINDOWS, STATIONS, 1, 3, NF), jnp.float32, -1.2, 1.2))
    base = jax.random.normal(third, shape, jnp.float32)
    return base * bin_scale * station_scale


def draw_owners(key, part):
    blocks = STATIONS // REC_DEV
    first, second = jax.random.split(jax.random.fold_in(key, 11))
    picks = jax.random.randint(first, (STEPS,), 0, blocks)
    order = jax.random.permutation(second, STEPS)
    picks = picks.at[order[0]].set(blocks - 1)
    return picks.at[order[1]].set(0).astype(jnp.int32)


def draw_source_slots(key, part):
    rows = []
    for step in range(STEPS):
        step_key = jax.random.fold_in(key, 100 + step)
        first, second = jax.random.split(step_key)
        perm = jax.random.permutation(first, REC_DEV).astype(jnp.int32)
        target = REC_DEV - 1 if step % 2 == 0 else 0
        head = perm[:SRC]
        present = jnp.any(head == target)
        position = jax.random.randint(second, (), 0, SRC)
        replaced = head.at[position].set(target)
        rows.append(jnp.where(present, head, replaced))
    return jnp.stack(rows).astype(jnp.int32)


def place_ends(drawn, stream_key, low, largest):
    longest = drawn.shape.index(max(drawn.shape))
    spots = []
    for shift in (0, 1):
        where = [jax.random.randint(jax.random.fold_in(stream_key, axis), (), 0, length) for axis, length in enumerate(drawn.shape)]
        where[longest] = (where[longest] + shift) % drawn.shape[longest]
        spots.append(tuple(where))
    return drawn.at[spots[0]].set(low).at[spots[1]].set(largest)


def setup_inputs(seed: int = 0) -> dict:
    key_of = jax.random.split(jax.random.key(seed), 5)
    spectra = draw_spectra(jax.random.fold_in(key_of[4], 71), 0)
    flags = place_ends((jax.random.randint(key_of[1], (WINDOWS, STATIONS), 0, 4) < 3).astype(jnp.int32), jax.random.fold_in(key_of[1], 1), 0, 1)
    owners = draw_owners(jax.random.fold_in(key_of[4], 71), 0)
    source_slots = draw_source_slots(jax.random.fold_in(key_of[4], 71), 0)
    return {"spectra": spectra, "flags": flags, "owners": owners, "source_slots": source_slots}


def whiten(spectra):
    shape = spectra.shape
    blocks = spectra.reshape(shape[0], shape[1], 2, 3, shape[4] // 64, 64)
    power = lax.optimization_barrier(jnp.mean(blocks * blocks, axis=(2, 3, 5), keepdims=True))
    return (blocks / jnp.sqrt(power + 1e-06)).reshape(shape)

def lag_table(bins, lags, windows):
    freq = jnp.arange(bins, dtype=jnp.int32) + 360
    shift = jnp.arange(lags, dtype=jnp.int32) - lags // 2
    phase = jnp.mod(freq[:, None] * shift[None, :], 7200).astype(jnp.float32) * (2.0 * math.pi / 7200.0)
    scale = 1.0 / math.sqrt(windows * bins)
    return jnp.concatenate([jnp.cos(phase) * scale, -jnp.sin(phase) * scale], axis=0).astype(jnp.bfloat16)

def correlate(picked, receivers, table):
    src_re = picked[:, :, 0][:, :, :, None, None, :]
    src_im = picked[:, :, 1][:, :, :, None, None, :]
    rec_re = receivers[:, :, 0][:, None, None, :, :, :]
    rec_im = receivers[:, :, 1][:, None, None, :, :, :]
    real = lax.optimization_barrier(jnp.sum(src_re * rec_re + src_im * rec_im, axis=0))
    imag = lax.optimization_barrier(jnp.sum(src_im * rec_re - src_re * rec_im, axis=0))
    shape = real.shape
    bins = shape[4]
    rows = jnp.concatenate([real.reshape(-1, bins), imag.reshape(-1, bins)], axis=1).astype(jnp.bfloat16)
    lagged = jnp.dot(rows, table, preferred_element_type=jnp.float32)
    return lagged.reshape(shape[0], shape[1], shape[2], shape[3], table.shape[1])

def reference(spectra, flags, owners, source_slots):
    whitened = whiten(spectra)
    weighted = whitened * flags.astype(jnp.float32)[:, :, None, None, None]
    table = lag_table(NF, NLAG, WINDOWS)
    results = []
    for step in range(STEPS):
        stations = (owners[step] * REC_DEV + source_slots[step]).astype(jnp.int32)
        picked = jnp.take(weighted, stations, axis=1)
        total = jnp.zeros((SRC, 3, STATIONS, 3, NLAG), jnp.float32)
        for group in range(N_WIN):
            low = group * WIN_DEV
            total = total + correlate(picked[low:low + WIN_DEV], weighted[low:low + WIN_DEV], table)
        results.append(total)
    return jnp.stack(results)
```

```python
import math

import jax
import jax.numpy as jnp
from jax import lax
from jax.sharding import Mesh
from jax.sharding import PartitionSpec as P

NLAG = 768
STEPS = 4
STA = ("y", "x", "zh")
WIN = ("zl", "c")


def fine_mesh(mesh):
    devs = mesh.devices
    n_sta, n_win = devs.shape
    col = devs[:, 0]
    ny = len({d.coords[1] for d in col})
    nx = len({d.coords[0] for d in col})
    nzh = n_sta // (ny * nx)
    nc = len({d.core_on_chip for d in devs[0, :]})
    nzl = n_win // nc
    return Mesh(devs.reshape(ny, nx, nzh, nzl, nc), STA + WIN)


def whiten(spectra):
    shape = spectra.shape
    blocks = spectra.reshape(shape[0], shape[1], 2, 3, shape[4] // 64, 64)
    power = jnp.mean(blocks * blocks, axis=(2, 3, 5), keepdims=True)
    return (blocks / jnp.sqrt(power + 1e-06)).reshape(shape)


def lag_table(bins, lags, windows):
    freq = jnp.arange(bins, dtype=jnp.int32) + 360
    shift = jnp.arange(lags, dtype=jnp.int32) - lags // 2
    phase = jnp.mod(freq[:, None] * shift[None, :], 7200).astype(jnp.float32) * (
        2.0 * math.pi / 7200.0
    )
    scale = 1.0 / math.sqrt(windows * bins)
    return jnp.concatenate([jnp.cos(phase) * scale, -jnp.sin(phase) * scale], axis=0).astype(
        jnp.bfloat16
    )


def correlate(picked, receivers, table):
    src_re = picked[:, :, 0][:, :, :, None, None, :]
    src_im = picked[:, :, 1][:, :, :, None, None, :]
    rec_re = receivers[:, :, 0][:, None, None, :, :, :]
    rec_im = receivers[:, :, 1][:, None, None, :, :, :]
    real = jnp.sum(src_re * rec_re + src_im * rec_im, axis=0)
    imag = jnp.sum(src_im * rec_re - src_re * rec_im, axis=0)
    shape = real.shape
    bins = shape[4]
    rows = jnp.concatenate([real.reshape(-1, bins), imag.reshape(-1, bins)], axis=1).astype(
        jnp.bfloat16
    )
    lagged = jnp.dot(rows, table, preferred_element_type=jnp.float32)
    return lagged.reshape(shape[0], shape[1], shape[2], shape[3], table.shape[1])


def on_device(spectra, flags, owners, source_slots):
    win_count = spectra.shape[0]
    bins = spectra.shape[4]
    weighted = whiten(spectra) * flags.astype(jnp.float32)[:, :, None, None, None]
    n_win = lax.axis_size(WIN)
    table = lag_table(bins, NLAG, win_count * n_win)
    me = lax.axis_index(STA)
    chosen = []
    for step in range(STEPS):
        block = jnp.take(weighted, source_slots[step], axis=1)
        chosen.append(jnp.where(me == owners[step], block, 0.0))
    picked_all = jnp.stack(chosen)
    for axis in ("zh", "x", "y"):
        picked_all = lax.psum(picked_all, axis)
    outputs = []
    for step in range(STEPS):
        outputs.append(correlate(picked_all[step], weighted, table))
    stacked = jnp.stack(outputs)
    for axis in ("c", "zl"):
        stacked = lax.psum(stacked, axis)
    return stacked


def solution(mesh):
    fine = fine_mesh(mesh)
    return jax.shard_map(
        on_device,
        mesh=fine,
        in_specs=(P(WIN, STA, None, None, None), P(WIN, STA), P(), P()),
        out_specs=P(None, None, None, STA, None, None),
        check_vma=False,
    )
```

```python
import math

import jax
import jax.numpy as jnp
from jax import lax
from jax.sharding import Mesh
from jax.sharding import PartitionSpec as P

NLAG = 768
STEPS = 4
STA = ("y", "x", "zh")
WIN = ("zl", "c")


def fine_mesh(mesh):
    devs = mesh.devices
    n_sta, n_win = devs.shape
    col = devs[:, 0]
    ny = len({d.coords[1] for d in col})
    nx = len({d.coords[0] for d in col})
    nzh = n_sta // (ny * nx)
    nc = len({d.core_on_chip for d in devs[0, :]})
    nzl = n_win // nc
    return Mesh(devs.reshape(ny, nx, nzh, nzl, nc), STA + WIN)


def a2a_sum(x, axes, n):
    parts = lax.all_to_all(x.reshape(n, -1), axes, 0, 0, tiled=True)
    return jnp.sum(parts.reshape(n, -1), axis=0)


def a2a_gather(x, axes, n):
    return lax.all_to_all(jnp.broadcast_to(x[None], (n, x.shape[0])), axes, 0, 0, tiled=True)


def broadcast_owner(masked):
    plane = ("y", "x")
    n = lax.axis_size(plane)
    piece = a2a_sum(masked, plane, n)
    piece = piece + lax.ppermute(piece, "zh", [(0, 1), (1, 0)])
    return a2a_gather(piece, plane, n).reshape(masked.shape)


def sum_over(x, axis, inner):
    n = lax.axis_size(axis)
    part = a2a_sum(x, axis, n)
    if inner is not None:
        part = sum_over_inner(part, inner)
    return a2a_gather(part, axis, n).reshape(x.shape)


def sum_over_inner(x, axis):
    n = lax.axis_size(axis)
    part = a2a_sum(x, axis, n)
    return a2a_gather(part, axis, n).reshape(x.shape)


def whiten(spectra):
    shape = spectra.shape
    blocks = spectra.reshape(shape[0], shape[1], 2, 3, shape[4] // 64, 64)
    power = jnp.mean(blocks * blocks, axis=(2, 3, 5), keepdims=True)
    return (blocks / jnp.sqrt(power + 1e-06)).reshape(shape)


def lag_table(bins, lags, windows):
    freq = jnp.arange(bins, dtype=jnp.int32) + 360
    shift = jnp.arange(lags, dtype=jnp.int32) - lags // 2
    phase = jnp.mod(freq[:, None] * shift[None, :], 7200).astype(jnp.float32) * (
        2.0 * math.pi / 7200.0
    )
    scale = 1.0 / math.sqrt(windows * bins)
    return jnp.concatenate([jnp.cos(phase) * scale, -jnp.sin(phase) * scale], axis=0).astype(
        jnp.bfloat16
    )


def correlate(picked, receivers, table):
    src_re = picked[:, :, 0][:, :, :, None, None, :]
    src_im = picked[:, :, 1][:, :, :, None, None, :]
    rec_re = receivers[:, :, 0][:, None, None, :, :, :]
    rec_im = receivers[:, :, 1][:, None, None, :, :, :]
    real = jnp.sum(src_re * rec_re + src_im * rec_im, axis=0)
    imag = jnp.sum(src_im * rec_re - src_re * rec_im, axis=0)
    shape = real.shape
    bins = shape[4]
    rows = jnp.concatenate([real.reshape(-1, bins), imag.reshape(-1, bins)], axis=1).astype(
        jnp.bfloat16
    )
    lagged = jnp.dot(rows, table, preferred_element_type=jnp.float32)
    return lagged.reshape(shape[0], shape[1], shape[2], shape[3], table.shape[1])


def on_device(spectra, flags, owners, source_slots):
    win_count = spectra.shape[0]
    bins = spectra.shape[4]
    weighted = whiten(spectra) * flags.astype(jnp.float32)[:, :, None, None, None]
    n_win = lax.axis_size(WIN)
    table = lag_table(bins, NLAG, win_count * n_win)
    me = lax.axis_index(STA)
    chosen = []
    for step in range(STEPS):
        block = jnp.take(weighted, source_slots[step], axis=1)
        chosen.append(jnp.where(me == owners[step], block, 0.0))
    picked_all = jnp.stack(chosen)
    picked_all = broadcast_owner(picked_all)
    outputs = []
    for step in range(STEPS):
        outputs.append(correlate(picked_all[step], weighted, table))
    stacked = jnp.stack(outputs)
    return sum_over(stacked, "c", "zl")


def solution(mesh):
    fine = fine_mesh(mesh)
    return jax.shard_map(
        on_device,
        mesh=fine,
        in_specs=(P(WIN, STA, None, None, None), P(WIN, STA), P(), P()),
        out_specs=P(None, None, None, STA, None, None),
        check_vma=False,
    )
```

```python
import math

import jax
import jax.numpy as jnp
from jax import lax
from jax.experimental import pallas as pl
from jax.experimental.pallas import tpu as pltpu
from jax.sharding import Mesh
from jax.sharding import PartitionSpec as P

NLAG = 768
STEPS = 4
STA = ("y", "x", "zh")
WIN = ("zl", "c")


def fine_mesh(mesh):
    devs = mesh.devices
    n_sta, n_win = devs.shape
    col = devs[:, 0]
    ny = len({d.coords[1] for d in col})
    nx = len({d.coords[0] for d in col})
    nzh = n_sta // (ny * nx)
    nc = len({d.core_on_chip for d in devs[0, :]})
    nzl = n_win // nc
    return Mesh(devs.reshape(ny, nx, nzh, nzl, nc), STA + WIN)


def a2a_sum(x, axes, n):
    parts = lax.all_to_all(x.reshape(n, -1), axes, 0, 0, tiled=True)
    return jnp.sum(parts.reshape(n, -1), axis=0)


def a2a_gather(x, axes, n):
    return lax.all_to_all(jnp.broadcast_to(x[None], (n, x.shape[0])), axes, 0, 0, tiled=True)


def broadcast_owner(masked):
    plane = ("y", "x")
    n = lax.axis_size(plane)
    piece = a2a_sum(masked, plane, n)
    piece = piece + lax.ppermute(piece, "zh", [(0, 1), (1, 0)])
    return a2a_gather(piece, plane, n).reshape(masked.shape)


def sum_over(x, axis, inner):
    n = lax.axis_size(axis)
    part = a2a_sum(x, axis, n)
    if inner is not None:
        part = sum_over_inner(part, inner)
    return a2a_gather(part, axis, n).reshape(x.shape)


def sum_over_inner(x, axis):
    n = lax.axis_size(axis)
    part = a2a_sum(x, axis, n)
    return a2a_gather(part, axis, n).reshape(x.shape)


def whiten(spectra):
    shape = spectra.shape
    blocks = spectra.reshape(shape[0], shape[1], 2, 3, shape[4] // 64, 64)
    power = jnp.mean(blocks * blocks, axis=(2, 3, 5), keepdims=True)
    return (blocks / jnp.sqrt(power + 1e-06)).reshape(shape)


def lag_table_fast(bins, lags, windows):
    freq = jnp.arange(bins, dtype=jnp.int32) + 360
    q = jnp.arange(lags // 128, dtype=jnp.int32) * 128 - lags // 2
    k = jnp.arange(128, dtype=jnp.int32)
    unit = 2.0 * math.pi / 7200.0
    a = jnp.mod(freq[:, None] * q[None, :], 7200).astype(jnp.float32) * unit
    b = jnp.mod(freq[:, None] * k[None, :], 7200).astype(jnp.float32) * unit
    ca, sa = jnp.cos(a)[:, :, None], jnp.sin(a)[:, :, None]
    cb, sb = jnp.cos(b)[:, None, :], jnp.sin(b)[:, None, :]
    scale = 1.0 / math.sqrt(windows * bins)
    cos = ((ca * cb - sa * sb) * scale).reshape(bins, lags)
    sin = ((sa * cb + ca * sb) * scale).reshape(bins, lags)
    return jnp.stack([cos, -sin]).astype(jnp.bfloat16)


def corr_kernel(src_ref, rec_ref, tab_ref, out_ref, rows_ref):
    n_win = src_ref.shape[1]
    n_src = src_ref.shape[2]
    n_cmp = src_ref.shape[4]
    n_rows = rec_ref.shape[2]
    for s in range(n_src):
        for i in range(n_cmp):
            acc_re = None
            acc_im = None
            for w in range(n_win):
                sre = src_ref[0, w, s, 0, pl.ds(i, 1), :]
                sim = src_ref[0, w, s, 1, pl.ds(i, 1), :]
                rre = rec_ref[w, 0]
                rim = rec_ref[w, 1]
                re = sre * rre + sim * rim
                im = sim * rre - sre * rim
                acc_re = re if acc_re is None else acc_re + re
                acc_im = im if acc_im is None else acc_im + im
            row = (s * n_cmp + i) * n_rows
            rows_ref[0, pl.ds(row, n_rows), :] = acc_re.astype(jnp.bfloat16)
            rows_ref[1, pl.ds(row, n_rows), :] = acc_im.astype(jnp.bfloat16)
    out_ref[0] = jnp.dot(rows_ref[0], tab_ref[0], preferred_element_type=jnp.float32) + jnp.dot(
        rows_ref[1], tab_ref[1], preferred_element_type=jnp.float32
    )


def correlate_all(picked_all, rec, table):
    steps, n_win, n_src, _, n_cmp, bins = picked_all.shape
    n_rows = rec.shape[2]
    lags = table.shape[2]
    m = n_src * n_cmp * n_rows
    return pl.pallas_call(
        corr_kernel,
        grid=(steps,),
        in_specs=[
            pl.BlockSpec((1, n_win, n_src, 2, n_cmp, bins), lambda t: (t, 0, 0, 0, 0, 0)),
            pl.BlockSpec(rec.shape, lambda t: (0, 0, 0, 0)),
            pl.BlockSpec(table.shape, lambda t: (0, 0, 0)),
        ],
        out_specs=pl.BlockSpec((1, m, lags), lambda t: (t, 0, 0)),
        out_shape=jax.ShapeDtypeStruct((steps, m, lags), jnp.float32),
        scratch_shapes=[pltpu.VMEM((2, m, bins), jnp.bfloat16)],
    )(picked_all, rec, table)


def on_device(spectra, flags, owners, source_slots):
    win_count = spectra.shape[0]
    bins = spectra.shape[4]
    weighted = whiten(spectra) * flags.astype(jnp.float32)[:, :, None, None, None]
    n_win = lax.axis_size(WIN)
    table = lag_table_fast(bins, NLAG, win_count * n_win)
    me = lax.axis_index(STA)
    chosen = []
    for step in range(STEPS):
        block = jnp.take(weighted, source_slots[step], axis=1)
        chosen.append(jnp.where(me == owners[step], block, 0.0))
    picked_all = jnp.stack(chosen)
    picked_all = broadcast_owner(picked_all)
    shape = weighted.shape
    rec = weighted.transpose(0, 2, 1, 3, 4).reshape(shape[0], 2, shape[1] * shape[3], shape[4])
    stacked = correlate_all(picked_all, rec, table).reshape(
        STEPS, shape[1], shape[3], shape[1], shape[3], NLAG
    )
    return sum_over(stacked, "c", "zl")


def solution(mesh):
    fine = fine_mesh(mesh)
    return jax.shard_map(
        on_device,
        mesh=fine,
        in_specs=(P(WIN, STA, None, None, None), P(WIN, STA), P(), P()),
        out_specs=P(None, None, None, STA, None, None),
        check_vma=False,
    )
```

```python
import math

import jax
import jax.numpy as jnp
from jax import lax
from jax.experimental import pallas as pl
from jax.experimental.pallas import tpu as pltpu
from jax.sharding import Mesh
from jax.sharding import PartitionSpec as P

NLAG = 768
STEPS = 4
MESH_ID = pl.DeviceIdType.MESH
STA = ("y", "x", "zh")
WIN = ("zl", "c")


def fine_mesh(mesh):
    devs = mesh.devices
    n_sta, n_win = devs.shape
    col = devs[:, 0]
    ny = len({d.coords[1] for d in col})
    nx = len({d.coords[0] for d in col})
    nzh = n_sta // (ny * nx)
    nc = len({d.core_on_chip for d in devs[0, :]})
    nzl = n_win // nc
    return Mesh(devs.reshape(ny, nx, nzh, nzl, nc), STA + WIN)


def a2a_sum(x, axes, n):
    parts = lax.all_to_all(x.reshape(n, -1), axes, 0, 0, tiled=True)
    return jnp.sum(parts.reshape(n, -1), axis=0)


def a2a_gather(x, axes, n):
    return lax.all_to_all(jnp.broadcast_to(x[None], (n, x.shape[0])), axes, 0, 0, tiled=True)


def broadcast_owner(masked):
    plane = ("y", "x")
    n = lax.axis_size(plane)
    piece = a2a_sum(masked, plane, n)
    piece = piece + lax.ppermute(piece, "zh", [(0, 1), (1, 0)])
    return a2a_gather(piece, plane, n).reshape(masked.shape)


def whiten(spectra):
    shape = spectra.shape
    blocks = spectra.reshape(shape[0], shape[1], 2, 3, shape[4] // 64, 64)
    power = jnp.mean(blocks * blocks, axis=(2, 3, 5), keepdims=True)
    return (blocks / jnp.sqrt(power + 1e-06)).reshape(shape)


def lag_table_fast(bins, lags, windows):
    freq = jnp.arange(bins, dtype=jnp.int32) + 360
    q = jnp.arange(lags // 128, dtype=jnp.int32) * 128 - lags // 2
    k = jnp.arange(128, dtype=jnp.int32)
    unit = 2.0 * math.pi / 7200.0
    a = jnp.mod(freq[:, None] * q[None, :], 7200).astype(jnp.float32) * unit
    b = jnp.mod(freq[:, None] * k[None, :], 7200).astype(jnp.float32) * unit
    ca, sa = jnp.cos(a)[:, :, None], jnp.sin(a)[:, :, None]
    cb, sb = jnp.cos(b)[:, None, :], jnp.sin(b)[:, None, :]
    scale = 1.0 / math.sqrt(windows * bins)
    cos = ((ca * cb - sa * sb) * scale).reshape(bins, lags)
    sin = ((sa * cb + ca * sb) * scale).reshape(bins, lags)
    return jnp.stack([cos, -sin]).astype(jnp.bfloat16)


def corr_kernel(src_ref, rec_ref, tab_ref, out_ref, rows_ref):
    n_win = src_ref.shape[1]
    n_src = src_ref.shape[2]
    n_cmp = src_ref.shape[4]
    n_rows = rec_ref.shape[2]
    for s in range(n_src):
        for i in range(n_cmp):
            acc_re = None
            acc_im = None
            for w in range(n_win):
                sre = src_ref[0, w, s, 0, pl.ds(i, 1), :]
                sim = src_ref[0, w, s, 1, pl.ds(i, 1), :]
                rre = rec_ref[w, 0]
                rim = rec_ref[w, 1]
                re = sre * rre + sim * rim
                im = sim * rre - sre * rim
                acc_re = re if acc_re is None else acc_re + re
                acc_im = im if acc_im is None else acc_im + im
            row = (s * n_cmp + i) * n_rows
            rows_ref[0, pl.ds(row, n_rows), :] = acc_re.astype(jnp.bfloat16)
            rows_ref[1, pl.ds(row, n_rows), :] = acc_im.astype(jnp.bfloat16)
    out_ref[0] = jnp.dot(rows_ref[0], tab_ref[0], preferred_element_type=jnp.float32) + jnp.dot(
        rows_ref[1], tab_ref[1], preferred_element_type=jnp.float32
    )


def correlate_all(picked_all, rec, table):
    steps, n_win, n_src, _, n_cmp, bins = picked_all.shape
    n_rows = rec.shape[2]
    lags = table.shape[2]
    m = n_src * n_cmp * n_rows
    return pl.pallas_call(
        corr_kernel,
        grid=(steps,),
        in_specs=[
            pl.BlockSpec((1, n_win, n_src, 2, n_cmp, bins), lambda t: (t, 0, 0, 0, 0, 0)),
            pl.BlockSpec(rec.shape, lambda t: (0, 0, 0, 0)),
            pl.BlockSpec(table.shape, lambda t: (0, 0, 0)),
        ],
        out_specs=pl.BlockSpec((1, m, lags), lambda t: (t, 0, 0)),
        out_shape=jax.ShapeDtypeStruct((steps, m, lags), jnp.float32),
        scratch_shapes=[pltpu.VMEM((2, m, bins), jnp.bfloat16)],
    )(picked_all, rec, table)


def win_sum_kernel(x_ref, out_ref, a1, a2, r1, r2, r3, send_sem, recv_sem):
    rows = x_ref.shape[0]
    h, q, e = rows // 2, rows // 4, rows // 8
    coords = [lax.axis_index(a) for a in STA + WIN]
    zl, c = coords[3], coords[4]
    b1 = zl % 2
    b2 = zl // 2
    peer_c = tuple(coords[:4]) + (1 - c,)
    peer_1 = tuple(coords[:3]) + (zl + 1 - 2 * b1, c)
    peer_2 = tuple(coords[:3]) + (zl + 2 - 4 * b2, c)

    barrier = pltpu.get_barrier_semaphore()
    for peer in (peer_c, peer_1, peer_2):
        pl.semaphore_signal(barrier, inc=1, device_id=peer, device_id_type=MESH_ID)
    pl.semaphore_wait(barrier, 3)

    def copy(src, dst, k, peer):
        return pltpu.make_async_remote_copy(
            src_ref=src, dst_ref=dst, send_sem=send_sem.at[k], recv_sem=recv_sem.at[k],
            device_id=peer, device_id_type=MESH_ID)

    mine1 = pl.multiple_of(c * h, 8)
    other1 = pl.multiple_of((1 - c) * h, 8)
    cp = copy(x_ref.at[pl.ds(other1, h)], r1, 0, peer_c)
    cp.start()
    cp.wait()
    a1[...] = x_ref[pl.ds(mine1, h), :] + r1[...]

    mine2 = pl.multiple_of(b1 * q, 8)
    other2 = pl.multiple_of((1 - b1) * q, 8)
    cp = copy(a1.at[pl.ds(other2, q)], r2, 1, peer_1)
    cp.start()
    cp.wait()
    a2[...] = a1[pl.ds(mine2, q), :] + r2[...]

    mine3 = pl.multiple_of(b2 * e, 8)
    other3 = pl.multiple_of((1 - b2) * e, 8)
    cp = copy(a2.at[pl.ds(other3, e)], r3, 2, peer_2)
    cp.start()
    cp.wait()
    base_q = pl.multiple_of(mine1 + mine2, 8)
    at_e = pl.multiple_of(base_q + mine3, 8)
    out_ref[pl.ds(at_e, e), :] = a2[pl.ds(mine3, e), :] + r3[...]

    cp = copy(out_ref.at[pl.ds(at_e, e)], out_ref.at[pl.ds(at_e, e)], 3, peer_2)
    cp.start()
    cp.wait()
    cp = copy(out_ref.at[pl.ds(base_q, q)], out_ref.at[pl.ds(base_q, q)], 4, peer_1)
    cp.start()
    cp.wait()
    cp = copy(out_ref.at[pl.ds(mine1, h)], out_ref.at[pl.ds(mine1, h)], 5, peer_c)
    cp.start()
    cp.wait()


def win_sum(x):
    rows, cols = x.shape
    return pl.pallas_call(
        win_sum_kernel,
        out_shape=jax.ShapeDtypeStruct((rows, cols), jnp.float32),
        in_specs=[pl.BlockSpec(memory_space=pltpu.VMEM)],
        out_specs=pl.BlockSpec(memory_space=pltpu.VMEM),
        scratch_shapes=[
            pltpu.VMEM((rows // 2, cols), jnp.float32),
            pltpu.VMEM((rows // 4, cols), jnp.float32),
            pltpu.VMEM((rows // 2, cols), jnp.float32),
            pltpu.VMEM((rows // 4, cols), jnp.float32),
            pltpu.VMEM((rows // 8, cols), jnp.float32),
            pltpu.SemaphoreType.DMA((6,)),
            pltpu.SemaphoreType.DMA((6,)),
        ],
        compiler_params=pltpu.CompilerParams(collective_id=0, has_side_effects=True),
    )(x)


def on_device(spectra, flags, owners, source_slots):
    win_count = spectra.shape[0]
    bins = spectra.shape[4]
    weighted = whiten(spectra) * flags.astype(jnp.float32)[:, :, None, None, None]
    n_win = lax.axis_size(WIN)
    table = lag_table_fast(bins, NLAG, win_count * n_win)
    me = lax.axis_index(STA)
    chosen = []
    for step in range(STEPS):
        block = jnp.take(weighted, source_slots[step], axis=1)
        chosen.append(jnp.where(me == owners[step], block, 0.0))
    picked_all = jnp.stack(chosen)
    picked_all = broadcast_owner(picked_all)
    shape = weighted.shape
    rec = weighted.transpose(0, 2, 1, 3, 4).reshape(shape[0], 2, shape[1] * shape[3], shape[4])
    stacked = correlate_all(picked_all, rec, table).reshape(
        STEPS, shape[1], shape[3], shape[1], shape[3], NLAG
    )
    return win_sum(stacked.reshape(-1, NLAG)).reshape(stacked.shape)


def solution(mesh):
    fine = fine_mesh(mesh)
    return jax.shard_map(
        on_device,
        mesh=fine,
        in_specs=(P(WIN, STA, None, None, None), P(WIN, STA), P(), P()),
        out_specs=P(None, None, None, STA, None, None),
        check_vma=False,
    )
```

```python
import math

import jax
import jax.numpy as jnp
from jax import lax
from jax.experimental import pallas as pl
from jax.experimental.pallas import tpu as pltpu
from jax.sharding import Mesh
from jax.sharding import PartitionSpec as P

NLAG = 768
STEPS = 4
MESH_ID = pl.DeviceIdType.MESH
STA = ("y", "x", "zh")
WIN = ("zl", "c")


def fine_mesh(mesh):
    devs = mesh.devices
    n_sta, n_win = devs.shape
    col = devs[:, 0]
    ny = len({d.coords[1] for d in col})
    nx = len({d.coords[0] for d in col})
    nzh = n_sta // (ny * nx)
    nc = len({d.core_on_chip for d in devs[0, :]})
    nzl = n_win // nc
    return Mesh(devs.reshape(ny, nx, nzh, nzl, nc), STA + WIN)


def whiten(spectra):
    shape = spectra.shape
    blocks = spectra.reshape(shape[0], shape[1], 2, 3, shape[4] // 64, 64)
    power = jnp.mean(blocks * blocks, axis=(2, 3, 5), keepdims=True)
    return (blocks / jnp.sqrt(power + 1e-06)).reshape(shape)


def lag_table_fast(bins, lags, windows):
    freq = jnp.arange(bins, dtype=jnp.int32) + 360
    q = jnp.arange(lags // 128, dtype=jnp.int32) * 128 - lags // 2
    k = jnp.arange(128, dtype=jnp.int32)
    unit = 2.0 * math.pi / 7200.0
    a = jnp.mod(freq[:, None] * q[None, :], 7200).astype(jnp.float32) * unit
    b = jnp.mod(freq[:, None] * k[None, :], 7200).astype(jnp.float32) * unit
    ca, sa = jnp.cos(a)[:, :, None], jnp.sin(a)[:, :, None]
    cb, sb = jnp.cos(b)[:, None, :], jnp.sin(b)[:, None, :]
    scale = 1.0 / math.sqrt(windows * bins)
    cos = ((ca * cb - sa * sb) * scale).reshape(bins, lags)
    sin = ((sa * cb + ca * sb) * scale).reshape(bins, lags)
    return jnp.stack([cos, -sin]).astype(jnp.bfloat16)


def corr_kernel(src_ref, rec_ref, tab_ref, out_ref, rows_ref):
    n_win = src_ref.shape[1]
    n_src = src_ref.shape[2]
    n_cmp = src_ref.shape[4]
    n_rows = rec_ref.shape[2]
    for s in range(n_src):
        for i in range(n_cmp):
            acc_re = None
            acc_im = None
            for w in range(n_win):
                sre = src_ref[0, w, s, 0, pl.ds(i, 1), :]
                sim = src_ref[0, w, s, 1, pl.ds(i, 1), :]
                rre = rec_ref[w, 0]
                rim = rec_ref[w, 1]
                re = sre * rre + sim * rim
                im = sim * rre - sre * rim
                acc_re = re if acc_re is None else acc_re + re
                acc_im = im if acc_im is None else acc_im + im
            row = (s * n_cmp + i) * n_rows
            rows_ref[0, pl.ds(row, n_rows), :] = acc_re.astype(jnp.bfloat16)
            rows_ref[1, pl.ds(row, n_rows), :] = acc_im.astype(jnp.bfloat16)
    out_ref[0] = jnp.dot(rows_ref[0], tab_ref[0], preferred_element_type=jnp.float32) + jnp.dot(
        rows_ref[1], tab_ref[1], preferred_element_type=jnp.float32
    )


def correlate_all(picked_all, rec, table):
    steps, n_win, n_src, _, n_cmp, bins = picked_all.shape
    n_rows = rec.shape[2]
    lags = table.shape[2]
    m = n_src * n_cmp * n_rows
    return pl.pallas_call(
        corr_kernel,
        grid=(steps,),
        in_specs=[
            pl.BlockSpec((1, n_win, n_src, 2, n_cmp, bins), lambda t: (t, 0, 0, 0, 0, 0)),
            pl.BlockSpec(rec.shape, lambda t: (0, 0, 0, 0)),
            pl.BlockSpec(table.shape, lambda t: (0, 0, 0)),
        ],
        out_specs=pl.BlockSpec((1, m, lags), lambda t: (t, 0, 0)),
        out_shape=jax.ShapeDtypeStruct((steps, m, lags), jnp.float32),
        scratch_shapes=[pltpu.VMEM((2, m, bins), jnp.bfloat16)],
    )(picked_all, rec, table)


def win_sum_kernel(x_ref, out_ref, a1, a2, r1, r2, r3, send_sem, recv_sem):
    rows = x_ref.shape[0]
    h, q, e = rows // 2, rows // 4, rows // 8
    coords = [lax.axis_index(a) for a in STA + WIN]
    zl, c = coords[3], coords[4]
    b1 = zl % 2
    b2 = zl // 2
    peer_c = tuple(coords[:4]) + (1 - c,)
    peer_1 = tuple(coords[:3]) + (zl + 1 - 2 * b1, c)
    peer_2 = tuple(coords[:3]) + (zl + 2 - 4 * b2, c)

    barrier = pltpu.get_barrier_semaphore()
    for peer in (peer_c, peer_1, peer_2):
        pl.semaphore_signal(barrier, inc=1, device_id=peer, device_id_type=MESH_ID)
    pl.semaphore_wait(barrier, 3)

    def copy(src, dst, k, peer):
        return pltpu.make_async_remote_copy(
            src_ref=src, dst_ref=dst, send_sem=send_sem.at[k], recv_sem=recv_sem.at[k],
            device_id=peer, device_id_type=MESH_ID)

    mine1 = pl.multiple_of(c * h, 8)
    other1 = pl.multiple_of((1 - c) * h, 8)
    cp = copy(x_ref.at[pl.ds(other1, h)], r1, 0, peer_c)
    cp.start()
    cp.wait()
    a1[...] = x_ref[pl.ds(mine1, h), :] + r1[...]

    mine2 = pl.multiple_of(b1 * q, 8)
    other2 = pl.multiple_of((1 - b1) * q, 8)
    cp = copy(a1.at[pl.ds(other2, q)], r2, 1, peer_1)
    cp.start()
    cp.wait()
    a2[...] = a1[pl.ds(mine2, q), :] + r2[...]

    mine3 = pl.multiple_of(b2 * e, 8)
    other3 = pl.multiple_of((1 - b2) * e, 8)
    cp = copy(a2.at[pl.ds(other3, e)], r3, 2, peer_2)
    cp.start()
    cp.wait()
    base_q = pl.multiple_of(mine1 + mine2, 8)
    at_e = pl.multiple_of(base_q + mine3, 8)
    out_ref[pl.ds(at_e, e), :] = a2[pl.ds(mine3, e), :] + r3[...]

    cp = copy(out_ref.at[pl.ds(at_e, e)], out_ref.at[pl.ds(at_e, e)], 3, peer_2)
    cp.start()
    cp.wait()
    cp = copy(out_ref.at[pl.ds(base_q, q)], out_ref.at[pl.ds(base_q, q)], 4, peer_1)
    cp.start()
    cp.wait()
    cp = copy(out_ref.at[pl.ds(mine1, h)], out_ref.at[pl.ds(mine1, h)], 5, peer_c)
    cp.start()
    cp.wait()


def win_sum(x):
    rows, cols = x.shape
    return pl.pallas_call(
        win_sum_kernel,
        out_shape=jax.ShapeDtypeStruct((rows, cols), jnp.float32),
        in_specs=[pl.BlockSpec(memory_space=pltpu.VMEM)],
        out_specs=pl.BlockSpec(memory_space=pltpu.VMEM),
        scratch_shapes=[
            pltpu.VMEM((rows // 2, cols), jnp.float32),
            pltpu.VMEM((rows // 4, cols), jnp.float32),
            pltpu.VMEM((rows // 2, cols), jnp.float32),
            pltpu.VMEM((rows // 4, cols), jnp.float32),
            pltpu.VMEM((rows // 8, cols), jnp.float32),
            pltpu.SemaphoreType.DMA((6,)),
            pltpu.SemaphoreType.DMA((6,)),
        ],
        compiler_params=pltpu.CompilerParams(collective_id=0, has_side_effects=True),
    )(x)


def bcast_kernel(m_ref, out_ref, rs_recv, piece, zh_recv, send_rs, recv_rs, send_ag, recv_ag, zsem):
    n = m_ref.shape[0]
    y, x, zh, zl, c = (lax.axis_index(a) for a in STA + WIN)
    nx = lax.axis_size("x")
    me = y * nx + x

    def plane_peer(p):
        return (p // nx, p % nx, zh, zl, c)

    zpeer = (y, x, 1 - zh, zl, c)
    barrier = pltpu.get_barrier_semaphore()
    for d in range(1, n):
        pl.semaphore_signal(barrier, inc=1, device_id=plane_peer((me + d) % n), device_id_type=MESH_ID)
    pl.semaphore_signal(barrier, inc=1, device_id=zpeer, device_id_type=MESH_ID)
    pl.semaphore_wait(barrier, n)

    copies = []
    for d in range(1, n):
        dst = (me + d) % n
        cp = pltpu.make_async_remote_copy(
            src_ref=m_ref.at[dst], dst_ref=rs_recv.at[me], send_sem=send_rs.at[d],
            recv_sem=recv_rs.at[d], device_id=plane_peer(dst), device_id_type=MESH_ID)
        cp.start()
        copies.append(cp)
    for cp in copies:
        cp.wait()
    total = m_ref[me]
    for d in range(1, n):
        total = total + rs_recv[(me + n - d) % n]
    piece[...] = total

    cp = pltpu.make_async_remote_copy(
        src_ref=piece, dst_ref=zh_recv, send_sem=zsem.at[0], recv_sem=zsem.at[1],
        device_id=zpeer, device_id_type=MESH_ID)
    cp.start()
    cp.wait()
    out_ref[me] = piece[...] + zh_recv[...]

    copies = []
    for d in range(1, n):
        dst = (me + d) % n
        cp = pltpu.make_async_remote_copy(
            src_ref=out_ref.at[me], dst_ref=out_ref.at[me], send_sem=send_ag.at[d],
            recv_sem=recv_ag.at[d], device_id=plane_peer(dst), device_id_type=MESH_ID)
        cp.start()
        copies.append(cp)
    for cp in copies:
        cp.wait()


def bcast(masked):
    n = masked.shape[0]
    shape = masked.shape
    return pl.pallas_call(
        bcast_kernel,
        out_shape=jax.ShapeDtypeStruct(shape, jnp.float32),
        in_specs=[pl.BlockSpec(memory_space=pltpu.VMEM)],
        out_specs=pl.BlockSpec(memory_space=pltpu.VMEM),
        scratch_shapes=[
            pltpu.VMEM(shape, jnp.float32),
            pltpu.VMEM(shape[1:], jnp.float32),
            pltpu.VMEM(shape[1:], jnp.float32),
            pltpu.SemaphoreType.DMA((n,)),
            pltpu.SemaphoreType.DMA((n,)),
            pltpu.SemaphoreType.DMA((n,)),
            pltpu.SemaphoreType.DMA((n,)),
            pltpu.SemaphoreType.DMA((2,)),
        ],
        compiler_params=pltpu.CompilerParams(collective_id=1, has_side_effects=True),
    )(masked)


def on_device(spectra, flags, owners, source_slots):
    win_count = spectra.shape[0]
    bins = spectra.shape[4]
    weighted = whiten(spectra) * flags.astype(jnp.float32)[:, :, None, None, None]
    n_win = lax.axis_size(WIN)
    table = lag_table_fast(bins, NLAG, win_count * n_win)
    me = lax.axis_index(STA)
    chosen = []
    for step in range(STEPS):
        block = jnp.take(weighted, source_slots[step], axis=1)
        chosen.append(jnp.where(me == owners[step], block, 0.0))
    picked_all = jnp.stack(chosen)
    plane = lax.axis_size(("y", "x"))
    picked_all = bcast(picked_all.reshape(plane, -1, 128)).reshape(picked_all.shape)
    shape = weighted.shape
    rec = weighted.transpose(0, 2, 1, 3, 4).reshape(shape[0], 2, shape[1] * shape[3], shape[4])
    stacked = correlate_all(picked_all, rec, table).reshape(
        STEPS, shape[1], shape[3], shape[1], shape[3], NLAG
    )
    return win_sum(stacked.reshape(-1, NLAG)).reshape(stacked.shape)


def solution(mesh):
    fine = fine_mesh(mesh)
    return jax.shard_map(
        on_device,
        mesh=fine,
        in_specs=(P(WIN, STA, None, None, None), P(WIN, STA), P(), P()),
        out_specs=P(None, None, None, STA, None, None),
        check_vma=False,
    )
```

```python
import functools
import math

import jax
import jax.numpy as jnp
from jax import lax
from jax.experimental import pallas as pl
from jax.experimental.pallas import tpu as pltpu
from jax.sharding import Mesh
from jax.sharding import PartitionSpec as P

NLAG = 768
STEPS = 4
MESH_ID = pl.DeviceIdType.MESH
STA = ("y", "x", "zh")
WIN = ("zl", "c")


def fine_mesh(mesh):
    devs = mesh.devices
    n_sta, n_win = devs.shape
    col = devs[:, 0]
    ny = len({d.coords[1] for d in col})
    nx = len({d.coords[0] for d in col})
    nzh = n_sta // (ny * nx)
    nc = len({d.core_on_chip for d in devs[0, :]})
    nzl = n_win // nc
    return Mesh(devs.reshape(ny, nx, nzh, nzl, nc), STA + WIN)


def whiten(spectra):
    shape = spectra.shape
    blocks = spectra.reshape(shape[0], shape[1], 2, 3, shape[4] // 64, 64)
    power = jnp.mean(blocks * blocks, axis=(2, 3, 5), keepdims=True)
    return (blocks / jnp.sqrt(power + 1e-06)).reshape(shape)


def lag_factors(bins, lags):
    freq = jnp.arange(bins, dtype=jnp.int32) + 360
    q = jnp.arange(lags // 128, dtype=jnp.int32) * 128 - lags // 2
    k = jnp.arange(128, dtype=jnp.int32)
    unit = 2.0 * math.pi / 7200.0
    a = jnp.mod(freq[:, None] * q[None, :], 7200).astype(jnp.float32) * unit
    b = jnp.mod(freq[:, None] * k[None, :], 7200).astype(jnp.float32) * unit
    return jnp.cos(a), jnp.sin(a), jnp.cos(b), jnp.sin(b)


def corr_kernel(scale, src_ref, rec_ref, ca_ref, sa_ref, cb_ref, sb_ref, out_ref, rows_ref, tab_ref):
    n_win = src_ref.shape[1]
    n_src = src_ref.shape[2]
    n_cmp = src_ref.shape[4]
    n_rows = rec_ref.shape[2]

    @pl.when(pl.program_id(0) == 0)
    def _():
        cb = cb_ref[...]
        sb = sb_ref[...]
        for q in range(ca_ref.shape[1]):
            ca = ca_ref[:, pl.ds(q, 1)]
            sa = sa_ref[:, pl.ds(q, 1)]
            cols = pl.ds(q * 128, 128)
            tab_ref[0, :, cols] = ((ca * cb - sa * sb) * scale).astype(jnp.bfloat16)
            tab_ref[1, :, cols] = (-((sa * cb + ca * sb) * scale)).astype(jnp.bfloat16)

    for s in range(n_src):
        for i in range(n_cmp):
            acc_re = None
            acc_im = None
            for w in range(n_win):
                sre = src_ref[0, w, s, 0, pl.ds(i, 1), :]
                sim = src_ref[0, w, s, 1, pl.ds(i, 1), :]
                rre = rec_ref[w, 0]
                rim = rec_ref[w, 1]
                re = sre * rre + sim * rim
                im = sim * rre - sre * rim
                acc_re = re if acc_re is None else acc_re + re
                acc_im = im if acc_im is None else acc_im + im
            row = (s * n_cmp + i) * n_rows
            rows_ref[0, pl.ds(row, n_rows), :] = acc_re.astype(jnp.bfloat16)
            rows_ref[1, pl.ds(row, n_rows), :] = acc_im.astype(jnp.bfloat16)
    out_ref[0] = jnp.dot(rows_ref[0], tab_ref[0], preferred_element_type=jnp.float32) + jnp.dot(
        rows_ref[1], tab_ref[1], preferred_element_type=jnp.float32
    )


def correlate_all(picked_all, rec, factors, windows):
    steps, n_win, n_src, _, n_cmp, bins = picked_all.shape
    n_rows = rec.shape[2]
    lags = NLAG
    m = n_src * n_cmp * n_rows
    scale = 1.0 / math.sqrt(windows * bins)
    whole = lambda t: (0, 0)
    return pl.pallas_call(
        functools.partial(corr_kernel, scale),
        grid=(steps,),
        in_specs=[
            pl.BlockSpec((1, n_win, n_src, 2, n_cmp, bins), lambda t: (t, 0, 0, 0, 0, 0)),
            pl.BlockSpec(rec.shape, lambda t: (0, 0, 0, 0)),
        ]
        + [pl.BlockSpec(f.shape, whole) for f in factors],
        out_specs=pl.BlockSpec((1, m, lags), lambda t: (t, 0, 0)),
        out_shape=jax.ShapeDtypeStruct((steps, m, lags), jnp.float32),
        scratch_shapes=[
            pltpu.VMEM((2, m, bins), jnp.bfloat16),
            pltpu.VMEM((2, bins, lags), jnp.bfloat16),
        ],
    )(picked_all, rec, *factors)


def win_sum_kernel(x_ref, out_ref, a1, a2, r1, r2, r3, send_sem, recv_sem):
    rows = x_ref.shape[0]
    h, q, e = rows // 2, rows // 4, rows // 8
    coords = [lax.axis_index(a) for a in STA + WIN]
    zl, c = coords[3], coords[4]
    b1 = zl % 2
    b2 = zl // 2
    peer_c = tuple(coords[:4]) + (1 - c,)
    peer_1 = tuple(coords[:3]) + (zl + 1 - 2 * b1, c)
    peer_2 = tuple(coords[:3]) + (zl + 2 - 4 * b2, c)

    barrier = pltpu.get_barrier_semaphore()
    for peer in (peer_c, peer_1, peer_2):
        pl.semaphore_signal(barrier, inc=1, device_id=peer, device_id_type=MESH_ID)
    pl.semaphore_wait(barrier, 3)

    def copy(src, dst, k, peer):
        return pltpu.make_async_remote_copy(
            src_ref=src, dst_ref=dst, send_sem=send_sem.at[k], recv_sem=recv_sem.at[k],
            device_id=peer, device_id_type=MESH_ID)

    mine1 = pl.multiple_of(c * h, 8)
    other1 = pl.multiple_of((1 - c) * h, 8)
    cp = copy(x_ref.at[pl.ds(other1, h)], r1, 0, peer_c)
    cp.start()
    cp.wait()
    a1[...] = x_ref[pl.ds(mine1, h), :] + r1[...]

    mine2 = pl.multiple_of(b1 * q, 8)
    other2 = pl.multiple_of((1 - b1) * q, 8)
    cp = copy(a1.at[pl.ds(other2, q)], r2, 1, peer_1)
    cp.start()
    cp.wait()
    a2[...] = a1[pl.ds(mine2, q), :] + r2[...]

    mine3 = pl.multiple_of(b2 * e, 8)
    other3 = pl.multiple_of((1 - b2) * e, 8)
    cp = copy(a2.at[pl.ds(other3, e)], r3, 2, peer_2)
    cp.start()
    cp.wait()
    base_q = pl.multiple_of(mine1 + mine2, 8)
    at_e = pl.multiple_of(base_q + mine3, 8)
    out_ref[pl.ds(at_e, e), :] = a2[pl.ds(mine3, e), :] + r3[...]

    cp = copy(out_ref.at[pl.ds(at_e, e)], out_ref.at[pl.ds(at_e, e)], 3, peer_2)
    cp.start()
    cp.wait()
    cp = copy(out_ref.at[pl.ds(base_q, q)], out_ref.at[pl.ds(base_q, q)], 4, peer_1)
    cp.start()
    cp.wait()
    cp = copy(out_ref.at[pl.ds(mine1, h)], out_ref.at[pl.ds(mine1, h)], 5, peer_c)
    cp.start()
    cp.wait()


def win_sum(x):
    rows, cols = x.shape
    return pl.pallas_call(
        win_sum_kernel,
        out_shape=jax.ShapeDtypeStruct((rows, cols), jnp.float32),
        in_specs=[pl.BlockSpec(memory_space=pltpu.VMEM)],
        out_specs=pl.BlockSpec(memory_space=pltpu.VMEM),
        scratch_shapes=[
            pltpu.VMEM((rows // 2, cols), jnp.float32),
            pltpu.VMEM((rows // 4, cols), jnp.float32),
            pltpu.VMEM((rows // 2, cols), jnp.float32),
            pltpu.VMEM((rows // 4, cols), jnp.float32),
            pltpu.VMEM((rows // 8, cols), jnp.float32),
            pltpu.SemaphoreType.DMA((6,)),
            pltpu.SemaphoreType.DMA((6,)),
        ],
        compiler_params=pltpu.CompilerParams(collective_id=0, has_side_effects=True),
    )(x)


def bcast_kernel(m_ref, out_ref, rs_recv, piece, zh_recv, send_rs, recv_rs, send_ag, recv_ag, zsem):
    n = m_ref.shape[0]
    y, x, zh, zl, c = (lax.axis_index(a) for a in STA + WIN)
    nx = lax.axis_size("x")
    me = y * nx + x

    def plane_peer(p):
        return (p // nx, p % nx, zh, zl, c)

    zpeer = (y, x, 1 - zh, zl, c)
    barrier = pltpu.get_barrier_semaphore()
    for d in range(1, n):
        pl.semaphore_signal(barrier, inc=1, device_id=plane_peer((me + d) % n), device_id_type=MESH_ID)
    pl.semaphore_signal(barrier, inc=1, device_id=zpeer, device_id_type=MESH_ID)
    pl.semaphore_wait(barrier, n)

    copies = []
    for d in range(1, n):
        dst = (me + d) % n
        cp = pltpu.make_async_remote_copy(
            src_ref=m_ref.at[dst], dst_ref=rs_recv.at[me], send_sem=send_rs.at[d],
            recv_sem=recv_rs.at[d], device_id=plane_peer(dst), device_id_type=MESH_ID)
        cp.start()
        copies.append(cp)
    for cp in copies:
        cp.wait()
    total = m_ref[me]
    for d in range(1, n):
        total = total + rs_recv[(me + n - d) % n]
    piece[...] = total

    cp = pltpu.make_async_remote_copy(
        src_ref=piece, dst_ref=zh_recv, send_sem=zsem.at[0], recv_sem=zsem.at[1],
        device_id=zpeer, device_id_type=MESH_ID)
    cp.start()
    cp.wait()
    out_ref[me] = piece[...] + zh_recv[...]

    copies = []
    for d in range(1, n):
        dst = (me + d) % n
        cp = pltpu.make_async_remote_copy(
            src_ref=out_ref.at[me], dst_ref=out_ref.at[me], send_sem=send_ag.at[d],
            recv_sem=recv_ag.at[d], device_id=plane_peer(dst), device_id_type=MESH_ID)
        cp.start()
        copies.append(cp)
    for cp in copies:
        cp.wait()


def bcast(masked):
    n = masked.shape[0]
    shape = masked.shape
    return pl.pallas_call(
        bcast_kernel,
        out_shape=jax.ShapeDtypeStruct(shape, jnp.float32),
        in_specs=[pl.BlockSpec(memory_space=pltpu.VMEM)],
        out_specs=pl.BlockSpec(memory_space=pltpu.VMEM),
        scratch_shapes=[
            pltpu.VMEM(shape, jnp.float32),
            pltpu.VMEM(shape[1:], jnp.float32),
            pltpu.VMEM(shape[1:], jnp.float32),
            pltpu.SemaphoreType.DMA((n,)),
            pltpu.SemaphoreType.DMA((n,)),
            pltpu.SemaphoreType.DMA((n,)),
            pltpu.SemaphoreType.DMA((n,)),
            pltpu.SemaphoreType.DMA((2,)),
        ],
        compiler_params=pltpu.CompilerParams(collective_id=1, has_side_effects=True),
    )(masked)


def on_device(spectra, flags, owners, source_slots):
    win_count = spectra.shape[0]
    bins = spectra.shape[4]
    weighted = whiten(spectra) * flags.astype(jnp.float32)[:, :, None, None, None]
    n_win = lax.axis_size(WIN)
    factors = lag_factors(bins, NLAG)
    me = lax.axis_index(STA)
    chosen = []
    for step in range(STEPS):
        block = jnp.take(weighted, source_slots[step], axis=1)
        chosen.append(jnp.where(me == owners[step], block, 0.0))
    picked_all = jnp.stack(chosen)
    plane = lax.axis_size(("y", "x"))
    picked_all = bcast(picked_all.reshape(plane, -1, 128)).reshape(picked_all.shape)
    shape = weighted.shape
    rec = weighted.transpose(0, 2, 1, 3, 4).reshape(shape[0], 2, shape[1] * shape[3], shape[4])
    stacked = correlate_all(picked_all, rec, factors, win_count * n_win).reshape(
        STEPS, shape[1], shape[3], shape[1], shape[3], NLAG
    )
    return win_sum(stacked.reshape(-1, NLAG)).reshape(stacked.shape)


def solution(mesh):
    fine = fine_mesh(mesh)
    return jax.shard_map(
        on_device,
        mesh=fine,
        in_specs=(P(WIN, STA, None, None, None), P(WIN, STA), P(), P()),
        out_specs=P(None, None, None, STA, None, None),
        check_vma=False,
    )
```

```python
import functools
import math

import jax
import jax.numpy as jnp
from jax import lax
from jax.experimental import pallas as pl
from jax.experimental.pallas import tpu as pltpu
from jax.sharding import Mesh
from jax.sharding import PartitionSpec as P

NLAG = 768
STEPS = 4
MESH_ID = pl.DeviceIdType.MESH
STA = ("y", "x", "zh")
WIN = ("zl", "c")


def fine_mesh(mesh):
    devs = mesh.devices
    n_sta, n_win = devs.shape
    col = devs[:, 0]
    ny = len({d.coords[1] for d in col})
    nx = len({d.coords[0] for d in col})
    nzh = n_sta // (ny * nx)
    nc = len({d.core_on_chip for d in devs[0, :]})
    nzl = n_win // nc
    return Mesh(devs.reshape(ny, nx, nzh, nzl, nc), STA + WIN)


def whiten(spectra):
    shape = spectra.shape
    blocks = spectra.reshape(shape[0], shape[1], 2, 3, shape[4] // 64, 64)
    power = jnp.mean(blocks * blocks, axis=(2, 3, 5), keepdims=True)
    return (blocks / jnp.sqrt(power + 1e-06)).reshape(shape)


def lag_phases(bins, lags):
    freq = jnp.arange(bins, dtype=jnp.int32) + 360
    q = jnp.arange(lags // 128, dtype=jnp.int32) * 128 - lags // 2
    k = jnp.arange(128, dtype=jnp.int32)
    unit = 2.0 * math.pi / 7200.0
    a = jnp.mod(freq[:, None] * q[None, :], 7200).astype(jnp.float32) * unit
    b = jnp.mod(freq[:, None] * k[None, :], 7200).astype(jnp.float32) * unit
    return a, b


def corr_kernel(scale, src_ref, rec_ref, a_ref, b_ref, out_ref, rows_ref, tab_ref):
    n_win = src_ref.shape[1]
    n_src = src_ref.shape[2]
    n_cmp = src_ref.shape[4]
    n_rows = rec_ref.shape[2]

    @pl.when(pl.program_id(0) == 0)
    def _():
        b = b_ref[...]
        cb = jnp.cos(b)
        sb = jnp.sin(b)
        for q in range(a_ref.shape[1]):
            a = a_ref[:, pl.ds(q, 1)]
            ca = jnp.cos(a)
            sa = jnp.sin(a)
            cols = pl.ds(q * 128, 128)
            tab_ref[0, :, cols] = ((ca * cb - sa * sb) * scale).astype(jnp.bfloat16)
            tab_ref[1, :, cols] = (-((sa * cb + ca * sb) * scale)).astype(jnp.bfloat16)

    for s in range(n_src):
        for i in range(n_cmp):
            acc_re = None
            acc_im = None
            for w in range(n_win):
                sre = src_ref[0, w, s, 0, pl.ds(i, 1), :]
                sim = src_ref[0, w, s, 1, pl.ds(i, 1), :]
                rre = rec_ref[w, 0]
                rim = rec_ref[w, 1]
                re = sre * rre + sim * rim
                im = sim * rre - sre * rim
                acc_re = re if acc_re is None else acc_re + re
                acc_im = im if acc_im is None else acc_im + im
            row = (s * n_cmp + i) * n_rows
            rows_ref[0, pl.ds(row, n_rows), :] = acc_re.astype(jnp.bfloat16)
            rows_ref[1, pl.ds(row, n_rows), :] = acc_im.astype(jnp.bfloat16)
    out_ref[0] = jnp.dot(rows_ref[0], tab_ref[0], preferred_element_type=jnp.float32) + jnp.dot(
        rows_ref[1], tab_ref[1], preferred_element_type=jnp.float32
    )


def correlate_all(picked_all, rec, factors, windows):
    steps, n_win, n_src, _, n_cmp, bins = picked_all.shape
    n_rows = rec.shape[2]
    lags = NLAG
    m = n_src * n_cmp * n_rows
    scale = 1.0 / math.sqrt(windows * bins)
    whole = lambda t: (0, 0)
    return pl.pallas_call(
        functools.partial(corr_kernel, scale),
        grid=(steps,),
        in_specs=[
            pl.BlockSpec((1, n_win, n_src, 2, n_cmp, bins), lambda t: (t, 0, 0, 0, 0, 0)),
            pl.BlockSpec(rec.shape, lambda t: (0, 0, 0, 0)),
        ]
        + [pl.BlockSpec(f.shape, whole) for f in factors],
        out_specs=pl.BlockSpec((1, m, lags), lambda t: (t, 0, 0)),
        out_shape=jax.ShapeDtypeStruct((steps, m, lags), jnp.float32),
        scratch_shapes=[
            pltpu.VMEM((2, m, bins), jnp.bfloat16),
            pltpu.VMEM((2, bins, lags), jnp.bfloat16),
        ],
    )(picked_all, rec, *factors)


def win_sum_kernel(x_ref, out_ref, a1, a2, r1, r2, r3, send_sem, recv_sem):
    rows = x_ref.shape[0]
    h, q, e = rows // 2, rows // 4, rows // 8
    coords = [lax.axis_index(a) for a in STA + WIN]
    zl, c = coords[3], coords[4]
    b1 = zl % 2
    b2 = zl // 2
    peer_c = tuple(coords[:4]) + (1 - c,)
    peer_1 = tuple(coords[:3]) + (zl + 1 - 2 * b1, c)
    peer_2 = tuple(coords[:3]) + (zl + 2 - 4 * b2, c)

    barrier = pltpu.get_barrier_semaphore()
    for peer in (peer_c, peer_1, peer_2):
        pl.semaphore_signal(barrier, inc=1, device_id=peer, device_id_type=MESH_ID)
    pl.semaphore_wait(barrier, 3)

    def copy(src, dst, k, peer):
        return pltpu.make_async_remote_copy(
            src_ref=src, dst_ref=dst, send_sem=send_sem.at[k], recv_sem=recv_sem.at[k],
            device_id=peer, device_id_type=MESH_ID)

    mine1 = pl.multiple_of(c * h, 8)
    other1 = pl.multiple_of((1 - c) * h, 8)
    cp = copy(x_ref.at[pl.ds(other1, h)], r1, 0, peer_c)
    cp.start()
    cp.wait()
    a1[...] = x_ref[pl.ds(mine1, h), :] + r1[...]

    mine2 = pl.multiple_of(b1 * q, 8)
    other2 = pl.multiple_of((1 - b1) * q, 8)
    cp = copy(a1.at[pl.ds(other2, q)], r2, 1, peer_1)
    cp.start()
    cp.wait()
    a2[...] = a1[pl.ds(mine2, q), :] + r2[...]

    mine3 = pl.multiple_of(b2 * e, 8)
    other3 = pl.multiple_of((1 - b2) * e, 8)
    cp = copy(a2.at[pl.ds(other3, e)], r3, 2, peer_2)
    cp.start()
    cp.wait()
    base_q = pl.multiple_of(mine1 + mine2, 8)
    at_e = pl.multiple_of(base_q + mine3, 8)
    out_ref[pl.ds(at_e, e), :] = a2[pl.ds(mine3, e), :] + r3[...]

    cp = copy(out_ref.at[pl.ds(at_e, e)], out_ref.at[pl.ds(at_e, e)], 3, peer_2)
    cp.start()
    cp.wait()
    cp = copy(out_ref.at[pl.ds(base_q, q)], out_ref.at[pl.ds(base_q, q)], 4, peer_1)
    cp.start()
    cp.wait()
    cp = copy(out_ref.at[pl.ds(mine1, h)], out_ref.at[pl.ds(mine1, h)], 5, peer_c)
    cp.start()
    cp.wait()


def win_sum(x):
    rows, cols = x.shape
    return pl.pallas_call(
        win_sum_kernel,
        out_shape=jax.ShapeDtypeStruct((rows, cols), jnp.float32),
        in_specs=[pl.BlockSpec(memory_space=pltpu.VMEM)],
        out_specs=pl.BlockSpec(memory_space=pltpu.VMEM),
        scratch_shapes=[
            pltpu.VMEM((rows // 2, cols), jnp.float32),
            pltpu.VMEM((rows // 4, cols), jnp.float32),
            pltpu.VMEM((rows // 2, cols), jnp.float32),
            pltpu.VMEM((rows // 4, cols), jnp.float32),
            pltpu.VMEM((rows // 8, cols), jnp.float32),
            pltpu.SemaphoreType.DMA((6,)),
            pltpu.SemaphoreType.DMA((6,)),
        ],
        compiler_params=pltpu.CompilerParams(collective_id=0, has_side_effects=True),
    )(x)


def bcast_kernel(m_ref, out_ref, rs_recv, piece, zh_recv, send_rs, recv_rs, send_ag, recv_ag, zsem):
    n = m_ref.shape[0]
    y, x, zh, zl, c = (lax.axis_index(a) for a in STA + WIN)
    nx = lax.axis_size("x")
    me = y * nx + x

    def plane_peer(p):
        return (p // nx, p % nx, zh, zl, c)

    zpeer = (y, x, 1 - zh, zl, c)
    barrier = pltpu.get_barrier_semaphore()
    for d in range(1, n):
        pl.semaphore_signal(barrier, inc=1, device_id=plane_peer((me + d) % n), device_id_type=MESH_ID)
    pl.semaphore_signal(barrier, inc=1, device_id=zpeer, device_id_type=MESH_ID)
    pl.semaphore_wait(barrier, n)

    copies = []
    for d in range(1, n):
        dst = (me + d) % n
        cp = pltpu.make_async_remote_copy(
            src_ref=m_ref.at[dst], dst_ref=rs_recv.at[me], send_sem=send_rs.at[d],
            recv_sem=recv_rs.at[d], device_id=plane_peer(dst), device_id_type=MESH_ID)
        cp.start()
        copies.append(cp)
    for cp in copies:
        cp.wait()
    total = m_ref[me]
    for d in range(1, n):
        total = total + rs_recv[(me + n - d) % n]
    piece[...] = total

    cp = pltpu.make_async_remote_copy(
        src_ref=piece, dst_ref=zh_recv, send_sem=zsem.at[0], recv_sem=zsem.at[1],
        device_id=zpeer, device_id_type=MESH_ID)
    cp.start()
    cp.wait()
    out_ref[me] = piece[...] + zh_recv[...]

    copies = []
    for d in range(1, n):
        dst = (me + d) % n
        cp = pltpu.make_async_remote_copy(
            src_ref=out_ref.at[me], dst_ref=out_ref.at[me], send_sem=send_ag.at[d],
            recv_sem=recv_ag.at[d], device_id=plane_peer(dst), device_id_type=MESH_ID)
        cp.start()
        copies.append(cp)
    for cp in copies:
        cp.wait()


def bcast(masked):
    n = masked.shape[0]
    shape = masked.shape
    return pl.pallas_call(
        bcast_kernel,
        out_shape=jax.ShapeDtypeStruct(shape, jnp.float32),
        in_specs=[pl.BlockSpec(memory_space=pltpu.VMEM)],
        out_specs=pl.BlockSpec(memory_space=pltpu.VMEM),
        scratch_shapes=[
            pltpu.VMEM(shape, jnp.float32),
            pltpu.VMEM(shape[1:], jnp.float32),
            pltpu.VMEM(shape[1:], jnp.float32),
            pltpu.SemaphoreType.DMA((n,)),
            pltpu.SemaphoreType.DMA((n,)),
            pltpu.SemaphoreType.DMA((n,)),
            pltpu.SemaphoreType.DMA((n,)),
            pltpu.SemaphoreType.DMA((2,)),
        ],
        compiler_params=pltpu.CompilerParams(collective_id=1, has_side_effects=True),
    )(masked)


def on_device(spectra, flags, owners, source_slots):
    win_count = spectra.shape[0]
    bins = spectra.shape[4]
    weighted = whiten(spectra) * flags.astype(jnp.float32)[:, :, None, None, None]
    n_win = lax.axis_size(WIN)
    factors = lag_phases(bins, NLAG)
    me = lax.axis_index(STA)
    chosen = []
    for step in range(STEPS):
        block = jnp.take(weighted, source_slots[step], axis=1)
        chosen.append(jnp.where(me == owners[step], block, 0.0))
    picked_all = jnp.stack(chosen)
    plane = lax.axis_size(("y", "x"))
    picked_all = bcast(picked_all.reshape(plane, -1, 128)).reshape(picked_all.shape)
    shape = weighted.shape
    rec = weighted.transpose(0, 2, 1, 3, 4).reshape(shape[0], 2, shape[1] * shape[3], shape[4])
    stacked = correlate_all(picked_all, rec, factors, win_count * n_win).reshape(
        STEPS, shape[1], shape[3], shape[1], shape[3], NLAG
    )
    return win_sum(stacked.reshape(-1, NLAG)).reshape(stacked.shape)


def solution(mesh):
    fine = fine_mesh(mesh)
    return jax.shard_map(
        on_device,
        mesh=fine,
        in_specs=(P(WIN, STA, None, None, None), P(WIN, STA), P(), P()),
        out_specs=P(None, None, None, STA, None, None),
        check_vma=False,
    )
```

```python
import functools
import math

import jax
import jax.numpy as jnp
from jax import lax
from jax.experimental import pallas as pl
from jax.experimental.pallas import tpu as pltpu
from jax.sharding import Mesh
from jax.sharding import PartitionSpec as P

NLAG = 768
STEPS = 4
MESH_ID = pl.DeviceIdType.MESH
STA = ("y", "x", "zh")
WIN = ("zl", "c")


def fine_mesh(mesh):
    devs = mesh.devices
    n_sta, n_win = devs.shape
    col = devs[:, 0]
    ny = len({d.coords[1] for d in col})
    nx = len({d.coords[0] for d in col})
    nzh = n_sta // (ny * nx)
    nc = len({d.core_on_chip for d in devs[0, :]})
    nzl = n_win // nc
    return Mesh(devs.reshape(ny, nx, nzh, nzl, nc), STA + WIN)


def whiten(spectra):
    shape = spectra.shape
    blocks = spectra.reshape(shape[0], shape[1], 2, 3, shape[4] // 64, 64)
    power = jnp.mean(blocks * blocks, axis=(2, 3, 5), keepdims=True)
    return (blocks / jnp.sqrt(power + 1e-06)).reshape(shape)


def lag_factors(bins, lags):
    freq = jnp.arange(bins, dtype=jnp.int32) + 360
    q = jnp.arange(lags // 128, dtype=jnp.int32) * 128 - lags // 2
    k = jnp.arange(128, dtype=jnp.int32)
    unit = 2.0 * math.pi / 7200.0
    a = jnp.mod(freq[:, None] * q[None, :], 7200).astype(jnp.float32) * unit
    b = jnp.mod(freq[:, None] * k[None, :], 7200).astype(jnp.float32) * unit
    return jnp.cos(a), jnp.sin(a), jnp.cos(b), jnp.sin(b)


def corr_kernel(scale, src_ref, rec_ref, ca_ref, sa_ref, cb_ref, sb_ref, out_ref, rows_ref, tab_ref):
    n_win = src_ref.shape[1]
    n_src = src_ref.shape[2]
    n_cmp = src_ref.shape[4]
    n_rows = rec_ref.shape[2]

    @pl.when(pl.program_id(0) == 0)
    def _():
        cb = cb_ref[...]
        sb = sb_ref[...]
        for q in range(ca_ref.shape[1]):
            ca = ca_ref[:, pl.ds(q, 1)]
            sa = sa_ref[:, pl.ds(q, 1)]
            cols = pl.ds(q * 128, 128)
            tab_ref[0, :, cols] = ((ca * cb - sa * sb) * scale).astype(jnp.bfloat16)
            tab_ref[1, :, cols] = (-((sa * cb + ca * sb) * scale)).astype(jnp.bfloat16)

    for s in range(n_src):
        for i in range(n_cmp):
            acc_re = None
            acc_im = None
            for w in range(n_win):
                sre = src_ref[0, w, s, 0, pl.ds(i, 1), :]
                sim = src_ref[0, w, s, 1, pl.ds(i, 1), :]
                rre = rec_ref[w, 0]
                rim = rec_ref[w, 1]
                re = sre * rre + sim * rim
                im = sim * rre - sre * rim
                acc_re = re if acc_re is None else acc_re + re
                acc_im = im if acc_im is None else acc_im + im
            row = (s * n_cmp + i) * n_rows
            rows_ref[0, pl.ds(row, n_rows), :] = acc_re.astype(jnp.bfloat16)
            rows_ref[1, pl.ds(row, n_rows), :] = acc_im.astype(jnp.bfloat16)
    out_ref[0] = jnp.dot(rows_ref[0], tab_ref[0], preferred_element_type=jnp.float32) + jnp.dot(
        rows_ref[1], tab_ref[1], preferred_element_type=jnp.float32
    )


def correlate_all(picked_all, rec, factors, windows):
    steps, n_win, n_src, _, n_cmp, bins = picked_all.shape
    n_rows = rec.shape[2]
    lags = NLAG
    m = n_src * n_cmp * n_rows
    scale = 1.0 / math.sqrt(windows * bins)
    whole = lambda t: (0, 0)
    return pl.pallas_call(
        functools.partial(corr_kernel, scale),
        grid=(steps,),
        in_specs=[
            pl.BlockSpec((1, n_win, n_src, 2, n_cmp, bins), lambda t: (t, 0, 0, 0, 0, 0)),
            pl.BlockSpec(rec.shape, lambda t: (0, 0, 0, 0)),
        ]
        + [pl.BlockSpec(f.shape, whole) for f in factors],
        out_specs=pl.BlockSpec((1, m, lags), lambda t: (t, 0, 0)),
        out_shape=jax.ShapeDtypeStruct((steps, m, lags), jnp.float32),
        scratch_shapes=[
            pltpu.VMEM((2, m, bins), jnp.bfloat16),
            pltpu.VMEM((2, bins, lags), jnp.bfloat16),
        ],
    )(picked_all, rec, *factors)


def win_sum_kernel(x_ref, out_ref, a1, a2, r1, r2, r3, send_sem, recv_sem):
    rows = x_ref.shape[0]
    h, q, e = rows // 2, rows // 4, rows // 8
    coords = [lax.axis_index(a) for a in STA + WIN]
    zl, c = coords[3], coords[4]
    b1 = zl % 2
    b2 = zl // 2
    peer_c = tuple(coords[:4]) + (1 - c,)
    peer_1 = tuple(coords[:3]) + (zl + 1 - 2 * b1, c)
    peer_2 = tuple(coords[:3]) + (zl + 2 - 4 * b2, c)

    barrier = pltpu.get_barrier_semaphore()
    for peer in (peer_c, peer_1, peer_2):
        pl.semaphore_signal(barrier, inc=1, device_id=peer, device_id_type=MESH_ID)
    pl.semaphore_wait(barrier, 3)

    def copy(src, dst, k, peer):
        return pltpu.make_async_remote_copy(
            src_ref=src, dst_ref=dst, send_sem=send_sem.at[k], recv_sem=recv_sem.at[k],
            device_id=peer, device_id_type=MESH_ID)

    mine1 = pl.multiple_of(c * h, 8)
    other1 = pl.multiple_of((1 - c) * h, 8)
    cp = copy(x_ref.at[pl.ds(other1, h)], r1, 0, peer_c)
    cp.start()
    cp.wait()
    a1[...] = x_ref[pl.ds(mine1, h), :] + r1[...]

    mine2 = pl.multiple_of(b1 * q, 8)
    other2 = pl.multiple_of((1 - b1) * q, 8)
    cp = copy(a1.at[pl.ds(other2, q)], r2, 1, peer_1)
    cp.start()
    cp.wait()
    a2[...] = a1[pl.ds(mine2, q), :] + r2[...]

    mine3 = pl.multiple_of(b2 * e, 8)
    other3 = pl.multiple_of((1 - b2) * e, 8)
    cp = copy(a2.at[pl.ds(other3, e)], r3, 2, peer_2)
    cp.start()
    cp.wait()
    base_q = pl.multiple_of(mine1 + mine2, 8)
    at_e = pl.multiple_of(base_q + mine3, 8)
    out_ref[pl.ds(at_e, e), :] = a2[pl.ds(mine3, e), :] + r3[...]

    cp = copy(out_ref.at[pl.ds(at_e, e)], out_ref.at[pl.ds(at_e, e)], 3, peer_2)
    cp.start()
    cp.wait()
    cp = copy(out_ref.at[pl.ds(base_q, q)], out_ref.at[pl.ds(base_q, q)], 4, peer_1)
    cp.start()
    cp.wait()
    cp = copy(out_ref.at[pl.ds(mine1, h)], out_ref.at[pl.ds(mine1, h)], 5, peer_c)
    cp.start()
    cp.wait()


def win_sum(x):
    rows, cols = x.shape
    return pl.pallas_call(
        win_sum_kernel,
        out_shape=jax.ShapeDtypeStruct((rows, cols), jnp.float32),
        in_specs=[pl.BlockSpec(memory_space=pltpu.VMEM)],
        out_specs=pl.BlockSpec(memory_space=pltpu.VMEM),
        scratch_shapes=[
            pltpu.VMEM((rows // 2, cols), jnp.float32),
            pltpu.VMEM((rows // 4, cols), jnp.float32),
            pltpu.VMEM((rows // 2, cols), jnp.float32),
            pltpu.VMEM((rows // 4, cols), jnp.float32),
            pltpu.VMEM((rows // 8, cols), jnp.float32),
            pltpu.SemaphoreType.DMA((6,)),
            pltpu.SemaphoreType.DMA((6,)),
        ],
        compiler_params=pltpu.CompilerParams(collective_id=0, has_side_effects=True),
    )(x)


def bcast_kernel(m_ref, out_ref, rx, s1, ry, piece, zr, sx, rxs, sy, rys, agy_s, agy_r, agx_s, agx_r, zsem):
    nx, ny = m_ref.shape[0], m_ref.shape[1]
    y, x, zh, zl, c = (lax.axis_index(a) for a in STA + WIN)
    xpeer = lambda p: (y, p, zh, zl, c)
    ypeer = lambda p: (p, x, zh, zl, c)
    zpeer = (y, x, 1 - zh, zl, c)

    barrier = pltpu.get_barrier_semaphore()
    for d in range(1, nx):
        pl.semaphore_signal(barrier, inc=1, device_id=xpeer((x + d) % nx), device_id_type=MESH_ID)
    for d in range(1, ny):
        pl.semaphore_signal(barrier, inc=1, device_id=ypeer((y + d) % ny), device_id_type=MESH_ID)
    pl.semaphore_signal(barrier, inc=1, device_id=zpeer, device_id_type=MESH_ID)
    pl.semaphore_wait(barrier, nx + ny - 1)

    def send_all(n, me, peer, src, dst, ssem, rsem):
        copies = []
        for d in range(1, n):
            to = (me + d) % n
            cp = pltpu.make_async_remote_copy(
                src_ref=src(to), dst_ref=dst, send_sem=ssem.at[d], recv_sem=rsem.at[d],
                device_id=peer(to), device_id_type=MESH_ID)
            cp.start()
            copies.append(cp)
        for cp in copies:
            cp.wait()

    send_all(nx, x, xpeer, lambda to: m_ref.at[to], rx.at[x], sx, rxs)
    total = m_ref[x]
    for d in range(1, nx):
        total = total + rx[(x + nx - d) % nx]
    s1[...] = total

    send_all(ny, y, ypeer, lambda to: s1.at[to], ry.at[y], sy, rys)
    part = s1[y]
    for d in range(1, ny):
        part = part + ry[(y + ny - d) % ny]
    piece[...] = part

    cp = pltpu.make_async_remote_copy(
        src_ref=piece, dst_ref=zr, send_sem=zsem.at[0], recv_sem=zsem.at[1],
        device_id=zpeer, device_id_type=MESH_ID)
    cp.start()
    cp.wait()
    out_ref[x, y] = piece[...] + zr[...]

    send_all(ny, y, ypeer, lambda to: out_ref.at[x, y], out_ref.at[x, y], agy_s, agy_r)
    send_all(nx, x, xpeer, lambda to: out_ref.at[x], out_ref.at[x], agx_s, agx_r)


def bcast(masked):
    shape = masked.shape
    nx, ny = shape[0], shape[1]
    return pl.pallas_call(
        bcast_kernel,
        out_shape=jax.ShapeDtypeStruct(shape, jnp.float32),
        in_specs=[pl.BlockSpec(memory_space=pltpu.VMEM)],
        out_specs=pl.BlockSpec(memory_space=pltpu.VMEM),
        scratch_shapes=[
            pltpu.VMEM(shape, jnp.float32),
            pltpu.VMEM(shape[1:], jnp.float32),
            pltpu.VMEM(shape[1:], jnp.float32),
            pltpu.VMEM(shape[2:], jnp.float32),
            pltpu.VMEM(shape[2:], jnp.float32),
            pltpu.SemaphoreType.DMA((nx,)),
            pltpu.SemaphoreType.DMA((nx,)),
            pltpu.SemaphoreType.DMA((ny,)),
            pltpu.SemaphoreType.DMA((ny,)),
            pltpu.SemaphoreType.DMA((ny,)),
            pltpu.SemaphoreType.DMA((ny,)),
            pltpu.SemaphoreType.DMA((nx,)),
            pltpu.SemaphoreType.DMA((nx,)),
            pltpu.SemaphoreType.DMA((2,)),
        ],
        compiler_params=pltpu.CompilerParams(collective_id=1, has_side_effects=True),
    )(masked)


def on_device(spectra, flags, owners, source_slots):
    win_count = spectra.shape[0]
    bins = spectra.shape[4]
    weighted = whiten(spectra) * flags.astype(jnp.float32)[:, :, None, None, None]
    n_win = lax.axis_size(WIN)
    factors = lag_factors(bins, NLAG)
    me = lax.axis_index(STA)
    chosen = []
    for step in range(STEPS):
        block = jnp.take(weighted, source_slots[step], axis=1)
        chosen.append(jnp.where(me == owners[step], block, 0.0))
    picked_all = jnp.stack(chosen)
    split = (lax.axis_size("x"), lax.axis_size("y"), -1, 128)
    picked_all = bcast(picked_all.reshape(split)).reshape(picked_all.shape)
    shape = weighted.shape
    rec = weighted.transpose(0, 2, 1, 3, 4).reshape(shape[0], 2, shape[1] * shape[3], shape[4])
    stacked = correlate_all(picked_all, rec, factors, win_count * n_win).reshape(
        STEPS, shape[1], shape[3], shape[1], shape[3], NLAG
    )
    return win_sum(stacked.reshape(-1, NLAG)).reshape(stacked.shape)


def solution(mesh):
    fine = fine_mesh(mesh)
    return jax.shard_map(
        on_device,
        mesh=fine,
        in_specs=(P(WIN, STA, None, None, None), P(WIN, STA), P(), P()),
        out_specs=P(None, None, None, STA, None, None),
        check_vma=False,
    )
```

```python
import functools
import math

import jax
import jax.numpy as jnp
from jax import lax
from jax.experimental import pallas as pl
from jax.experimental.pallas import tpu as pltpu
from jax.sharding import Mesh
from jax.sharding import PartitionSpec as P

NLAG = 768
STEPS = 4
MESH_ID = pl.DeviceIdType.MESH
STA = ("y", "x", "zh")
WIN = ("zl", "c")


def fine_mesh(mesh):
    devs = mesh.devices
    n_sta, n_win = devs.shape
    col = devs[:, 0]
    ny = len({d.coords[1] for d in col})
    nx = len({d.coords[0] for d in col})
    nzh = n_sta // (ny * nx)
    nc = len({d.core_on_chip for d in devs[0, :]})
    nzl = n_win // nc
    return Mesh(devs.reshape(ny, nx, nzh, nzl, nc), STA + WIN)


def whiten(spectra):
    shape = spectra.shape
    blocks = spectra.reshape(shape[0], shape[1], 2, 3, shape[4] // 64, 64)
    power = jnp.mean(blocks * blocks, axis=(2, 3, 5), keepdims=True)
    return (blocks / jnp.sqrt(power + 1e-06)).reshape(shape)


def lag_factors(bins, lags):
    shift = jnp.arange(lags, dtype=jnp.int32) - lags // 2
    hi = jnp.arange(bins // 64, dtype=jnp.int32) * 64 + 360
    lo = jnp.arange(64, dtype=jnp.int32)
    unit = 2.0 * math.pi / 7200.0
    a = jnp.mod(hi[:, None] * shift[None, :], 7200).astype(jnp.float32) * unit
    b = jnp.mod(lo[:, None] * shift[None, :], 7200).astype(jnp.float32) * unit
    return jnp.cos(a), jnp.sin(a), jnp.cos(b), jnp.sin(b)


def corr_kernel(scale, src_ref, rec_ref, ca_ref, sa_ref, cb_ref, sb_ref, out_ref, rows_ref, tab_ref):
    n_win = src_ref.shape[1]
    n_src = src_ref.shape[2]
    n_cmp = src_ref.shape[4]
    n_rows = rec_ref.shape[2]

    @pl.when(pl.program_id(0) == 0)
    def _():
        cb = cb_ref[...]
        sb = sb_ref[...]
        step = cb_ref.shape[0]
        for f1 in range(ca_ref.shape[0]):
            ca = ca_ref[pl.ds(f1, 1), :]
            sa = sa_ref[pl.ds(f1, 1), :]
            rows = pl.ds(f1 * step, step)
            tab_ref[0, rows, :] = ((ca * cb - sa * sb) * scale).astype(jnp.bfloat16)
            tab_ref[1, rows, :] = (-((sa * cb + ca * sb) * scale)).astype(jnp.bfloat16)

    for s in range(n_src):
        for i in range(n_cmp):
            acc_re = None
            acc_im = None
            for w in range(n_win):
                sre = src_ref[0, w, s, 0, pl.ds(i, 1), :]
                sim = src_ref[0, w, s, 1, pl.ds(i, 1), :]
                rre = rec_ref[w, 0]
                rim = rec_ref[w, 1]
                re = sre * rre + sim * rim
                im = sim * rre - sre * rim
                acc_re = re if acc_re is None else acc_re + re
                acc_im = im if acc_im is None else acc_im + im
            row = (s * n_cmp + i) * n_rows
            rows_ref[0, pl.ds(row, n_rows), :] = acc_re.astype(jnp.bfloat16)
            rows_ref[1, pl.ds(row, n_rows), :] = acc_im.astype(jnp.bfloat16)
    out_ref[0] = jnp.dot(rows_ref[0], tab_ref[0], preferred_element_type=jnp.float32) + jnp.dot(
        rows_ref[1], tab_ref[1], preferred_element_type=jnp.float32
    )


def correlate_all(picked_all, rec, factors, windows):
    steps, n_win, n_src, _, n_cmp, bins = picked_all.shape
    n_rows = rec.shape[2]
    lags = NLAG
    m = n_src * n_cmp * n_rows
    scale = 1.0 / math.sqrt(windows * bins)
    whole = lambda t: (0, 0)
    return pl.pallas_call(
        functools.partial(corr_kernel, scale),
        grid=(steps,),
        in_specs=[
            pl.BlockSpec((1, n_win, n_src, 2, n_cmp, bins), lambda t: (t, 0, 0, 0, 0, 0)),
            pl.BlockSpec(rec.shape, lambda t: (0, 0, 0, 0)),
        ]
        + [pl.BlockSpec(f.shape, whole) for f in factors],
        out_specs=pl.BlockSpec((1, m, lags), lambda t: (t, 0, 0)),
        out_shape=jax.ShapeDtypeStruct((steps, m, lags), jnp.float32),
        scratch_shapes=[
            pltpu.VMEM((2, m, bins), jnp.bfloat16),
            pltpu.VMEM((2, bins, lags), jnp.bfloat16),
        ],
    )(picked_all, rec, *factors)


def win_sum_kernel(x_ref, out_ref, a1, a2, r1, r2, r3, send_sem, recv_sem):
    rows = x_ref.shape[0]
    h, q, e = rows // 2, rows // 4, rows // 8
    coords = [lax.axis_index(a) for a in STA + WIN]
    zl, c = coords[3], coords[4]
    b1 = zl % 2
    b2 = zl // 2
    peer_c = tuple(coords[:4]) + (1 - c,)
    peer_1 = tuple(coords[:3]) + (zl + 1 - 2 * b1, c)
    peer_2 = tuple(coords[:3]) + (zl + 2 - 4 * b2, c)

    barrier = pltpu.get_barrier_semaphore()
    for peer in (peer_c, peer_1, peer_2):
        pl.semaphore_signal(barrier, inc=1, device_id=peer, device_id_type=MESH_ID)
    pl.semaphore_wait(barrier, 3)

    def copy(src, dst, k, peer):
        return pltpu.make_async_remote_copy(
            src_ref=src, dst_ref=dst, send_sem=send_sem.at[k], recv_sem=recv_sem.at[k],
            device_id=peer, device_id_type=MESH_ID)

    mine1 = pl.multiple_of(c * h, 8)
    other1 = pl.multiple_of((1 - c) * h, 8)
    cp = copy(x_ref.at[pl.ds(other1, h)], r1, 0, peer_c)
    cp.start()
    cp.wait()
    a1[...] = x_ref[pl.ds(mine1, h), :] + r1[...]

    mine2 = pl.multiple_of(b1 * q, 8)
    other2 = pl.multiple_of((1 - b1) * q, 8)
    cp = copy(a1.at[pl.ds(other2, q)], r2, 1, peer_1)
    cp.start()
    cp.wait()
    a2[...] = a1[pl.ds(mine2, q), :] + r2[...]

    mine3 = pl.multiple_of(b2 * e, 8)
    other3 = pl.multiple_of((1 - b2) * e, 8)
    cp = copy(a2.at[pl.ds(other3, e)], r3, 2, peer_2)
    cp.start()
    cp.wait()
    base_q = pl.multiple_of(mine1 + mine2, 8)
    at_e = pl.multiple_of(base_q + mine3, 8)
    out_ref[pl.ds(at_e, e), :] = a2[pl.ds(mine3, e), :] + r3[...]

    cp = copy(out_ref.at[pl.ds(at_e, e)], out_ref.at[pl.ds(at_e, e)], 3, peer_2)
    cp.start()
    cp.wait()
    cp = copy(out_ref.at[pl.ds(base_q, q)], out_ref.at[pl.ds(base_q, q)], 4, peer_1)
    cp.start()
    cp.wait()
    cp = copy(out_ref.at[pl.ds(mine1, h)], out_ref.at[pl.ds(mine1, h)], 5, peer_c)
    cp.start()
    cp.wait()


def win_sum(x):
    rows, cols = x.shape
    return pl.pallas_call(
        win_sum_kernel,
        out_shape=jax.ShapeDtypeStruct((rows, cols), jnp.float32),
        in_specs=[pl.BlockSpec(memory_space=pltpu.VMEM)],
        out_specs=pl.BlockSpec(memory_space=pltpu.VMEM),
        scratch_shapes=[
            pltpu.VMEM((rows // 2, cols), jnp.float32),
            pltpu.VMEM((rows // 4, cols), jnp.float32),
            pltpu.VMEM((rows // 2, cols), jnp.float32),
            pltpu.VMEM((rows // 4, cols), jnp.float32),
            pltpu.VMEM((rows // 8, cols), jnp.float32),
            pltpu.SemaphoreType.DMA((6,)),
            pltpu.SemaphoreType.DMA((6,)),
        ],
        compiler_params=pltpu.CompilerParams(collective_id=0, has_side_effects=True),
    )(x)


def bcast_kernel(m_ref, out_ref, rx, s1, ry, piece, zr, sx, rxs, sy, rys, agy_s, agy_r, agx_s, agx_r, zsem):
    nx, ny = m_ref.shape[0], m_ref.shape[1]
    y, x, zh, zl, c = (lax.axis_index(a) for a in STA + WIN)
    xpeer = lambda p: (y, p, zh, zl, c)
    ypeer = lambda p: (p, x, zh, zl, c)
    zpeer = (y, x, 1 - zh, zl, c)

    barrier = pltpu.get_barrier_semaphore()
    for d in range(1, nx):
        pl.semaphore_signal(barrier, inc=1, device_id=xpeer((x + d) % nx), device_id_type=MESH_ID)
    for d in range(1, ny):
        pl.semaphore_signal(barrier, inc=1, device_id=ypeer((y + d) % ny), device_id_type=MESH_ID)
    pl.semaphore_signal(barrier, inc=1, device_id=zpeer, device_id_type=MESH_ID)
    pl.semaphore_wait(barrier, nx + ny - 1)

    def send_all(n, me, peer, src, dst, ssem, rsem):
        copies = []
        for d in range(1, n):
            to = (me + d) % n
            cp = pltpu.make_async_remote_copy(
                src_ref=src(to), dst_ref=dst, send_sem=ssem.at[d], recv_sem=rsem.at[d],
                device_id=peer(to), device_id_type=MESH_ID)
            cp.start()
            copies.append(cp)
        for cp in copies:
            cp.wait()

    send_all(nx, x, xpeer, lambda to: m_ref.at[to], rx.at[x], sx, rxs)
    total = m_ref[x]
    for d in range(1, nx):
        total = total + rx[(x + nx - d) % nx]
    s1[...] = total

    send_all(ny, y, ypeer, lambda to: s1.at[to], ry.at[y], sy, rys)
    part = s1[y]
    for d in range(1, ny):
        part = part + ry[(y + ny - d) % ny]
    piece[...] = part

    cp = pltpu.make_async_remote_copy(
        src_ref=piece, dst_ref=zr, send_sem=zsem.at[0], recv_sem=zsem.at[1],
        device_id=zpeer, device_id_type=MESH_ID)
    cp.start()
    cp.wait()
    out_ref[x, y] = piece[...] + zr[...]

    send_all(ny, y, ypeer, lambda to: out_ref.at[x, y], out_ref.at[x, y], agy_s, agy_r)
    send_all(nx, x, xpeer, lambda to: out_ref.at[x], out_ref.at[x], agx_s, agx_r)


def bcast(masked):
    shape = masked.shape
    nx, ny = shape[0], shape[1]
    return pl.pallas_call(
        bcast_kernel,
        out_shape=jax.ShapeDtypeStruct(shape, jnp.float32),
        in_specs=[pl.BlockSpec(memory_space=pltpu.VMEM)],
        out_specs=pl.BlockSpec(memory_space=pltpu.VMEM),
        scratch_shapes=[
            pltpu.VMEM(shape, jnp.float32),
            pltpu.VMEM(shape[1:], jnp.float32),
            pltpu.VMEM(shape[1:], jnp.float32),
            pltpu.VMEM(shape[2:], jnp.float32),
            pltpu.VMEM(shape[2:], jnp.float32),
            pltpu.SemaphoreType.DMA((nx,)),
            pltpu.SemaphoreType.DMA((nx,)),
            pltpu.SemaphoreType.DMA((ny,)),
            pltpu.SemaphoreType.DMA((ny,)),
            pltpu.SemaphoreType.DMA((ny,)),
            pltpu.SemaphoreType.DMA((ny,)),
            pltpu.SemaphoreType.DMA((nx,)),
            pltpu.SemaphoreType.DMA((nx,)),
            pltpu.SemaphoreType.DMA((2,)),
        ],
        compiler_params=pltpu.CompilerParams(collective_id=1, has_side_effects=True),
    )(masked)


def on_device(spectra, flags, owners, source_slots):
    win_count = spectra.shape[0]
    bins = spectra.shape[4]
    weighted = whiten(spectra) * flags.astype(jnp.float32)[:, :, None, None, None]
    n_win = lax.axis_size(WIN)
    factors = lag_factors(bins, NLAG)
    me = lax.axis_index(STA)
    chosen = []
    for step in range(STEPS):
        block = jnp.take(weighted, source_slots[step], axis=1)
        chosen.append(jnp.where(me == owners[step], block, 0.0))
    picked_all = jnp.stack(chosen)
    split = (lax.axis_size("x"), lax.axis_size("y"), -1, 128)
    picked_all = bcast(picked_all.reshape(split)).reshape(picked_all.shape)
    shape = weighted.shape
    rec = weighted.transpose(0, 2, 1, 3, 4).reshape(shape[0], 2, shape[1] * shape[3], shape[4])
    stacked = correlate_all(picked_all, rec, factors, win_count * n_win).reshape(
        STEPS, shape[1], shape[3], shape[1], shape[3], NLAG
    )
    return win_sum(stacked.reshape(-1, NLAG)).reshape(stacked.shape)


def solution(mesh):
    fine = fine_mesh(mesh)
    return jax.shard_map(
        on_device,
        mesh=fine,
        in_specs=(P(WIN, STA, None, None, None), P(WIN, STA), P(), P()),
        out_specs=P(None, None, None, STA, None, None),
        check_vma=False,
    )
```

```python
import functools
import math

import jax
import jax.numpy as jnp
from jax import lax
from jax.experimental import pallas as pl
from jax.experimental.pallas import tpu as pltpu
from jax.sharding import Mesh
from jax.sharding import PartitionSpec as P

NLAG = 768
STEPS = 4
MESH_ID = pl.DeviceIdType.MESH
STA = ("y", "x", "zh")
WIN = ("zl", "c")


def fine_mesh(mesh):
    devs = mesh.devices
    n_sta, n_win = devs.shape
    col = devs[:, 0]
    ny = len({d.coords[1] for d in col})
    nx = len({d.coords[0] for d in col})
    nzh = n_sta // (ny * nx)
    nc = len({d.core_on_chip for d in devs[0, :]})
    nzl = n_win // nc
    return Mesh(devs.reshape(ny, nx, nzh, nzl, nc), STA + WIN)


def whiten(spectra):
    shape = spectra.shape
    blocks = spectra.reshape(shape[0], shape[1], 2, 3, shape[4] // 64, 64)
    power = jnp.mean(blocks * blocks, axis=(2, 3, 5), keepdims=True)
    return (blocks / jnp.sqrt(power + 1e-06)).reshape(shape)


def lag_factors(bins, lags):
    shift = jnp.arange(lags, dtype=jnp.int32) - lags // 2
    hi = jnp.arange(bins // 64, dtype=jnp.int32) * 64 + 360
    lo = jnp.arange(64, dtype=jnp.int32)
    unit = 2.0 * math.pi / 7200.0
    a = jnp.mod(hi[:, None] * shift[None, :], 7200).astype(jnp.float32) * unit
    b = jnp.mod(lo[:, None] * shift[None, :], 7200).astype(jnp.float32) * unit
    return jnp.cos(a), jnp.sin(a), jnp.cos(b), jnp.sin(b)


def corr_kernel(scale, src_ref, rec_ref, ca_ref, sa_ref, cb_ref, sb_ref, out_ref, rows_ref, tab_ref):
    n_win = src_ref.shape[1]
    n_src = src_ref.shape[2]
    n_cmp = src_ref.shape[4]
    n_rows = rec_ref.shape[2]

    @pl.when(pl.program_id(0) == 0)
    def _():
        cb = cb_ref[...]
        sb = sb_ref[...]
        step = cb_ref.shape[0]
        for f1 in range(ca_ref.shape[0]):
            ca = ca_ref[pl.ds(f1, 1), :]
            sa = sa_ref[pl.ds(f1, 1), :]
            rows = pl.ds(f1 * step, step)
            tab_ref[0, rows, :] = ((ca * cb - sa * sb) * scale).astype(jnp.bfloat16)
            tab_ref[1, rows, :] = (-((sa * cb + ca * sb) * scale)).astype(jnp.bfloat16)

    for s in range(n_src):
        for i in range(n_cmp):
            acc_re = None
            acc_im = None
            for w in range(n_win):
                sre = src_ref[0, w, s, 0, pl.ds(i, 1), :]
                sim = src_ref[0, w, s, 1, pl.ds(i, 1), :]
                rre = rec_ref[w, 0]
                rim = rec_ref[w, 1]
                re = sre * rre + sim * rim
                im = sim * rre - sre * rim
                acc_re = re if acc_re is None else acc_re + re
                acc_im = im if acc_im is None else acc_im + im
            row = (s * n_cmp + i) * n_rows
            rows_ref[0, pl.ds(row, n_rows), :] = acc_re.astype(jnp.bfloat16)
            rows_ref[1, pl.ds(row, n_rows), :] = acc_im.astype(jnp.bfloat16)
    out_ref[0] = jnp.dot(rows_ref[0], tab_ref[0], preferred_element_type=jnp.float32) + jnp.dot(
        rows_ref[1], tab_ref[1], preferred_element_type=jnp.float32
    )


def correlate_all(picked_all, rec, factors, windows):
    steps, n_win, n_src, _, n_cmp, bins = picked_all.shape
    n_rows = rec.shape[2]
    lags = NLAG
    m = n_src * n_cmp * n_rows
    scale = 1.0 / math.sqrt(windows * bins)
    whole = lambda t: (0, 0)
    return pl.pallas_call(
        functools.partial(corr_kernel, scale),
        grid=(steps,),
        in_specs=[
            pl.BlockSpec((1, n_win, n_src, 2, n_cmp, bins), lambda t: (t, 0, 0, 0, 0, 0)),
            pl.BlockSpec(rec.shape, lambda t: (0, 0, 0, 0)),
        ]
        + [pl.BlockSpec(f.shape, whole) for f in factors],
        out_specs=pl.BlockSpec((1, m, lags), lambda t: (t, 0, 0)),
        out_shape=jax.ShapeDtypeStruct((steps, m, lags), jnp.float32),
        scratch_shapes=[
            pltpu.VMEM((2, m, bins), jnp.bfloat16),
            pltpu.VMEM((2, bins, lags), jnp.bfloat16),
        ],
    )(picked_all, rec, *factors)


def win_sum_kernel(x_ref, out_ref, a1, a2, r1, r2, r3, send_sem, recv_sem):
    rows = x_ref.shape[0]
    h, q, e = rows // 2, rows // 4, rows // 8
    coords = [lax.axis_index(a) for a in STA + WIN]
    zl, c = coords[3], coords[4]
    b1 = zl % 2
    b2 = zl // 2
    peer_c = tuple(coords[:4]) + (1 - c,)
    peer_1 = tuple(coords[:3]) + (zl + 1 - 2 * b1, c)
    peer_2 = tuple(coords[:3]) + (zl + 2 - 4 * b2, c)

    barrier = pltpu.get_barrier_semaphore()
    for peer in (peer_c, peer_1, peer_2):
        pl.semaphore_signal(barrier, inc=1, device_id=peer, device_id_type=MESH_ID)
    pl.semaphore_wait(barrier, 3)

    def copy(src, dst, k, peer):
        return pltpu.make_async_remote_copy(
            src_ref=src, dst_ref=dst, send_sem=send_sem.at[k], recv_sem=recv_sem.at[k],
            device_id=peer, device_id_type=MESH_ID)

    mine1 = pl.multiple_of(c * h, 8)
    other1 = pl.multiple_of((1 - c) * h, 8)
    cp = copy(x_ref.at[pl.ds(other1, h)], r1, 0, peer_c)
    cp.start()
    cp.wait()
    a1[...] = x_ref[pl.ds(mine1, h), :] + r1[...]

    mine2 = pl.multiple_of(b1 * q, 8)
    other2 = pl.multiple_of((1 - b1) * q, 8)
    cp = copy(a1.at[pl.ds(other2, q)], r2, 1, peer_1)
    cp.start()
    cp.wait()
    a2[...] = a1[pl.ds(mine2, q), :] + r2[...]

    mine3 = pl.multiple_of(b2 * e, 8)
    other3 = pl.multiple_of((1 - b2) * e, 8)
    cp = copy(a2.at[pl.ds(other3, e)], r3, 2, peer_2)
    cp.start()
    cp.wait()
    base_q = pl.multiple_of(mine1 + mine2, 8)
    at_e = pl.multiple_of(base_q + mine3, 8)
    out_ref[pl.ds(at_e, e), :] = a2[pl.ds(mine3, e), :] + r3[...]

    cp = copy(out_ref.at[pl.ds(at_e, e)], out_ref.at[pl.ds(at_e, e)], 3, peer_2)
    cp.start()
    cp.wait()
    cp = copy(out_ref.at[pl.ds(base_q, q)], out_ref.at[pl.ds(base_q, q)], 4, peer_1)
    cp.start()
    cp.wait()
    cp = copy(out_ref.at[pl.ds(mine1, h)], out_ref.at[pl.ds(mine1, h)], 5, peer_c)
    cp.start()
    cp.wait()


def win_sum(x):
    rows, cols = x.shape
    return pl.pallas_call(
        win_sum_kernel,
        out_shape=jax.ShapeDtypeStruct((rows, cols), jnp.float32),
        in_specs=[pl.BlockSpec(memory_space=pltpu.VMEM)],
        out_specs=pl.BlockSpec(memory_space=pltpu.VMEM),
        scratch_shapes=[
            pltpu.VMEM((rows // 2, cols), jnp.float32),
            pltpu.VMEM((rows // 4, cols), jnp.float32),
            pltpu.VMEM((rows // 2, cols), jnp.float32),
            pltpu.VMEM((rows // 4, cols), jnp.float32),
            pltpu.VMEM((rows // 8, cols), jnp.float32),
            pltpu.SemaphoreType.DMA((6,)),
            pltpu.SemaphoreType.DMA((6,)),
        ],
        compiler_params=pltpu.CompilerParams(collective_id=0, has_side_effects=True),
    )(x)


def bcast_kernel(m_ref, out_ref, rx, s1, ry, piece, zr, rlp, rlm, sx, rxs, sy, rys, agy_s, agy_r, agx_s, agx_r, zsem):
    nx, ny = m_ref.shape[0], m_ref.shape[1]
    hy = ny // 2
    y, x, zh, zl, c = (lax.axis_index(a) for a in STA + WIN)
    xpeer = lambda p: (y, p % nx, zh, zl, c)
    ypeer = lambda p: (p, x, zh, zl, c)
    zpeer = (y, x, 1 - zh, zl, c)
    up, down = (x + 1) % nx, (x + nx - 1) % nx
    far = (x + 2) % nx

    barrier = pltpu.get_barrier_semaphore()
    for p in (up, down):
        pl.semaphore_signal(barrier, inc=1, device_id=xpeer(p), device_id_type=MESH_ID)
    for d in range(1, ny):
        pl.semaphore_signal(barrier, inc=1, device_id=ypeer((y + d) % ny), device_id_type=MESH_ID)
    pl.semaphore_signal(barrier, inc=1, device_id=zpeer, device_id_type=MESH_ID)
    pl.semaphore_wait(barrier, ny + 2)

    def remote(src, dst, ssem, rsem, k, peer):
        cp = pltpu.make_async_remote_copy(
            src_ref=src, dst_ref=dst, send_sem=ssem.at[k], recv_sem=rsem.at[k],
            device_id=peer, device_id_type=MESH_ID)
        cp.start()
        return cp

    lo, hi = pl.ds(0, hy), pl.ds(hy, ny - hy)
    first = [
        remote(m_ref.at[up], rx.at[x], sx, rxs, 0, xpeer(up)),
        remote(m_ref.at[down], rx.at[x], sx, rxs, 1, xpeer(down)),
        remote(m_ref.at[far, lo], rlp, sx, rxs, 2, xpeer(up)),
        remote(m_ref.at[far, hi], rlm, sx, rxs, 3, xpeer(down)),
    ]
    for cp in first:
        cp.wait()
    second = [
        remote(rlp, rx.at[down, lo], sx, rxs, 4, xpeer(up)),
        remote(rlm, rx.at[up, hi], sx, rxs, 5, xpeer(down)),
    ]
    for cp in second:
        cp.wait()
    s1[...] = m_ref[x] + rx[up] + rx[down] + rx[far]

    copies = []
    for d in range(1, ny):
        to = (y + d) % ny
        copies.append(remote(s1.at[to], ry.at[y], sy, rys, d, ypeer(to)))
    for cp in copies:
        cp.wait()
    part = s1[y]
    for d in range(1, ny):
        part = part + ry[(y + ny - d) % ny]
    piece[...] = part

    cp = pltpu.make_async_remote_copy(
        src_ref=piece, dst_ref=zr, send_sem=zsem.at[0], recv_sem=zsem.at[1],
        device_id=zpeer, device_id_type=MESH_ID)
    cp.start()
    cp.wait()
    out_ref[x, y] = piece[...] + zr[...]

    copies = []
    for d in range(1, ny):
        to = (y + d) % ny
        copies.append(remote(out_ref.at[x, y], out_ref.at[x, y], agy_s, agy_r, d, ypeer(to)))
    for cp in copies:
        cp.wait()

    first = [
        remote(out_ref.at[x], out_ref.at[x], agx_s, agx_r, 0, xpeer(up)),
        remote(out_ref.at[x], out_ref.at[x], agx_s, agx_r, 1, xpeer(down)),
    ]
    for cp in first:
        cp.wait()
    second = [
        remote(out_ref.at[down, lo], out_ref.at[down, lo], agx_s, agx_r, 2, xpeer(up)),
        remote(out_ref.at[up, hi], out_ref.at[up, hi], agx_s, agx_r, 3, xpeer(down)),
    ]
    for cp in second:
        cp.wait()


def bcast(masked):
    shape = masked.shape
    nx, ny = shape[0], shape[1]
    return pl.pallas_call(
        bcast_kernel,
        out_shape=jax.ShapeDtypeStruct(shape, jnp.float32),
        in_specs=[pl.BlockSpec(memory_space=pltpu.VMEM)],
        out_specs=pl.BlockSpec(memory_space=pltpu.VMEM),
        scratch_shapes=[
            pltpu.VMEM(shape, jnp.float32),
            pltpu.VMEM(shape[1:], jnp.float32),
            pltpu.VMEM(shape[1:], jnp.float32),
            pltpu.VMEM(shape[2:], jnp.float32),
            pltpu.VMEM(shape[2:], jnp.float32),
            pltpu.VMEM((shape[1] // 2,) + shape[2:], jnp.float32),
            pltpu.VMEM((shape[1] - shape[1] // 2,) + shape[2:], jnp.float32),
            pltpu.SemaphoreType.DMA((6,)),
            pltpu.SemaphoreType.DMA((6,)),
            pltpu.SemaphoreType.DMA((ny,)),
            pltpu.SemaphoreType.DMA((ny,)),
            pltpu.SemaphoreType.DMA((ny,)),
            pltpu.SemaphoreType.DMA((ny,)),
            pltpu.SemaphoreType.DMA((4,)),
            pltpu.SemaphoreType.DMA((4,)),
            pltpu.SemaphoreType.DMA((2,)),
        ],
        compiler_params=pltpu.CompilerParams(collective_id=1, has_side_effects=True),
    )(masked)


def on_device(spectra, flags, owners, source_slots):
    win_count = spectra.shape[0]
    bins = spectra.shape[4]
    weighted = whiten(spectra) * flags.astype(jnp.float32)[:, :, None, None, None]
    n_win = lax.axis_size(WIN)
    factors = lag_factors(bins, NLAG)
    me = lax.axis_index(STA)
    chosen = []
    for step in range(STEPS):
        block = jnp.take(weighted, source_slots[step], axis=1)
        chosen.append(jnp.where(me == owners[step], block, 0.0))
    picked_all = jnp.stack(chosen)
    split = (lax.axis_size("x"), lax.axis_size("y"), -1, 128)
    picked_all = bcast(picked_all.reshape(split)).reshape(picked_all.shape)
    shape = weighted.shape
    rec = weighted.transpose(0, 2, 1, 3, 4).reshape(shape[0], 2, shape[1] * shape[3], shape[4])
    stacked = correlate_all(picked_all, rec, factors, win_count * n_win).reshape(
        STEPS, shape[1], shape[3], shape[1], shape[3], NLAG
    )
    return win_sum(stacked.reshape(-1, NLAG)).reshape(stacked.shape)


def solution(mesh):
    fine = fine_mesh(mesh)
    return jax.shard_map(
        on_device,
        mesh=fine,
        in_specs=(P(WIN, STA, None, None, None), P(WIN, STA), P(), P()),
        out_specs=P(None, None, None, STA, None, None),
        check_vma=False,
    )
```

```python
import functools
import math

import jax
import jax.numpy as jnp
from jax import lax
from jax.experimental import pallas as pl
from jax.experimental.pallas import tpu as pltpu
from jax.sharding import Mesh
from jax.sharding import PartitionSpec as P

NLAG = 768
STEPS = 4
MESH_ID = pl.DeviceIdType.MESH
STA = ("y", "x", "zh")
WIN = ("zl", "c")


def fine_mesh(mesh):
    devs = mesh.devices
    n_sta, n_win = devs.shape
    col = devs[:, 0]
    ny = len({d.coords[1] for d in col})
    nx = len({d.coords[0] for d in col})
    nzh = n_sta // (ny * nx)
    nc = len({d.core_on_chip for d in devs[0, :]})
    nzl = n_win // nc
    return Mesh(devs.reshape(ny, nx, nzh, nzl, nc), STA + WIN)


def whiten(spectra):
    shape = spectra.shape
    blocks = spectra.reshape(shape[0], shape[1], 2, 3, shape[4] // 64, 64)
    power = jnp.mean(blocks * blocks, axis=(2, 3, 5), keepdims=True)
    return (blocks / jnp.sqrt(power + 1e-06)).reshape(shape)


def lag_factors(bins, lags):
    shift = jnp.arange(lags, dtype=jnp.int32) - lags // 2
    hi = jnp.arange(bins // 64, dtype=jnp.int32) * 64 + 360
    lo = jnp.arange(64, dtype=jnp.int32)
    unit = 2.0 * math.pi / 7200.0
    a = jnp.mod(hi[:, None] * shift[None, :], 7200).astype(jnp.float32) * unit
    b = jnp.mod(lo[:, None] * shift[None, :], 7200).astype(jnp.float32) * unit
    return jnp.cos(a), jnp.sin(a), jnp.cos(b), jnp.sin(b)


def corr_kernel(scale, src_ref, rec_ref, ca_ref, sa_ref, cb_ref, sb_ref, out_ref, rows_ref, tab_ref):
    n_win = src_ref.shape[1]
    n_src = src_ref.shape[2]
    n_cmp = src_ref.shape[4]
    n_rows = rec_ref.shape[2]

    @pl.when(pl.program_id(0) == 0)
    def _():
        cb = cb_ref[...]
        sb = sb_ref[...]
        step = cb_ref.shape[0]
        for f1 in range(ca_ref.shape[0]):
            ca = ca_ref[pl.ds(f1, 1), :]
            sa = sa_ref[pl.ds(f1, 1), :]
            rows = pl.ds(f1 * step, step)
            tab_ref[0, rows, :] = ((ca * cb - sa * sb) * scale).astype(jnp.bfloat16)
            tab_ref[1, rows, :] = (-((sa * cb + ca * sb) * scale)).astype(jnp.bfloat16)

    for s in range(n_src):
        for i in range(n_cmp):
            acc_re = None
            acc_im = None
            for w in range(n_win):
                sre = src_ref[0, w, s, 0, pl.ds(i, 1), :]
                sim = src_ref[0, w, s, 1, pl.ds(i, 1), :]
                rre = rec_ref[w, 0]
                rim = rec_ref[w, 1]
                re = sre * rre + sim * rim
                im = sim * rre - sre * rim
                acc_re = re if acc_re is None else acc_re + re
                acc_im = im if acc_im is None else acc_im + im
            row = (s * n_cmp + i) * n_rows
            rows_ref[0, pl.ds(row, n_rows), :] = acc_re.astype(jnp.bfloat16)
            rows_ref[1, pl.ds(row, n_rows), :] = acc_im.astype(jnp.bfloat16)
    out_ref[0] = jnp.dot(rows_ref[0], tab_ref[0], preferred_element_type=jnp.float32) + jnp.dot(
        rows_ref[1], tab_ref[1], preferred_element_type=jnp.float32
    )


def correlate_all(picked_all, rec, factors, windows):
    steps, n_win, n_src, _, n_cmp, bins = picked_all.shape
    n_rows = rec.shape[2]
    lags = NLAG
    m = n_src * n_cmp * n_rows
    scale = 1.0 / math.sqrt(windows * bins)
    whole = lambda t: (0, 0)
    return pl.pallas_call(
        functools.partial(corr_kernel, scale),
        grid=(steps,),
        in_specs=[
            pl.BlockSpec((1, n_win, n_src, 2, n_cmp, bins), lambda t: (t, 0, 0, 0, 0, 0)),
            pl.BlockSpec(rec.shape, lambda t: (0, 0, 0, 0)),
        ]
        + [pl.BlockSpec(f.shape, whole) for f in factors],
        out_specs=pl.BlockSpec((1, m, lags), lambda t: (t, 0, 0)),
        out_shape=jax.ShapeDtypeStruct((steps, m, lags), jnp.float32),
        scratch_shapes=[
            pltpu.VMEM((2, m, bins), jnp.bfloat16),
            pltpu.VMEM((2, bins, lags), jnp.bfloat16),
        ],
    )(picked_all, rec, *factors)


def win_sum_kernel(x_ref, out_ref, a1, a2, r1, r2, r3, send_sem, recv_sem):
    rows = x_ref.shape[0]
    h, q, e = rows // 2, rows // 4, rows // 8
    coords = [lax.axis_index(a) for a in STA + WIN]
    zl, c = coords[3], coords[4]
    b1 = zl % 2
    b2 = zl // 2
    peer_c = tuple(coords[:4]) + (1 - c,)
    peer_1 = tuple(coords[:3]) + (zl + 1 - 2 * b1, c)
    peer_2 = tuple(coords[:3]) + (zl + 2 - 4 * b2, c)

    barrier = pltpu.get_barrier_semaphore()
    for peer in (peer_c, peer_1, peer_2):
        pl.semaphore_signal(barrier, inc=1, device_id=peer, device_id_type=MESH_ID)
    pl.semaphore_wait(barrier, 3)

    def copy(src, dst, k, peer):
        return pltpu.make_async_remote_copy(
            src_ref=src, dst_ref=dst, send_sem=send_sem.at[k], recv_sem=recv_sem.at[k],
            device_id=peer, device_id_type=MESH_ID)

    mine1 = pl.multiple_of(c * h, 8)
    other1 = pl.multiple_of((1 - c) * h, 8)
    cp = copy(x_ref.at[pl.ds(other1, h)], r1, 0, peer_c)
    cp.start()
    cp.wait()
    a1[...] = x_ref[pl.ds(mine1, h), :] + r1[...]

    mine2 = pl.multiple_of(b1 * q, 8)
    other2 = pl.multiple_of((1 - b1) * q, 8)
    cp = copy(a1.at[pl.ds(other2, q)], r2, 1, peer_1)
    cp.start()
    cp.wait()
    a2[...] = a1[pl.ds(mine2, q), :] + r2[...]

    mine3 = pl.multiple_of(b2 * e, 8)
    other3 = pl.multiple_of((1 - b2) * e, 8)
    cp = copy(a2.at[pl.ds(other3, e)], r3, 2, peer_2)
    cp.start()
    cp.wait()
    base_q = pl.multiple_of(mine1 + mine2, 8)
    at_e = pl.multiple_of(base_q + mine3, 8)
    out_ref[pl.ds(at_e, e), :] = a2[pl.ds(mine3, e), :] + r3[...]

    cp = copy(out_ref.at[pl.ds(at_e, e)], out_ref.at[pl.ds(at_e, e)], 3, peer_2)
    cp.start()
    cp.wait()
    cp = copy(out_ref.at[pl.ds(base_q, q)], out_ref.at[pl.ds(base_q, q)], 4, peer_1)
    cp.start()
    cp.wait()
    cp = copy(out_ref.at[pl.ds(mine1, h)], out_ref.at[pl.ds(mine1, h)], 5, peer_c)
    cp.start()
    cp.wait()


def win_sum(x):
    rows, cols = x.shape
    return pl.pallas_call(
        win_sum_kernel,
        out_shape=jax.ShapeDtypeStruct((rows, cols), jnp.float32),
        in_specs=[pl.BlockSpec(memory_space=pltpu.VMEM)],
        out_specs=pl.BlockSpec(memory_space=pltpu.VMEM),
        scratch_shapes=[
            pltpu.VMEM((rows // 2, cols), jnp.float32),
            pltpu.VMEM((rows // 4, cols), jnp.float32),
            pltpu.VMEM((rows // 2, cols), jnp.float32),
            pltpu.VMEM((rows // 4, cols), jnp.float32),
            pltpu.VMEM((rows // 8, cols), jnp.float32),
            pltpu.SemaphoreType.DMA((6,)),
            pltpu.SemaphoreType.DMA((6,)),
        ],
        compiler_params=pltpu.CompilerParams(collective_id=0, has_side_effects=True),
    )(x)


def bcast_kernel(m_ref, out_ref, rx, s1, ry, piece, zr, sx, rxs, sy, rys, agy_s, agy_r, agx_s, agx_r, zsem):
    nx, ny = m_ref.shape[0], m_ref.shape[1]
    y, x, zh, zl, c = (lax.axis_index(a) for a in STA + WIN)
    xpeer = lambda p: (y, p, zh, zl, c)
    ypeer = lambda p: (p, x, zh, zl, c)
    zpeer = (y, x, 1 - zh, zl, c)

    barrier = pltpu.get_barrier_semaphore()
    for d in range(1, nx):
        pl.semaphore_signal(barrier, inc=1, device_id=xpeer((x + d) % nx), device_id_type=MESH_ID)
    for d in range(1, ny):
        pl.semaphore_signal(barrier, inc=1, device_id=ypeer((y + d) % ny), device_id_type=MESH_ID)
    pl.semaphore_signal(barrier, inc=1, device_id=zpeer, device_id_type=MESH_ID)
    pl.semaphore_wait(barrier, nx + ny - 1)

    def send_all(n, me, peer, src, dst, ssem, rsem):
        copies = []
        for d in range(1, n):
            to = (me + d) % n
            cp = pltpu.make_async_remote_copy(
                src_ref=src(to), dst_ref=dst, send_sem=ssem.at[d], recv_sem=rsem.at[d],
                device_id=peer(to), device_id_type=MESH_ID)
            cp.start()
            copies.append(cp)
        for cp in copies:
            cp.wait()

    send_all(nx, x, xpeer, lambda to: m_ref.at[to], rx.at[x], sx, rxs)
    total = m_ref[x]
    for d in range(1, nx):
        total = total + rx[(x + nx - d) % nx]
    s1[...] = total

    send_all(ny, y, ypeer, lambda to: s1.at[to], ry.at[y], sy, rys)
    part = s1[y]
    for d in range(1, ny):
        part = part + ry[(y + ny - d) % ny]
    piece[...] = part

    cp = pltpu.make_async_remote_copy(
        src_ref=piece, dst_ref=zr, send_sem=zsem.at[0], recv_sem=zsem.at[1],
        device_id=zpeer, device_id_type=MESH_ID)
    cp.start()
    cp.wait()
    out_ref[x, y] = piece[...] + zr[...]

    send_all(ny, y, ypeer, lambda to: out_ref.at[x, y], out_ref.at[x, y], agy_s, agy_r)
    send_all(nx, x, xpeer, lambda to: out_ref.at[x], out_ref.at[x], agx_s, agx_r)


def bcast(masked):
    shape = masked.shape
    nx, ny = shape[0], shape[1]
    return pl.pallas_call(
        bcast_kernel,
        out_shape=jax.ShapeDtypeStruct(shape, jnp.float32),
        in_specs=[pl.BlockSpec(memory_space=pltpu.VMEM)],
        out_specs=pl.BlockSpec(memory_space=pltpu.VMEM),
        scratch_shapes=[
            pltpu.VMEM(shape, jnp.float32),
            pltpu.VMEM(shape[1:], jnp.float32),
            pltpu.VMEM(shape[1:], jnp.float32),
            pltpu.VMEM(shape[2:], jnp.float32),
            pltpu.VMEM(shape[2:], jnp.float32),
            pltpu.SemaphoreType.DMA((nx,)),
            pltpu.SemaphoreType.DMA((nx,)),
            pltpu.SemaphoreType.DMA((ny,)),
            pltpu.SemaphoreType.DMA((ny,)),
            pltpu.SemaphoreType.DMA((ny,)),
            pltpu.SemaphoreType.DMA((ny,)),
            pltpu.SemaphoreType.DMA((nx,)),
            pltpu.SemaphoreType.DMA((nx,)),
            pltpu.SemaphoreType.DMA((2,)),
        ],
        compiler_params=pltpu.CompilerParams(collective_id=1, has_side_effects=True),
    )(masked)


def on_device(spectra, flags, owners, source_slots):
    win_count = spectra.shape[0]
    bins = spectra.shape[4]
    weighted = whiten(spectra) * flags.astype(jnp.float32)[:, :, None, None, None]
    n_win = lax.axis_size(WIN)
    factors = lag_factors(bins, NLAG)
    me = lax.axis_index(STA)
    slots = source_slots[:, None, :, None, None, None]
    picked_all = jnp.zeros((STEPS,) + weighted.shape, weighted.dtype)
    for k in range(weighted.shape[1]):
        picked_all = jnp.where(slots == k, weighted[None, :, k : k + 1], picked_all)
    picked_all = jnp.where((me == owners)[:, None, None, None, None, None], picked_all, 0.0)
    split = (lax.axis_size("x"), lax.axis_size("y"), -1, 128)
    picked_all = bcast(picked_all.reshape(split)).reshape(picked_all.shape)
    shape = weighted.shape
    rec = weighted.transpose(0, 2, 1, 3, 4).reshape(shape[0], 2, shape[1] * shape[3], shape[4])
    stacked = correlate_all(picked_all, rec, factors, win_count * n_win).reshape(
        STEPS, shape[1], shape[3], shape[1], shape[3], NLAG
    )
    return win_sum(stacked.reshape(-1, NLAG)).reshape(stacked.shape)


def solution(mesh):
    fine = fine_mesh(mesh)
    return jax.shard_map(
        on_device,
        mesh=fine,
        in_specs=(P(WIN, STA, None, None, None), P(WIN, STA), P(), P()),
        out_specs=P(None, None, None, STA, None, None),
        check_vma=False,
    )
```

```python
import functools
import math

import jax
import jax.numpy as jnp
from jax import lax
from jax.experimental import pallas as pl
from jax.experimental.pallas import tpu as pltpu
from jax.sharding import Mesh
from jax.sharding import PartitionSpec as P

NLAG = 768
STEPS = 4
MESH_ID = pl.DeviceIdType.MESH
STA = ("y", "x", "zh")
WIN = ("zl", "c")


def fine_mesh(mesh):
    devs = mesh.devices
    n_sta, n_win = devs.shape
    col = devs[:, 0]
    ny = len({d.coords[1] for d in col})
    nx = len({d.coords[0] for d in col})
    nzh = n_sta // (ny * nx)
    nc = len({d.core_on_chip for d in devs[0, :]})
    nzl = n_win // nc
    return Mesh(devs.reshape(ny, nx, nzh, nzl, nc), STA + WIN)


def whiten(spectra):
    shape = spectra.shape
    blocks = spectra.reshape(shape[0], shape[1], 2, 3, shape[4] // 64, 64)
    power = jnp.mean(blocks * blocks, axis=(2, 3, 5), keepdims=True)
    return (blocks / jnp.sqrt(power + 1e-06)).reshape(shape)


def lag_factors(bins, lags):
    shift = jnp.arange(lags, dtype=jnp.int32) - lags // 2
    hi = jnp.arange(bins // 64, dtype=jnp.int32) * 64 + 360
    lo = jnp.arange(64, dtype=jnp.int32)
    unit = 2.0 * math.pi / 7200.0
    a = jnp.mod(hi[:, None] * shift[None, :], 7200).astype(jnp.float32) * unit
    b = jnp.mod(lo[:, None] * shift[None, :], 7200).astype(jnp.float32) * unit
    return jnp.cos(a), jnp.sin(a), jnp.cos(b), jnp.sin(b)


def corr_kernel(scale, src_ref, rec_ref, ca_ref, sa_ref, cb_ref, sb_ref, out_ref, rows_ref, tab_ref):
    n_win = rec_ref.shape[0]
    n_src = src_ref.shape[1] // n_win
    n_cmp = src_ref.shape[2] // 2
    n_rows = rec_ref.shape[2]

    @pl.when(pl.program_id(0) == 0)
    def _():
        cb = cb_ref[...]
        sb = sb_ref[...]
        step = cb_ref.shape[0]
        for f1 in range(ca_ref.shape[0]):
            ca = ca_ref[pl.ds(f1, 1), :]
            sa = sa_ref[pl.ds(f1, 1), :]
            rows = pl.ds(f1 * step, step)
            tab_ref[0, rows, :] = ((ca * cb - sa * sb) * scale).astype(jnp.bfloat16)
            tab_ref[1, rows, :] = (-((sa * cb + ca * sb) * scale)).astype(jnp.bfloat16)

    for s in range(n_src):
        for i in range(n_cmp):
            acc_re = None
            acc_im = None
            for w in range(n_win):
                sre = src_ref[0, w * n_src + s, pl.ds(i, 1), :]
                sim = src_ref[0, w * n_src + s, pl.ds(n_cmp + i, 1), :]
                rre = rec_ref[w, 0]
                rim = rec_ref[w, 1]
                re = sre * rre + sim * rim
                im = sim * rre - sre * rim
                acc_re = re if acc_re is None else acc_re + re
                acc_im = im if acc_im is None else acc_im + im
            row = (s * n_cmp + i) * n_rows
            rows_ref[0, pl.ds(row, n_rows), :] = acc_re.astype(jnp.bfloat16)
            rows_ref[1, pl.ds(row, n_rows), :] = acc_im.astype(jnp.bfloat16)
    out_ref[0] = jnp.dot(rows_ref[0], tab_ref[0], preferred_element_type=jnp.float32) + jnp.dot(
        rows_ref[1], tab_ref[1], preferred_element_type=jnp.float32
    )


def correlate_all(picked_all, rec, factors, windows):
    steps, n_ws, n_ri, bins = picked_all.shape
    n_win = rec.shape[0]
    n_src, n_cmp = n_ws // n_win, n_ri // 2
    n_rows = rec.shape[2]
    lags = NLAG
    m = n_src * n_cmp * n_rows
    scale = 1.0 / math.sqrt(windows * bins)
    whole = lambda t: (0, 0)
    return pl.pallas_call(
        functools.partial(corr_kernel, scale),
        grid=(steps,),
        in_specs=[
            pl.BlockSpec((1, n_ws, n_ri, bins), lambda t: (t, 0, 0, 0)),
            pl.BlockSpec(rec.shape, lambda t: (0, 0, 0, 0)),
        ]
        + [pl.BlockSpec(f.shape, whole) for f in factors],
        out_specs=pl.BlockSpec((1, m, lags), lambda t: (t, 0, 0)),
        out_shape=jax.ShapeDtypeStruct((steps, m, lags), jnp.float32),
        scratch_shapes=[
            pltpu.VMEM((2, m, bins), jnp.bfloat16),
            pltpu.VMEM((2, bins, lags), jnp.bfloat16),
        ],
    )(picked_all, rec, *factors)


def win_sum_kernel(x_ref, out_ref, a1, a2, r1, r2, r3, send_sem, recv_sem):
    rows = x_ref.shape[0]
    h, q, e = rows // 2, rows // 4, rows // 8
    coords = [lax.axis_index(a) for a in STA + WIN]
    zl, c = coords[3], coords[4]
    b1 = zl % 2
    b2 = zl // 2
    peer_c = tuple(coords[:4]) + (1 - c,)
    peer_1 = tuple(coords[:3]) + (zl + 1 - 2 * b1, c)
    peer_2 = tuple(coords[:3]) + (zl + 2 - 4 * b2, c)

    barrier = pltpu.get_barrier_semaphore()
    for peer in (peer_c, peer_1, peer_2):
        pl.semaphore_signal(barrier, inc=1, device_id=peer, device_id_type=MESH_ID)
    pl.semaphore_wait(barrier, 3)

    def copy(src, dst, k, peer):
        return pltpu.make_async_remote_copy(
            src_ref=src, dst_ref=dst, send_sem=send_sem.at[k], recv_sem=recv_sem.at[k],
            device_id=peer, device_id_type=MESH_ID)

    mine1 = pl.multiple_of(c * h, 8)
    other1 = pl.multiple_of((1 - c) * h, 8)
    cp = copy(x_ref.at[pl.ds(other1, h)], r1, 0, peer_c)
    cp.start()
    cp.wait()
    a1[...] = x_ref[pl.ds(mine1, h), :] + r1[...]

    mine2 = pl.multiple_of(b1 * q, 8)
    other2 = pl.multiple_of((1 - b1) * q, 8)
    cp = copy(a1.at[pl.ds(other2, q)], r2, 1, peer_1)
    cp.start()
    cp.wait()
    a2[...] = a1[pl.ds(mine2, q), :] + r2[...]

    mine3 = pl.multiple_of(b2 * e, 8)
    other3 = pl.multiple_of((1 - b2) * e, 8)
    cp = copy(a2.at[pl.ds(other3, e)], r3, 2, peer_2)
    cp.start()
    cp.wait()
    base_q = pl.multiple_of(mine1 + mine2, 8)
    at_e = pl.multiple_of(base_q + mine3, 8)
    out_ref[pl.ds(at_e, e), :] = a2[pl.ds(mine3, e), :] + r3[...]

    cp = copy(out_ref.at[pl.ds(at_e, e)], out_ref.at[pl.ds(at_e, e)], 3, peer_2)
    cp.start()
    cp.wait()
    cp = copy(out_ref.at[pl.ds(base_q, q)], out_ref.at[pl.ds(base_q, q)], 4, peer_1)
    cp.start()
    cp.wait()
    cp = copy(out_ref.at[pl.ds(mine1, h)], out_ref.at[pl.ds(mine1, h)], 5, peer_c)
    cp.start()
    cp.wait()


def win_sum(x):
    rows, cols = x.shape
    return pl.pallas_call(
        win_sum_kernel,
        out_shape=jax.ShapeDtypeStruct((rows, cols), jnp.float32),
        in_specs=[pl.BlockSpec(memory_space=pltpu.VMEM)],
        out_specs=pl.BlockSpec(memory_space=pltpu.VMEM),
        scratch_shapes=[
            pltpu.VMEM((rows // 2, cols), jnp.float32),
            pltpu.VMEM((rows // 4, cols), jnp.float32),
            pltpu.VMEM((rows // 2, cols), jnp.float32),
            pltpu.VMEM((rows // 4, cols), jnp.float32),
            pltpu.VMEM((rows // 8, cols), jnp.float32),
            pltpu.SemaphoreType.DMA((6,)),
            pltpu.SemaphoreType.DMA((6,)),
        ],
        compiler_params=pltpu.CompilerParams(collective_id=0, has_side_effects=True),
    )(x)


def bcast_kernel(m_ref, out_ref, rx, s1, ry, piece, zr, sx, rxs, sy, rys, agy_s, agy_r, agx_s, agx_r, zsem):
    nx, ny = m_ref.shape[0], m_ref.shape[1]
    y, x, zh, zl, c = (lax.axis_index(a) for a in STA + WIN)
    xpeer = lambda p: (y, p, zh, zl, c)
    ypeer = lambda p: (p, x, zh, zl, c)
    zpeer = (y, x, 1 - zh, zl, c)

    barrier = pltpu.get_barrier_semaphore()
    for d in range(1, nx):
        pl.semaphore_signal(barrier, inc=1, device_id=xpeer((x + d) % nx), device_id_type=MESH_ID)
    for d in range(1, ny):
        pl.semaphore_signal(barrier, inc=1, device_id=ypeer((y + d) % ny), device_id_type=MESH_ID)
    pl.semaphore_signal(barrier, inc=1, device_id=zpeer, device_id_type=MESH_ID)
    pl.semaphore_wait(barrier, nx + ny - 1)

    def send_all(n, me, peer, src, dst, ssem, rsem):
        copies = []
        for d in range(1, n):
            to = (me + d) % n
            cp = pltpu.make_async_remote_copy(
                src_ref=src(to), dst_ref=dst, send_sem=ssem.at[d], recv_sem=rsem.at[d],
                device_id=peer(to), device_id_type=MESH_ID)
            cp.start()
            copies.append(cp)
        for cp in copies:
            cp.wait()

    send_all(nx, x, xpeer, lambda to: m_ref.at[to], rx.at[x], sx, rxs)
    total = m_ref[x]
    for d in range(1, nx):
        total = total + rx[(x + nx - d) % nx]
    s1[...] = total

    send_all(ny, y, ypeer, lambda to: s1.at[to], ry.at[y], sy, rys)
    part = s1[y]
    for d in range(1, ny):
        part = part + ry[(y + ny - d) % ny]
    piece[...] = part

    cp = pltpu.make_async_remote_copy(
        src_ref=piece, dst_ref=zr, send_sem=zsem.at[0], recv_sem=zsem.at[1],
        device_id=zpeer, device_id_type=MESH_ID)
    cp.start()
    cp.wait()
    out_ref[x, y] = piece[...] + zr[...]

    send_all(ny, y, ypeer, lambda to: out_ref.at[x, y], out_ref.at[x, y], agy_s, agy_r)
    send_all(nx, x, xpeer, lambda to: out_ref.at[x], out_ref.at[x], agx_s, agx_r)


def bcast(masked):
    shape = masked.shape
    nx, ny = shape[0], shape[1]
    return pl.pallas_call(
        bcast_kernel,
        out_shape=jax.ShapeDtypeStruct(shape, jnp.float32),
        in_specs=[pl.BlockSpec(memory_space=pltpu.VMEM)],
        out_specs=pl.BlockSpec(memory_space=pltpu.VMEM),
        scratch_shapes=[
            pltpu.VMEM(shape, jnp.float32),
            pltpu.VMEM(shape[1:], jnp.float32),
            pltpu.VMEM(shape[1:], jnp.float32),
            pltpu.VMEM(shape[2:], jnp.float32),
            pltpu.VMEM(shape[2:], jnp.float32),
            pltpu.SemaphoreType.DMA((nx,)),
            pltpu.SemaphoreType.DMA((nx,)),
            pltpu.SemaphoreType.DMA((ny,)),
            pltpu.SemaphoreType.DMA((ny,)),
            pltpu.SemaphoreType.DMA((ny,)),
            pltpu.SemaphoreType.DMA((ny,)),
            pltpu.SemaphoreType.DMA((nx,)),
            pltpu.SemaphoreType.DMA((nx,)),
            pltpu.SemaphoreType.DMA((2,)),
        ],
        compiler_params=pltpu.CompilerParams(collective_id=1, has_side_effects=True),
    )(masked)


def on_device(spectra, flags, owners, source_slots):
    win_count = spectra.shape[0]
    bins = spectra.shape[4]
    weighted = whiten(spectra) * flags.astype(jnp.float32)[:, :, None, None, None]
    n_win = lax.axis_size(WIN)
    factors = lag_factors(bins, NLAG)
    me = lax.axis_index(STA)
    slots = source_slots[:, None, :, None, None, None]
    picked_all = jnp.zeros((STEPS,) + weighted.shape, weighted.dtype)
    for k in range(weighted.shape[1]):
        picked_all = jnp.where(slots == k, weighted[None, :, k : k + 1], picked_all)
    picked_all = jnp.where((me == owners)[:, None, None, None, None, None], picked_all, 0.0)
    shape6 = picked_all.shape
    split = (lax.axis_size("x"), lax.axis_size("y"), -1, shape6[-1])
    rows = (STEPS, shape6[1] * shape6[2], shape6[3] * shape6[4], shape6[5])
    picked_all = bcast(picked_all.reshape(split)).reshape(rows)
    shape = weighted.shape
    rec = weighted.transpose(0, 2, 1, 3, 4).reshape(shape[0], 2, shape[1] * shape[3], shape[4])
    stacked = correlate_all(picked_all, rec, factors, win_count * n_win).reshape(
        STEPS, shape[1], shape[3], shape[1], shape[3], NLAG
    )
    return win_sum(stacked.reshape(-1, NLAG)).reshape(stacked.shape)


def solution(mesh):
    fine = fine_mesh(mesh)
    return jax.shard_map(
        on_device,
        mesh=fine,
        in_specs=(P(WIN, STA, None, None, None), P(WIN, STA), P(), P()),
        out_specs=P(None, None, None, STA, None, None),
        check_vma=False,
    )
```

```python
import functools
import math

import jax
import jax.numpy as jnp
from jax import lax
from jax.experimental import pallas as pl
from jax.experimental.pallas import tpu as pltpu
from jax.sharding import Mesh
from jax.sharding import PartitionSpec as P

NLAG = 768
STEPS = 4
MESH_ID = pl.DeviceIdType.MESH
WIN_CHUNKS = 3
STA = ("y", "x", "zh")
WIN = ("zl", "c")


def fine_mesh(mesh):
    devs = mesh.devices
    n_sta, n_win = devs.shape
    col = devs[:, 0]
    ny = len({d.coords[1] for d in col})
    nx = len({d.coords[0] for d in col})
    nzh = n_sta // (ny * nx)
    nc = len({d.core_on_chip for d in devs[0, :]})
    nzl = n_win // nc
    return Mesh(devs.reshape(ny, nx, nzh, nzl, nc), STA + WIN)


def whiten(spectra):
    shape = spectra.shape
    blocks = spectra.reshape(shape[0], shape[1], 2, 3, shape[4] // 64, 64)
    power = jnp.mean(blocks * blocks, axis=(2, 3, 5), keepdims=True)
    return (blocks / jnp.sqrt(power + 1e-06)).reshape(shape)


def lag_factors(bins, lags):
    shift = jnp.arange(lags, dtype=jnp.int32) - lags // 2
    hi = jnp.arange(bins // 64, dtype=jnp.int32) * 64 + 360
    lo = jnp.arange(64, dtype=jnp.int32)
    unit = 2.0 * math.pi / 7200.0
    a = jnp.mod(hi[:, None] * shift[None, :], 7200).astype(jnp.float32) * unit
    b = jnp.mod(lo[:, None] * shift[None, :], 7200).astype(jnp.float32) * unit
    return jnp.cos(a), jnp.sin(a), jnp.cos(b), jnp.sin(b)


def corr_kernel(scale, src_ref, rec_ref, ca_ref, sa_ref, cb_ref, sb_ref, out_ref, rows_ref, tab_ref):
    n_win = src_ref.shape[1]
    n_src = src_ref.shape[2]
    n_cmp = src_ref.shape[4]
    n_rows = rec_ref.shape[2]

    @pl.when(pl.program_id(0) == 0)
    def _():
        cb = cb_ref[...]
        sb = sb_ref[...]
        step = cb_ref.shape[0]
        for f1 in range(ca_ref.shape[0]):
            ca = ca_ref[pl.ds(f1, 1), :]
            sa = sa_ref[pl.ds(f1, 1), :]
            rows = pl.ds(f1 * step, step)
            tab_ref[0, rows, :] = ((ca * cb - sa * sb) * scale).astype(jnp.bfloat16)
            tab_ref[1, rows, :] = (-((sa * cb + ca * sb) * scale)).astype(jnp.bfloat16)

    for s in range(n_src):
        for i in range(n_cmp):
            acc_re = None
            acc_im = None
            for w in range(n_win):
                sre = src_ref[0, w, s, 0, pl.ds(i, 1), :]
                sim = src_ref[0, w, s, 1, pl.ds(i, 1), :]
                rre = rec_ref[w, 0]
                rim = rec_ref[w, 1]
                re = sre * rre + sim * rim
                im = sim * rre - sre * rim
                acc_re = re if acc_re is None else acc_re + re
                acc_im = im if acc_im is None else acc_im + im
            row = (s * n_cmp + i) * n_rows
            rows_ref[0, pl.ds(row, n_rows), :] = acc_re.astype(jnp.bfloat16)
            rows_ref[1, pl.ds(row, n_rows), :] = acc_im.astype(jnp.bfloat16)
    out_ref[0] = jnp.dot(rows_ref[0], tab_ref[0], preferred_element_type=jnp.float32) + jnp.dot(
        rows_ref[1], tab_ref[1], preferred_element_type=jnp.float32
    )


def correlate_all(picked_all, rec, factors, windows):
    steps, n_win, n_src, _, n_cmp, bins = picked_all.shape
    n_rows = rec.shape[2]
    lags = NLAG
    m = n_src * n_cmp * n_rows
    scale = 1.0 / math.sqrt(windows * bins)
    whole = lambda t: (0, 0)
    return pl.pallas_call(
        functools.partial(corr_kernel, scale),
        grid=(steps,),
        in_specs=[
            pl.BlockSpec((1, n_win, n_src, 2, n_cmp, bins), lambda t: (t, 0, 0, 0, 0, 0)),
            pl.BlockSpec(rec.shape, lambda t: (0, 0, 0, 0)),
        ]
        + [pl.BlockSpec(f.shape, whole) for f in factors],
        out_specs=pl.BlockSpec((1, m, lags), lambda t: (t, 0, 0)),
        out_shape=jax.ShapeDtypeStruct((steps, m, lags), jnp.float32),
        scratch_shapes=[
            pltpu.VMEM((2, m, bins), jnp.bfloat16),
            pltpu.VMEM((2, bins, lags), jnp.bfloat16),
        ],
    )(picked_all, rec, *factors)


def win_sum_kernel(x_ref, out_ref, a1, a2, r1, r2, r3, send_sem, recv_sem):
    rows = x_ref.shape[0]
    h, q, e = rows // 2, rows // 4, rows // 8
    coords = [lax.axis_index(a) for a in STA + WIN]
    zl, c = coords[3], coords[4]
    b1 = zl % 2
    b2 = zl // 2
    peer_c = tuple(coords[:4]) + (1 - c,)
    peer_1 = tuple(coords[:3]) + (zl + 1 - 2 * b1, c)
    peer_2 = tuple(coords[:3]) + (zl + 2 - 4 * b2, c)

    barrier = pltpu.get_barrier_semaphore()
    for peer in (peer_c, peer_1, peer_2):
        pl.semaphore_signal(barrier, inc=1, device_id=peer, device_id_type=MESH_ID)
    pl.semaphore_wait(barrier, 3)

    chunks = send_sem.shape[0] // 6
    width = x_ref.shape[1] // chunks

    class copy:
        def __init__(self, src, dst, k, peer):
            self.parts = [
                pltpu.make_async_remote_copy(
                    src_ref=src.at[:, pl.ds(j * width, width)],
                    dst_ref=dst.at[:, pl.ds(j * width, width)],
                    send_sem=send_sem.at[k * chunks + j], recv_sem=recv_sem.at[k * chunks + j],
                    device_id=peer, device_id_type=MESH_ID)
                for j in range(chunks)
            ]

        def start(self):
            for part in self.parts:
                part.start()

        def wait(self):
            for part in self.parts:
                part.wait()

    mine1 = pl.multiple_of(c * h, 8)
    other1 = pl.multiple_of((1 - c) * h, 8)
    cp = copy(x_ref.at[pl.ds(other1, h)], r1, 0, peer_c)
    cp.start()
    cp.wait()
    a1[...] = x_ref[pl.ds(mine1, h), :] + r1[...]

    mine2 = pl.multiple_of(b1 * q, 8)
    other2 = pl.multiple_of((1 - b1) * q, 8)
    cp = copy(a1.at[pl.ds(other2, q)], r2, 1, peer_1)
    cp.start()
    cp.wait()
    a2[...] = a1[pl.ds(mine2, q), :] + r2[...]

    mine3 = pl.multiple_of(b2 * e, 8)
    other3 = pl.multiple_of((1 - b2) * e, 8)
    cp = copy(a2.at[pl.ds(other3, e)], r3, 2, peer_2)
    cp.start()
    cp.wait()
    base_q = pl.multiple_of(mine1 + mine2, 8)
    at_e = pl.multiple_of(base_q + mine3, 8)
    out_ref[pl.ds(at_e, e), :] = a2[pl.ds(mine3, e), :] + r3[...]

    cp = copy(out_ref.at[pl.ds(at_e, e)], out_ref.at[pl.ds(at_e, e)], 3, peer_2)
    cp.start()
    cp.wait()
    cp = copy(out_ref.at[pl.ds(base_q, q)], out_ref.at[pl.ds(base_q, q)], 4, peer_1)
    cp.start()
    cp.wait()
    cp = copy(out_ref.at[pl.ds(mine1, h)], out_ref.at[pl.ds(mine1, h)], 5, peer_c)
    cp.start()
    cp.wait()


def win_sum(x):
    rows, cols = x.shape
    return pl.pallas_call(
        win_sum_kernel,
        out_shape=jax.ShapeDtypeStruct((rows, cols), jnp.float32),
        in_specs=[pl.BlockSpec(memory_space=pltpu.VMEM)],
        out_specs=pl.BlockSpec(memory_space=pltpu.VMEM),
        scratch_shapes=[
            pltpu.VMEM((rows // 2, cols), jnp.float32),
            pltpu.VMEM((rows // 4, cols), jnp.float32),
            pltpu.VMEM((rows // 2, cols), jnp.float32),
            pltpu.VMEM((rows // 4, cols), jnp.float32),
            pltpu.VMEM((rows // 8, cols), jnp.float32),
            pltpu.SemaphoreType.DMA((6 * WIN_CHUNKS,)),
            pltpu.SemaphoreType.DMA((6 * WIN_CHUNKS,)),
        ],
        compiler_params=pltpu.CompilerParams(collective_id=0, has_side_effects=True),
    )(x)


def bcast_kernel(m_ref, out_ref, rx, s1, ry, piece, zr, sx, rxs, sy, rys, agy_s, agy_r, agx_s, agx_r, zsem):
    nx, ny = m_ref.shape[0], m_ref.shape[1]
    y, x, zh, zl, c = (lax.axis_index(a) for a in STA + WIN)
    xpeer = lambda p: (y, p, zh, zl, c)
    ypeer = lambda p: (p, x, zh, zl, c)
    zpeer = (y, x, 1 - zh, zl, c)

    barrier = pltpu.get_barrier_semaphore()
    for d in range(1, nx):
        pl.semaphore_signal(barrier, inc=1, device_id=xpeer((x + d) % nx), device_id_type=MESH_ID)
    for d in range(1, ny):
        pl.semaphore_signal(barrier, inc=1, device_id=ypeer((y + d) % ny), device_id_type=MESH_ID)
    pl.semaphore_signal(barrier, inc=1, device_id=zpeer, device_id_type=MESH_ID)
    pl.semaphore_wait(barrier, nx + ny - 1)

    def send_all(n, me, peer, src, dst, ssem, rsem):
        copies = []
        for d in range(1, n):
            to = (me + d) % n
            cp = pltpu.make_async_remote_copy(
                src_ref=src(to), dst_ref=dst, send_sem=ssem.at[d], recv_sem=rsem.at[d],
                device_id=peer(to), device_id_type=MESH_ID)
            cp.start()
            copies.append(cp)
        for cp in copies:
            cp.wait()

    send_all(nx, x, xpeer, lambda to: m_ref.at[to], rx.at[x], sx, rxs)
    total = m_ref[x]
    for d in range(1, nx):
        total = total + rx[(x + nx - d) % nx]
    s1[...] = total

    send_all(ny, y, ypeer, lambda to: s1.at[to], ry.at[y], sy, rys)
    part = s1[y]
    for d in range(1, ny):
        part = part + ry[(y + ny - d) % ny]
    piece[...] = part

    cp = pltpu.make_async_remote_copy(
        src_ref=piece, dst_ref=zr, send_sem=zsem.at[0], recv_sem=zsem.at[1],
        device_id=zpeer, device_id_type=MESH_ID)
    cp.start()
    cp.wait()
    out_ref[x, y] = piece[...] + zr[...]

    send_all(ny, y, ypeer, lambda to: out_ref.at[x, y], out_ref.at[x, y], agy_s, agy_r)
    send_all(nx, x, xpeer, lambda to: out_ref.at[x], out_ref.at[x], agx_s, agx_r)


def bcast(masked):
    shape = masked.shape
    nx, ny = shape[0], shape[1]
    return pl.pallas_call(
        bcast_kernel,
        out_shape=jax.ShapeDtypeStruct(shape, jnp.float32),
        in_specs=[pl.BlockSpec(memory_space=pltpu.VMEM)],
        out_specs=pl.BlockSpec(memory_space=pltpu.VMEM),
        scratch_shapes=[
            pltpu.VMEM(shape, jnp.float32),
            pltpu.VMEM(shape[1:], jnp.float32),
            pltpu.VMEM(shape[1:], jnp.float32),
            pltpu.VMEM(shape[2:], jnp.float32),
            pltpu.VMEM(shape[2:], jnp.float32),
            pltpu.SemaphoreType.DMA((nx,)),
            pltpu.SemaphoreType.DMA((nx,)),
            pltpu.SemaphoreType.DMA((ny,)),
            pltpu.SemaphoreType.DMA((ny,)),
            pltpu.SemaphoreType.DMA((ny,)),
            pltpu.SemaphoreType.DMA((ny,)),
            pltpu.SemaphoreType.DMA((nx,)),
            pltpu.SemaphoreType.DMA((nx,)),
            pltpu.SemaphoreType.DMA((2,)),
        ],
        compiler_params=pltpu.CompilerParams(collective_id=1, has_side_effects=True),
    )(masked)


def on_device(spectra, flags, owners, source_slots):
    win_count = spectra.shape[0]
    bins = spectra.shape[4]
    weighted = whiten(spectra) * flags.astype(jnp.float32)[:, :, None, None, None]
    n_win = lax.axis_size(WIN)
    factors = lag_factors(bins, NLAG)
    me = lax.axis_index(STA)
    slots = source_slots[:, None, :, None, None, None]
    picked_all = jnp.zeros((STEPS,) + weighted.shape, weighted.dtype)
    for k in range(weighted.shape[1]):
        picked_all = jnp.where(slots == k, weighted[None, :, k : k + 1], picked_all)
    picked_all = jnp.where((me == owners)[:, None, None, None, None, None], picked_all, 0.0)
    split = (lax.axis_size("x"), lax.axis_size("y"), -1, 128)
    picked_all = bcast(picked_all.reshape(split)).reshape(picked_all.shape)
    shape = weighted.shape
    rec = weighted.transpose(0, 2, 1, 3, 4).reshape(shape[0], 2, shape[1] * shape[3], shape[4])
    stacked = correlate_all(picked_all, rec, factors, win_count * n_win).reshape(
        STEPS, shape[1], shape[3], shape[1], shape[3], NLAG
    )
    return win_sum(stacked.reshape(-1, NLAG)).reshape(stacked.shape)


def solution(mesh):
    fine = fine_mesh(mesh)
    return jax.shard_map(
        on_device,
        mesh=fine,
        in_specs=(P(WIN, STA, None, None, None), P(WIN, STA), P(), P()),
        out_specs=P(None, None, None, STA, None, None),
        check_vma=False,
    )
```

```python
import functools
import math

import jax
import jax.numpy as jnp
from jax import lax
from jax.experimental import pallas as pl
from jax.experimental.pallas import tpu as pltpu
from jax.sharding import Mesh
from jax.sharding import PartitionSpec as P

NLAG = 768
STEPS = 4
MESH_ID = pl.DeviceIdType.MESH
STA = ("y", "x", "zh")
WIN = ("zl", "c")


def fine_mesh(mesh):
    devs = mesh.devices
    n_sta, n_win = devs.shape
    col = devs[:, 0]
    ny = len({d.coords[1] for d in col})
    nx = len({d.coords[0] for d in col})
    nzh = n_sta // (ny * nx)
    nc = len({d.core_on_chip for d in devs[0, :]})
    nzl = n_win // nc
    return Mesh(devs.reshape(ny, nx, nzh, nzl, nc), STA + WIN)


def whiten(spectra):
    shape = spectra.shape
    blocks = spectra.reshape(shape[0], shape[1], 2, 3, shape[4] // 64, 64)
    power = jnp.mean(blocks * blocks, axis=(2, 3, 5), keepdims=True)
    return (blocks / jnp.sqrt(power + 1e-06)).reshape(shape)


def lag_factors(bins, lags):
    shift = jnp.arange(lags, dtype=jnp.int32) - lags // 2
    hi = jnp.arange(bins // 64, dtype=jnp.int32) * 64 + 360
    lo = jnp.arange(64, dtype=jnp.int32)
    unit = 2.0 * math.pi / 7200.0
    a = jnp.mod(hi[:, None] * shift[None, :], 7200).astype(jnp.float32) * unit
    b = jnp.mod(lo[:, None] * shift[None, :], 7200).astype(jnp.float32) * unit
    return jnp.cos(a), jnp.sin(a), jnp.cos(b), jnp.sin(b)


def corr_kernel(scale, src_ref, rec_ref, ca_ref, sa_ref, cb_ref, sb_ref, out_ref, rows_ref, tab_ref):
    n_win = src_ref.shape[1]
    n_src = src_ref.shape[2]
    n_cmp = src_ref.shape[4]
    n_rows = rec_ref.shape[2]

    @pl.when(pl.program_id(0) == 0)
    def _():
        cb = cb_ref[...]
        sb = sb_ref[...]
        step = cb_ref.shape[0]
        for f1 in range(ca_ref.shape[0]):
            ca = ca_ref[pl.ds(f1, 1), :]
            sa = sa_ref[pl.ds(f1, 1), :]
            rows = pl.ds(f1 * step, step)
            tab_ref[0, rows, :] = ((ca * cb - sa * sb) * scale).astype(jnp.bfloat16)
            tab_ref[1, rows, :] = (-((sa * cb + ca * sb) * scale)).astype(jnp.bfloat16)

    for s in range(n_src):
        for i in range(n_cmp):
            acc_re = None
            acc_im = None
            for w in range(n_win):
                sre = src_ref[0, w, s, 0, pl.ds(i, 1), :]
                sim = src_ref[0, w, s, 1, pl.ds(i, 1), :]
                rre = rec_ref[w, 0]
                rim = rec_ref[w, 1]
                re = sre * rre + sim * rim
                im = sim * rre - sre * rim
                acc_re = re if acc_re is None else acc_re + re
                acc_im = im if acc_im is None else acc_im + im
            row = (s * n_cmp + i) * n_rows
            rows_ref[0, pl.ds(row, n_rows), :] = acc_re.astype(jnp.bfloat16)
            rows_ref[1, pl.ds(row, n_rows), :] = acc_im.astype(jnp.bfloat16)
    out_ref[0] = jnp.dot(rows_ref[0], tab_ref[0], preferred_element_type=jnp.float32) + jnp.dot(
        rows_ref[1], tab_ref[1], preferred_element_type=jnp.float32
    )


def correlate_all(picked_all, rec, factors, windows):
    steps, n_win, n_src, _, n_cmp, bins = picked_all.shape
    n_rows = rec.shape[2]
    lags = NLAG
    m = n_src * n_cmp * n_rows
    scale = 1.0 / math.sqrt(windows * bins)
    whole = lambda t: (0, 0)
    return pl.pallas_call(
        functools.partial(corr_kernel, scale),
        grid=(steps,),
        in_specs=[
            pl.BlockSpec((1, n_win, n_src, 2, n_cmp, bins), lambda t: (t, 0, 0, 0, 0, 0)),
            pl.BlockSpec(rec.shape, lambda t: (0, 0, 0, 0)),
        ]
        + [pl.BlockSpec(f.shape, whole) for f in factors],
        out_specs=pl.BlockSpec((1, m, lags), lambda t: (t, 0, 0)),
        out_shape=jax.ShapeDtypeStruct((steps, m, lags), jnp.float32),
        scratch_shapes=[
            pltpu.VMEM((2, m, bins), jnp.bfloat16),
            pltpu.VMEM((2, bins, lags), jnp.bfloat16),
        ],
    )(picked_all, rec, *factors)


def win_sum_kernel(x_ref, out_ref, a1, a2, r1, r2, r3, send_sem, recv_sem):
    rows = x_ref.shape[0]
    h, q, e = rows // 2, rows // 4, rows // 8
    coords = [lax.axis_index(a) for a in STA + WIN]
    zl, c = coords[3], coords[4]
    b1 = zl % 2
    b2 = zl // 2
    peer_c = tuple(coords[:4]) + (1 - c,)
    peer_1 = tuple(coords[:3]) + (zl + 1 - 2 * b1, c)
    peer_2 = tuple(coords[:3]) + (zl + 2 - 4 * b2, c)

    barrier = pltpu.get_barrier_semaphore()
    for peer in (peer_c, peer_1, peer_2):
        pl.semaphore_signal(barrier, inc=1, device_id=peer, device_id_type=MESH_ID)
    pl.semaphore_wait(barrier, 3)

    def copy(src, dst, k, peer):
        return pltpu.make_async_remote_copy(
            src_ref=src, dst_ref=dst, send_sem=send_sem.at[k], recv_sem=recv_sem.at[k],
            device_id=peer, device_id_type=MESH_ID)

    mine1 = pl.multiple_of(c * h, 8)
    other1 = pl.multiple_of((1 - c) * h, 8)
    mine2 = pl.multiple_of(b1 * q, 8)
    other2 = pl.multiple_of((1 - b1) * q, 8)
    first_c = copy(x_ref.at[pl.ds(other1 + other2, q)], r1.at[pl.ds(other2, q)], 0, peer_c)
    first_c.start()
    second_c = copy(x_ref.at[pl.ds(other1 + mine2, q)], r1.at[pl.ds(mine2, q)], 1, peer_c)
    second_c.start()
    first_c.wait()
    a1[pl.ds(other2, q), :] = x_ref[pl.ds(mine1 + other2, q), :] + r1[pl.ds(other2, q), :]
    up_1 = copy(a1.at[pl.ds(other2, q)], r2, 2, peer_1)
    up_1.start()
    second_c.wait()
    a1[pl.ds(mine2, q), :] = x_ref[pl.ds(mine1 + mine2, q), :] + r1[pl.ds(mine2, q), :]
    up_1.wait()
    a2[...] = a1[pl.ds(mine2, q), :] + r2[...]

    mine3 = pl.multiple_of(b2 * e, 8)
    other3 = pl.multiple_of((1 - b2) * e, 8)
    cp = copy(a2.at[pl.ds(other3, e)], r3, 3, peer_2)
    cp.start()
    cp.wait()
    base_q = pl.multiple_of(mine1 + mine2, 8)
    at_e = pl.multiple_of(base_q + mine3, 8)
    out_ref[pl.ds(at_e, e), :] = a2[pl.ds(mine3, e), :] + r3[...]

    cp = copy(out_ref.at[pl.ds(at_e, e)], out_ref.at[pl.ds(at_e, e)], 4, peer_2)
    cp.start()
    cp.wait()
    down_c1 = copy(out_ref.at[pl.ds(base_q, q)], out_ref.at[pl.ds(base_q, q)], 5, peer_c)
    down_c1.start()
    down_1 = copy(out_ref.at[pl.ds(base_q, q)], out_ref.at[pl.ds(base_q, q)], 6, peer_1)
    down_1.start()
    down_1.wait()
    other_q = pl.multiple_of(mine1 + other2, 8)
    down_c2 = copy(out_ref.at[pl.ds(other_q, q)], out_ref.at[pl.ds(other_q, q)], 7, peer_c)
    down_c2.start()
    down_c1.wait()
    down_c2.wait()


def win_sum(x):
    rows, cols = x.shape
    return pl.pallas_call(
        win_sum_kernel,
        out_shape=jax.ShapeDtypeStruct((rows, cols), jnp.float32),
        in_specs=[pl.BlockSpec(memory_space=pltpu.VMEM)],
        out_specs=pl.BlockSpec(memory_space=pltpu.VMEM),
        scratch_shapes=[
            pltpu.VMEM((rows // 2, cols), jnp.float32),
            pltpu.VMEM((rows // 4, cols), jnp.float32),
            pltpu.VMEM((rows // 2, cols), jnp.float32),
            pltpu.VMEM((rows // 4, cols), jnp.float32),
            pltpu.VMEM((rows // 8, cols), jnp.float32),
            pltpu.SemaphoreType.DMA((8,)),
            pltpu.SemaphoreType.DMA((8,)),
        ],
        compiler_params=pltpu.CompilerParams(collective_id=0, has_side_effects=True),
    )(x)


def bcast_kernel(m_ref, out_ref, rx, s1, ry, piece, zr, sx, rxs, sy, rys, agy_s, agy_r, agx_s, agx_r, zsem):
    nx, ny = m_ref.shape[0], m_ref.shape[1]
    y, x, zh, zl, c = (lax.axis_index(a) for a in STA + WIN)
    xpeer = lambda p: (y, p, zh, zl, c)
    ypeer = lambda p: (p, x, zh, zl, c)
    zpeer = (y, x, 1 - zh, zl, c)

    barrier = pltpu.get_barrier_semaphore()
    for d in range(1, nx):
        pl.semaphore_signal(barrier, inc=1, device_id=xpeer((x + d) % nx), device_id_type=MESH_ID)
    for d in range(1, ny):
        pl.semaphore_signal(barrier, inc=1, device_id=ypeer((y + d) % ny), device_id_type=MESH_ID)
    pl.semaphore_signal(barrier, inc=1, device_id=zpeer, device_id_type=MESH_ID)
    pl.semaphore_wait(barrier, nx + ny - 1)

    def send_all(n, me, peer, src, dst, ssem, rsem):
        copies = []
        for d in range(1, n):
            to = (me + d) % n
            cp = pltpu.make_async_remote_copy(
                src_ref=src(to), dst_ref=dst, send_sem=ssem.at[d], recv_sem=rsem.at[d],
                device_id=peer(to), device_id_type=MESH_ID)
            cp.start()
            copies.append(cp)
        for cp in copies:
            cp.wait()

    send_all(nx, x, xpeer, lambda to: m_ref.at[to], rx.at[x], sx, rxs)
    total = m_ref[x]
    for d in range(1, nx):
        total = total + rx[(x + nx - d) % nx]
    s1[...] = total

    send_all(ny, y, ypeer, lambda to: s1.at[to], ry.at[y], sy, rys)
    part = s1[y]
    for d in range(1, ny):
        part = part + ry[(y + ny - d) % ny]
    piece[...] = part

    cp = pltpu.make_async_remote_copy(
        src_ref=piece, dst_ref=zr, send_sem=zsem.at[0], recv_sem=zsem.at[1],
        device_id=zpeer, device_id_type=MESH_ID)
    cp.start()
    cp.wait()
    out_ref[x, y] = piece[...] + zr[...]

    send_all(ny, y, ypeer, lambda to: out_ref.at[x, y], out_ref.at[x, y], agy_s, agy_r)
    send_all(nx, x, xpeer, lambda to: out_ref.at[x], out_ref.at[x], agx_s, agx_r)


def bcast(masked):
    shape = masked.shape
    nx, ny = shape[0], shape[1]
    return pl.pallas_call(
        bcast_kernel,
        out_shape=jax.ShapeDtypeStruct(shape, jnp.float32),
        in_specs=[pl.BlockSpec(memory_space=pltpu.VMEM)],
        out_specs=pl.BlockSpec(memory_space=pltpu.VMEM),
        scratch_shapes=[
            pltpu.VMEM(shape, jnp.float32),
            pltpu.VMEM(shape[1:], jnp.float32),
            pltpu.VMEM(shape[1:], jnp.float32),
            pltpu.VMEM(shape[2:], jnp.float32),
            pltpu.VMEM(shape[2:], jnp.float32),
            pltpu.SemaphoreType.DMA((nx,)),
            pltpu.SemaphoreType.DMA((nx,)),
            pltpu.SemaphoreType.DMA((ny,)),
            pltpu.SemaphoreType.DMA((ny,)),
            pltpu.SemaphoreType.DMA((ny,)),
            pltpu.SemaphoreType.DMA((ny,)),
            pltpu.SemaphoreType.DMA((nx,)),
            pltpu.SemaphoreType.DMA((nx,)),
            pltpu.SemaphoreType.DMA((2,)),
        ],
        compiler_params=pltpu.CompilerParams(collective_id=1, has_side_effects=True),
    )(masked)


def on_device(spectra, flags, owners, source_slots):
    win_count = spectra.shape[0]
    bins = spectra.shape[4]
    weighted = whiten(spectra) * flags.astype(jnp.float32)[:, :, None, None, None]
    n_win = lax.axis_size(WIN)
    factors = lag_factors(bins, NLAG)
    me = lax.axis_index(STA)
    slots = source_slots[:, None, :, None, None, None]
    picked_all = jnp.zeros((STEPS,) + weighted.shape, weighted.dtype)
    for k in range(weighted.shape[1]):
        picked_all = jnp.where(slots == k, weighted[None, :, k : k + 1], picked_all)
    picked_all = jnp.where((me == owners)[:, None, None, None, None, None], picked_all, 0.0)
    split = (lax.axis_size("x"), lax.axis_size("y"), -1, 128)
    picked_all = bcast(picked_all.reshape(split)).reshape(picked_all.shape)
    shape = weighted.shape
    rec = weighted.transpose(0, 2, 1, 3, 4).reshape(shape[0], 2, shape[1] * shape[3], shape[4])
    stacked = correlate_all(picked_all, rec, factors, win_count * n_win).reshape(
        STEPS, shape[1], shape[3], shape[1], shape[3], NLAG
    )
    return win_sum(stacked.reshape(-1, NLAG)).reshape(stacked.shape)


def solution(mesh):
    fine = fine_mesh(mesh)
    return jax.shard_map(
        on_device,
        mesh=fine,
        in_specs=(P(WIN, STA, None, None, None), P(WIN, STA), P(), P()),
        out_specs=P(None, None, None, STA, None, None),
        check_vma=False,
    )
```

```python
import functools
import math

import jax
import jax.numpy as jnp
from jax import lax
from jax.experimental import pallas as pl
from jax.experimental.pallas import tpu as pltpu
from jax.sharding import Mesh
from jax.sharding import PartitionSpec as P

NLAG = 768
STEPS = 4
MESH_ID = pl.DeviceIdType.MESH
STA = ("y", "x", "zh")
WIN = ("zl", "c")


def fine_mesh(mesh):
    devs = mesh.devices
    n_sta, n_win = devs.shape
    col = devs[:, 0]
    ny = len({d.coords[1] for d in col})
    nx = len({d.coords[0] for d in col})
    nzh = n_sta // (ny * nx)
    nc = len({d.core_on_chip for d in devs[0, :]})
    nzl = n_win // nc
    return Mesh(devs.reshape(ny, nx, nzh, nzl, nc), STA + WIN)


def whiten(spectra):
    shape = spectra.shape
    blocks = spectra.reshape(shape[0], shape[1], 2, 3, shape[4] // 64, 64)
    power = jnp.mean(blocks * blocks, axis=(2, 3, 5), keepdims=True)
    return (blocks / jnp.sqrt(power + 1e-06)).reshape(shape)


def lag_factors(bins, lags):
    shift = jnp.arange(lags, dtype=jnp.int32) - lags // 2
    hi = jnp.arange(bins // 64, dtype=jnp.int32) * 64 + 360
    lo = jnp.arange(64, dtype=jnp.int32)
    unit = 2.0 * math.pi / 7200.0
    a = jnp.mod(hi[:, None] * shift[None, :], 7200).astype(jnp.float32) * unit
    b = jnp.mod(lo[:, None] * shift[None, :], 7200).astype(jnp.float32) * unit
    return jnp.cos(a), jnp.sin(a), jnp.cos(b), jnp.sin(b)


def corr_kernel(scale, src_ref, rec_ref, ca_ref, sa_ref, cb_ref, sb_ref, out_ref, rows_ref, tab_ref):
    n_win = src_ref.shape[1]
    n_src = src_ref.shape[2]
    n_cmp = src_ref.shape[4]
    n_rows = rec_ref.shape[2]

    @pl.when(pl.program_id(0) == 0)
    def _():
        cb = cb_ref[...]
        sb = sb_ref[...]
        step = cb_ref.shape[0]
        for f1 in range(ca_ref.shape[0]):
            ca = ca_ref[pl.ds(f1, 1), :]
            sa = sa_ref[pl.ds(f1, 1), :]
            rows = pl.ds(f1 * step, step)
            tab_ref[0, rows, :] = ((ca * cb - sa * sb) * scale).astype(jnp.bfloat16)
            tab_ref[1, rows, :] = (-((sa * cb + ca * sb) * scale)).astype(jnp.bfloat16)

    for s in range(n_src):
        for i in range(n_cmp):
            acc_re = None
            acc_im = None
            for w in range(n_win):
                sre = src_ref[0, w, s, 0, pl.ds(i, 1), :]
                sim = src_ref[0, w, s, 1, pl.ds(i, 1), :]
                rre = rec_ref[w, 0]
                rim = rec_ref[w, 1]
                re = sre * rre + sim * rim
                im = sim * rre - sre * rim
                acc_re = re if acc_re is None else acc_re + re
                acc_im = im if acc_im is None else acc_im + im
            row = (s * n_cmp + i) * n_rows
            rows_ref[0, pl.ds(row, n_rows), :] = acc_re.astype(jnp.bfloat16)
            rows_ref[1, pl.ds(row, n_rows), :] = acc_im.astype(jnp.bfloat16)
    out_ref[0] = jnp.dot(rows_ref[0], tab_ref[0], preferred_element_type=jnp.float32) + jnp.dot(
        rows_ref[1], tab_ref[1], preferred_element_type=jnp.float32
    )


def correlate_all(picked_all, rec, factors, windows):
    steps, n_win, n_src, _, n_cmp, bins = picked_all.shape
    n_rows = rec.shape[2]
    lags = NLAG
    m = n_src * n_cmp * n_rows
    scale = 1.0 / math.sqrt(windows * bins)
    whole = lambda t: (0, 0)
    return pl.pallas_call(
        functools.partial(corr_kernel, scale),
        grid=(steps,),
        in_specs=[
            pl.BlockSpec((1, n_win, n_src, 2, n_cmp, bins), lambda t: (t, 0, 0, 0, 0, 0)),
            pl.BlockSpec(rec.shape, lambda t: (0, 0, 0, 0)),
        ]
        + [pl.BlockSpec(f.shape, whole) for f in factors],
        out_specs=pl.BlockSpec((1, m, lags), lambda t: (t, 0, 0)),
        out_shape=jax.ShapeDtypeStruct((steps, m, lags), jnp.float32),
        scratch_shapes=[
            pltpu.VMEM((2, m, bins), jnp.bfloat16),
            pltpu.VMEM((2, bins, lags), jnp.bfloat16),
        ],
    )(picked_all, rec, *factors)


def win_sum_kernel(x_ref, out_ref, a1, a2, r1, r2, r3, send_sem, recv_sem):
    rows = x_ref.shape[0]
    h, q, e = rows // 2, rows // 4, rows // 8
    coords = [lax.axis_index(a) for a in STA + WIN]
    zl, c = coords[3], coords[4]
    b1 = zl % 2
    b2 = zl // 2
    peer_c = tuple(coords[:4]) + (1 - c,)
    peer_1 = tuple(coords[:3]) + (zl + 1 - 2 * b1, c)
    peer_2 = tuple(coords[:3]) + (zl + 2 - 4 * b2, c)

    barrier = pltpu.get_barrier_semaphore()
    for peer in (peer_c, peer_1, peer_2):
        pl.semaphore_signal(barrier, inc=1, device_id=peer, device_id_type=MESH_ID)
    pl.semaphore_wait(barrier, 3)

    def copy(src, dst, k, peer):
        return pltpu.make_async_remote_copy(
            src_ref=src, dst_ref=dst, send_sem=send_sem.at[k], recv_sem=recv_sem.at[k],
            device_id=peer, device_id_type=MESH_ID)

    mine1 = pl.multiple_of(c * h, 8)
    other1 = pl.multiple_of((1 - c) * h, 8)
    mine2 = pl.multiple_of(b1 * q, 8)
    other2 = pl.multiple_of((1 - b1) * q, 8)
    first_c = copy(x_ref.at[pl.ds(other1 + other2, q)], r1.at[pl.ds(other2, q)], 0, peer_c)
    first_c.start()
    second_c = copy(x_ref.at[pl.ds(other1 + mine2, q)], r1.at[pl.ds(mine2, q)], 1, peer_c)
    second_c.start()
    first_c.wait()
    a1[pl.ds(other2, q), :] = x_ref[pl.ds(mine1 + other2, q), :] + r1[pl.ds(other2, q), :]
    up_1 = copy(a1.at[pl.ds(other2, q)], r2, 2, peer_1)
    up_1.start()
    second_c.wait()
    a1[pl.ds(mine2, q), :] = x_ref[pl.ds(mine1 + mine2, q), :] + r1[pl.ds(mine2, q), :]
    up_1.wait()
    a2[...] = a1[pl.ds(mine2, q), :] + r2[...]

    mine3 = pl.multiple_of(b2 * e, 8)
    other3 = pl.multiple_of((1 - b2) * e, 8)
    cp = copy(a2.at[pl.ds(other3, e)], r3, 3, peer_2)
    cp.start()
    cp.wait()
    base_q = pl.multiple_of(mine1 + mine2, 8)
    at_e = pl.multiple_of(base_q + mine3, 8)
    out_ref[pl.ds(at_e, e), :] = a2[pl.ds(mine3, e), :] + r3[...]

    cp = copy(out_ref.at[pl.ds(at_e, e)], out_ref.at[pl.ds(at_e, e)], 4, peer_2)
    cp.start()
    cp.wait()
    down_c1 = copy(out_ref.at[pl.ds(base_q, q)], out_ref.at[pl.ds(base_q, q)], 5, peer_c)
    down_c1.start()
    down_1 = copy(out_ref.at[pl.ds(base_q, q)], out_ref.at[pl.ds(base_q, q)], 6, peer_1)
    down_1.start()
    down_1.wait()
    other_q = pl.multiple_of(mine1 + other2, 8)
    down_c2 = copy(out_ref.at[pl.ds(other_q, q)], out_ref.at[pl.ds(other_q, q)], 7, peer_c)
    down_c2.start()
    down_c1.wait()
    down_c2.wait()


def win_sum(x):
    rows, cols = x.shape
    return pl.pallas_call(
        win_sum_kernel,
        out_shape=jax.ShapeDtypeStruct((rows, cols), jnp.float32),
        in_specs=[pl.BlockSpec(memory_space=pltpu.VMEM)],
        out_specs=pl.BlockSpec(memory_space=pltpu.VMEM),
        scratch_shapes=[
            pltpu.VMEM((rows // 2, cols), jnp.float32),
            pltpu.VMEM((rows // 4, cols), jnp.float32),
            pltpu.VMEM((rows // 2, cols), jnp.float32),
            pltpu.VMEM((rows // 4, cols), jnp.float32),
            pltpu.VMEM((rows // 8, cols), jnp.float32),
            pltpu.SemaphoreType.DMA((8,)),
            pltpu.SemaphoreType.DMA((8,)),
        ],
        compiler_params=pltpu.CompilerParams(collective_id=0, has_side_effects=True),
    )(x)


def bcast_kernel(m_ref, out_ref, rx, s1, ry, piece, zr, sx, rxs, sy, rys, agy_s, agy_r, agx_s, agx_r, zsem):
    nx, ny = m_ref.shape[0], m_ref.shape[1]
    y, x, zh, zl, c = (lax.axis_index(a) for a in STA + WIN)
    xpeer = lambda p: (y, p, zh, zl, c)
    ypeer = lambda p: (p, x, zh, zl, c)
    zpeer = (y, x, 1 - zh, zl, c)

    barrier = pltpu.get_barrier_semaphore()
    for d in range(1, nx):
        pl.semaphore_signal(barrier, inc=1, device_id=xpeer((x + d) % nx), device_id_type=MESH_ID)
    for d in range(1, ny):
        pl.semaphore_signal(barrier, inc=1, device_id=ypeer((y + d) % ny), device_id_type=MESH_ID)
    pl.semaphore_signal(barrier, inc=1, device_id=zpeer, device_id_type=MESH_ID)
    pl.semaphore_wait(barrier, nx + ny - 1)

    def remote(src, dst, ssem, rsem, k, peer):
        cp = pltpu.make_async_remote_copy(
            src_ref=src, dst_ref=dst, send_sem=ssem.at[k], recv_sem=rsem.at[k],
            device_id=peer, device_id_type=MESH_ID)
        cp.start()
        return cp

    order = list(range(1, ny)) + [0]
    rs_x = {}
    for d in order:
        row = (y + d) % ny
        rs_x[d] = [
            remote(m_ref.at[(x + dx) % nx, row], rx.at[x, row], sx, rxs, d * nx + dx, xpeer((x + dx) % nx))
            for dx in range(1, nx)
        ]
    rs_y = []
    for d in order:
        row = (y + d) % ny
        for cp in rs_x[d]:
            cp.wait()
        total = m_ref[x, row]
        for dx in range(1, nx):
            total = total + rx[(x + nx - dx) % nx, row]
        if d == 0:
            part = total
        else:
            s1[row] = total
            rs_y.append(remote(s1.at[row], ry.at[y], sy, rys, d, ypeer(row)))
    for cp in rs_y:
        cp.wait()
    for d in range(1, ny):
        part = part + ry[(y + ny - d) % ny]
    piece[...] = part

    cp = pltpu.make_async_remote_copy(
        src_ref=piece, dst_ref=zr, send_sem=zsem.at[0], recv_sem=zsem.at[1],
        device_id=zpeer, device_id_type=MESH_ID)
    cp.start()
    cp.wait()
    out_ref[x, y] = piece[...] + zr[...]

    ag_y = {d: remote(out_ref.at[x, y], out_ref.at[x, y], agy_s, agy_r, d, ypeer((y + d) % ny)) for d in range(1, ny)}
    ag_x = []
    for d in [0] + list(range(1, ny)):
        if d:
            ag_y[d].wait()
        row = (y + ny - d) % ny
        for dx in range(1, nx):
            ag_x.append(remote(out_ref.at[x, row], out_ref.at[x, row], agx_s, agx_r, d * nx + dx, xpeer((x + dx) % nx)))
    for cp in ag_x:
        cp.wait()


def bcast(masked):
    shape = masked.shape
    nx, ny = shape[0], shape[1]
    return pl.pallas_call(
        bcast_kernel,
        out_shape=jax.ShapeDtypeStruct(shape, jnp.float32),
        in_specs=[pl.BlockSpec(memory_space=pltpu.VMEM)],
        out_specs=pl.BlockSpec(memory_space=pltpu.VMEM),
        scratch_shapes=[
            pltpu.VMEM(shape, jnp.float32),
            pltpu.VMEM(shape[1:], jnp.float32),
            pltpu.VMEM(shape[1:], jnp.float32),
            pltpu.VMEM(shape[2:], jnp.float32),
            pltpu.VMEM(shape[2:], jnp.float32),
            pltpu.SemaphoreType.DMA((nx * ny,)),
            pltpu.SemaphoreType.DMA((nx * ny,)),
            pltpu.SemaphoreType.DMA((ny,)),
            pltpu.SemaphoreType.DMA((ny,)),
            pltpu.SemaphoreType.DMA((ny,)),
            pltpu.SemaphoreType.DMA((ny,)),
            pltpu.SemaphoreType.DMA((nx * ny,)),
            pltpu.SemaphoreType.DMA((nx * ny,)),
            pltpu.SemaphoreType.DMA((2,)),
        ],
        compiler_params=pltpu.CompilerParams(collective_id=1, has_side_effects=True),
    )(masked)


def on_device(spectra, flags, owners, source_slots):
    win_count = spectra.shape[0]
    bins = spectra.shape[4]
    weighted = whiten(spectra) * flags.astype(jnp.float32)[:, :, None, None, None]
    n_win = lax.axis_size(WIN)
    factors = lag_factors(bins, NLAG)
    me = lax.axis_index(STA)
    slots = source_slots[:, None, :, None, None, None]
    picked_all = jnp.zeros((STEPS,) + weighted.shape, weighted.dtype)
    for k in range(weighted.shape[1]):
        picked_all = jnp.where(slots == k, weighted[None, :, k : k + 1], picked_all)
    picked_all = jnp.where((me == owners)[:, None, None, None, None, None], picked_all, 0.0)
    split = (lax.axis_size("x"), lax.axis_size("y"), -1, 128)
    picked_all = bcast(picked_all.reshape(split)).reshape(picked_all.shape)
    shape = weighted.shape
    rec = weighted.transpose(0, 2, 1, 3, 4).reshape(shape[0], 2, shape[1] * shape[3], shape[4])
    stacked = correlate_all(picked_all, rec, factors, win_count * n_win).reshape(
        STEPS, shape[1], shape[3], shape[1], shape[3], NLAG
    )
    return win_sum(stacked.reshape(-1, NLAG)).reshape(stacked.shape)


def solution(mesh):
    fine = fine_mesh(mesh)
    return jax.shard_map(
        on_device,
        mesh=fine,
        in_specs=(P(WIN, STA, None, None, None), P(WIN, STA), P(), P()),
        out_specs=P(None, None, None, STA, None, None),
        check_vma=False,
    )
```

```python
import functools
import math

import jax
import jax.numpy as jnp
from jax import lax
from jax.experimental import pallas as pl
from jax.experimental.pallas import tpu as pltpu
from jax.sharding import Mesh
from jax.sharding import PartitionSpec as P

NLAG = 768
STEPS = 4
MESH_ID = pl.DeviceIdType.MESH
STA = ("y", "x", "zh")
WIN = ("zl", "c")


def fine_mesh(mesh):
    devs = mesh.devices
    n_sta, n_win = devs.shape
    col = devs[:, 0]
    ny = len({d.coords[1] for d in col})
    nx = len({d.coords[0] for d in col})
    nzh = n_sta // (ny * nx)
    nc = len({d.core_on_chip for d in devs[0, :]})
    nzl = n_win // nc
    return Mesh(devs.reshape(ny, nx, nzh, nzl, nc), STA + WIN)


def whiten(spectra):
    shape = spectra.shape
    blocks = spectra.reshape(shape[0], shape[1], 2, 3, shape[4] // 64, 64)
    power = jnp.mean(blocks * blocks, axis=(2, 3, 5), keepdims=True)
    return (blocks / jnp.sqrt(power + 1e-06)).reshape(shape)


def lag_factors(bins, lags):
    shift = jnp.arange(lags, dtype=jnp.int32) - lags // 2
    hi = jnp.arange(bins // 64, dtype=jnp.int32) * 64 + 360
    lo = jnp.arange(64, dtype=jnp.int32)
    unit = 2.0 * math.pi / 7200.0
    a = jnp.mod(hi[:, None] * shift[None, :], 7200).astype(jnp.float32) * unit
    b = jnp.mod(lo[:, None] * shift[None, :], 7200).astype(jnp.float32) * unit
    return jnp.cos(a), jnp.sin(a), jnp.cos(b), jnp.sin(b)


def corr_kernel(scale, src_ref, rec_ref, ca_ref, sa_ref, cb_ref, sb_ref, out_ref, rows_ref, tab_ref):
    n_win = src_ref.shape[1]
    n_src = src_ref.shape[2]
    n_cmp = src_ref.shape[4]
    n_rows = rec_ref.shape[2]

    @pl.when(pl.program_id(0) == 0)
    def _():
        cb = cb_ref[...]
        sb = sb_ref[...]
        step = cb_ref.shape[0]
        for f1 in range(ca_ref.shape[0]):
            ca = ca_ref[pl.ds(f1, 1), :]
            sa = sa_ref[pl.ds(f1, 1), :]
            rows = pl.ds(f1 * step, step)
            tab_ref[0, rows, :] = ((ca * cb - sa * sb) * scale).astype(jnp.bfloat16)
            tab_ref[1, rows, :] = (-((sa * cb + ca * sb) * scale)).astype(jnp.bfloat16)

    for s in range(n_src):
        for i in range(n_cmp):
            acc_re = None
            acc_im = None
            for w in range(n_win):
                sre = src_ref[0, w, s, 0, pl.ds(i, 1), :]
                sim = src_ref[0, w, s, 1, pl.ds(i, 1), :]
                rre = rec_ref[w, 0]
                rim = rec_ref[w, 1]
                re = sre * rre + sim * rim
                im = sim * rre - sre * rim
                acc_re = re if acc_re is None else acc_re + re
                acc_im = im if acc_im is None else acc_im + im
            row = (s * n_cmp + i) * n_rows
            rows_ref[0, pl.ds(row, n_rows), :] = acc_re.astype(jnp.bfloat16)
            rows_ref[1, pl.ds(row, n_rows), :] = acc_im.astype(jnp.bfloat16)
    out_ref[0] = jnp.dot(rows_ref[0], tab_ref[0], preferred_element_type=jnp.float32) + jnp.dot(
        rows_ref[1], tab_ref[1], preferred_element_type=jnp.float32
    )


def correlate_all(picked_all, rec, factors, windows):
    steps, n_win, n_src, _, n_cmp, bins = picked_all.shape
    n_rows = rec.shape[2]
    lags = NLAG
    m = n_src * n_cmp * n_rows
    scale = 1.0 / math.sqrt(windows * bins)
    whole = lambda t: (0, 0)
    return pl.pallas_call(
        functools.partial(corr_kernel, scale),
        grid=(steps,),
        in_specs=[
            pl.BlockSpec((1, n_win, n_src, 2, n_cmp, bins), lambda t: (t, 0, 0, 0, 0, 0)),
            pl.BlockSpec(rec.shape, lambda t: (0, 0, 0, 0)),
        ]
        + [pl.BlockSpec(f.shape, whole) for f in factors],
        out_specs=pl.BlockSpec((1, m, lags), lambda t: (t, 0, 0)),
        out_shape=jax.ShapeDtypeStruct((steps, m, lags), jnp.float32),
        scratch_shapes=[
            pltpu.VMEM((2, m, bins), jnp.bfloat16),
            pltpu.VMEM((2, bins, lags), jnp.bfloat16),
        ],
    )(picked_all, rec, *factors)


def win_sum_kernel(x_ref, out_ref, a1, a2, r1, r2, r3, send_sem, recv_sem):
    rows = x_ref.shape[0]
    h, q, e = rows // 2, rows // 4, rows // 8
    coords = [lax.axis_index(a) for a in STA + WIN]
    zl, c = coords[3], coords[4]
    b1 = zl % 2
    b2 = zl // 2
    peer_c = tuple(coords[:4]) + (1 - c,)
    peer_1 = tuple(coords[:3]) + (zl + 1 - 2 * b1, c)
    peer_2 = tuple(coords[:3]) + (zl + 2 - 4 * b2, c)

    barrier = pltpu.get_barrier_semaphore()
    for peer in (peer_c, peer_1, peer_2):
        pl.semaphore_signal(barrier, inc=1, device_id=peer, device_id_type=MESH_ID)
    pl.semaphore_wait(barrier, 3)

    def copy(src, dst, k, peer):
        return pltpu.make_async_remote_copy(
            src_ref=src, dst_ref=dst, send_sem=send_sem.at[k], recv_sem=recv_sem.at[k],
            device_id=peer, device_id_type=MESH_ID)

    mine1 = pl.multiple_of(c * h, 8)
    other1 = pl.multiple_of((1 - c) * h, 8)
    mine2 = pl.multiple_of(b1 * q, 8)
    other2 = pl.multiple_of((1 - b1) * q, 8)
    mine3 = pl.multiple_of(b2 * e, 8)
    other3 = pl.multiple_of((1 - b2) * e, 8)
    base_q = pl.multiple_of(mine1 + mine2, 8)
    at_e = pl.multiple_of(base_q + mine3, 8)
    n_chunks = send_sem.shape[0] // 6
    width = x_ref.shape[1] // n_chunks

    def stages(j):
        cols = pl.ds(j * width, width)
        k = 6 * j

        def run(src, dst, i, peer):
            cp = copy(src, dst, k + i, peer)
            cp.start()
            return cp

        cp = run(x_ref.at[pl.ds(other1, h), cols], r1.at[:, cols], 0, peer_c)
        yield
        cp.wait()
        a1[:, cols] = x_ref[pl.ds(mine1, h), cols] + r1[:, cols]
        cp = run(a1.at[pl.ds(other2, q), cols], r2.at[:, cols], 1, peer_1)
        yield
        cp.wait()
        a2[:, cols] = a1[pl.ds(mine2, q), cols] + r2[:, cols]
        cp = run(a2.at[pl.ds(other3, e), cols], r3.at[:, cols], 2, peer_2)
        yield
        cp.wait()
        out_ref[pl.ds(at_e, e), cols] = a2[pl.ds(mine3, e), cols] + r3[:, cols]
        cp = run(out_ref.at[pl.ds(at_e, e), cols], out_ref.at[pl.ds(at_e, e), cols], 3, peer_2)
        yield
        cp.wait()
        cp = run(out_ref.at[pl.ds(base_q, q), cols], out_ref.at[pl.ds(base_q, q), cols], 4, peer_1)
        yield
        cp.wait()
        cp = run(out_ref.at[pl.ds(mine1, h), cols], out_ref.at[pl.ds(mine1, h), cols], 5, peer_c)
        yield
        cp.wait()

    live = [stages(j) for j in range(n_chunks)]
    next(live[0])
    started = 1
    while live:
        if started < len(live):
            next(live[started])
            started += 1
        for g in list(live[:started]):
            try:
                next(g)
            except StopIteration:
                live.remove(g)
                started -= 1


def win_sum(x):
    rows, cols = x.shape
    return pl.pallas_call(
        win_sum_kernel,
        out_shape=jax.ShapeDtypeStruct((rows, cols), jnp.float32),
        in_specs=[pl.BlockSpec(memory_space=pltpu.VMEM)],
        out_specs=pl.BlockSpec(memory_space=pltpu.VMEM),
        scratch_shapes=[
            pltpu.VMEM((rows // 2, cols), jnp.float32),
            pltpu.VMEM((rows // 4, cols), jnp.float32),
            pltpu.VMEM((rows // 2, cols), jnp.float32),
            pltpu.VMEM((rows // 4, cols), jnp.float32),
            pltpu.VMEM((rows // 8, cols), jnp.float32),
            pltpu.SemaphoreType.DMA((12,)),
            pltpu.SemaphoreType.DMA((12,)),
        ],
        compiler_params=pltpu.CompilerParams(collective_id=0, has_side_effects=True),
    )(x)


def bcast_kernel(m_ref, out_ref, rx, s1, ry, piece, zr, sx, rxs, sy, rys, agy_s, agy_r, agx_s, agx_r, zsem):
    nx, ny = m_ref.shape[0], m_ref.shape[1]
    y, x, zh, zl, c = (lax.axis_index(a) for a in STA + WIN)
    xpeer = lambda p: (y, p, zh, zl, c)
    ypeer = lambda p: (p, x, zh, zl, c)
    zpeer = (y, x, 1 - zh, zl, c)

    barrier = pltpu.get_barrier_semaphore()
    for d in range(1, nx):
        pl.semaphore_signal(barrier, inc=1, device_id=xpeer((x + d) % nx), device_id_type=MESH_ID)
    for d in range(1, ny):
        pl.semaphore_signal(barrier, inc=1, device_id=ypeer((y + d) % ny), device_id_type=MESH_ID)
    pl.semaphore_signal(barrier, inc=1, device_id=zpeer, device_id_type=MESH_ID)
    pl.semaphore_wait(barrier, nx + ny - 1)

    def remote(src, dst, ssem, rsem, k, peer):
        cp = pltpu.make_async_remote_copy(
            src_ref=src, dst_ref=dst, send_sem=ssem.at[k], recv_sem=rsem.at[k],
            device_id=peer, device_id_type=MESH_ID)
        cp.start()
        return cp

    order = list(range(1, ny)) + [0]
    rs_x = {}
    for d in order:
        row = (y + d) % ny
        rs_x[d] = [
            remote(m_ref.at[(x + dx) % nx, row], rx.at[x, row], sx, rxs, d * nx + dx, xpeer((x + dx) % nx))
            for dx in range(1, nx)
        ]
    rs_y = []
    for d in order:
        row = (y + d) % ny
        for cp in rs_x[d]:
            cp.wait()
        total = m_ref[x, row]
        for dx in range(1, nx):
            total = total + rx[(x + nx - dx) % nx, row]
        if d == 0:
            part = total
        else:
            s1[row] = total
            rs_y.append(remote(s1.at[row], ry.at[y], sy, rys, d, ypeer(row)))
    for cp in rs_y:
        cp.wait()
    for d in range(1, ny):
        part = part + ry[(y + ny - d) % ny]
    piece[...] = part

    cp = pltpu.make_async_remote_copy(
        src_ref=piece, dst_ref=zr, send_sem=zsem.at[0], recv_sem=zsem.at[1],
        device_id=zpeer, device_id_type=MESH_ID)
    cp.start()
    cp.wait()
    out_ref[x, y] = piece[...] + zr[...]

    ag_y = {d: remote(out_ref.at[x, y], out_ref.at[x, y], agy_s, agy_r, d, ypeer((y + d) % ny)) for d in range(1, ny)}
    ag_x = []
    for d in [0] + list(range(1, ny)):
        if d:
            ag_y[d].wait()
        row = (y + ny - d) % ny
        for dx in range(1, nx):
            ag_x.append(remote(out_ref.at[x, row], out_ref.at[x, row], agx_s, agx_r, d * nx + dx, xpeer((x + dx) % nx)))
    for cp in ag_x:
        cp.wait()


def bcast(masked):
    shape = masked.shape
    nx, ny = shape[0], shape[1]
    return pl.pallas_call(
        bcast_kernel,
        out_shape=jax.ShapeDtypeStruct(shape, jnp.float32),
        in_specs=[pl.BlockSpec(memory_space=pltpu.VMEM)],
        out_specs=pl.BlockSpec(memory_space=pltpu.VMEM),
        scratch_shapes=[
            pltpu.VMEM(shape, jnp.float32),
            pltpu.VMEM(shape[1:], jnp.float32),
            pltpu.VMEM(shape[1:], jnp.float32),
            pltpu.VMEM(shape[2:], jnp.float32),
            pltpu.VMEM(shape[2:], jnp.float32),
            pltpu.SemaphoreType.DMA((nx * ny,)),
            pltpu.SemaphoreType.DMA((nx * ny,)),
            pltpu.SemaphoreType.DMA((ny,)),
            pltpu.SemaphoreType.DMA((ny,)),
            pltpu.SemaphoreType.DMA((ny,)),
            pltpu.SemaphoreType.DMA((ny,)),
            pltpu.SemaphoreType.DMA((nx * ny,)),
            pltpu.SemaphoreType.DMA((nx * ny,)),
            pltpu.SemaphoreType.DMA((2,)),
        ],
        compiler_params=pltpu.CompilerParams(collective_id=1, has_side_effects=True),
    )(masked)


def on_device(spectra, flags, owners, source_slots):
    win_count = spectra.shape[0]
    bins = spectra.shape[4]
    weighted = whiten(spectra) * flags.astype(jnp.float32)[:, :, None, None, None]
    n_win = lax.axis_size(WIN)
    factors = lag_factors(bins, NLAG)
    me = lax.axis_index(STA)
    slots = source_slots[:, None, :, None, None, None]
    picked_all = jnp.zeros((STEPS,) + weighted.shape, weighted.dtype)
    for k in range(weighted.shape[1]):
        picked_all = jnp.where(slots == k, weighted[None, :, k : k + 1], picked_all)
    picked_all = jnp.where((me == owners)[:, None, None, None, None, None], picked_all, 0.0)
    split = (lax.axis_size("x"), lax.axis_size("y"), -1, 128)
    picked_all = bcast(picked_all.reshape(split)).reshape(picked_all.shape)
    shape = weighted.shape
    rec = weighted.transpose(0, 2, 1, 3, 4).reshape(shape[0], 2, shape[1] * shape[3], shape[4])
    stacked = correlate_all(picked_all, rec, factors, win_count * n_win).reshape(
        STEPS, shape[1], shape[3], shape[1], shape[3], NLAG
    )
    return win_sum(stacked.reshape(-1, NLAG)).reshape(stacked.shape)


def solution(mesh):
    fine = fine_mesh(mesh)
    return jax.shard_map(
        on_device,
        mesh=fine,
        in_specs=(P(WIN, STA, None, None, None), P(WIN, STA), P(), P()),
        out_specs=P(None, None, None, STA, None, None),
        check_vma=False,
    )
```

```python
import functools
import math

import jax
import jax.numpy as jnp
from jax import lax
from jax.experimental import pallas as pl
from jax.experimental.pallas import tpu as pltpu
from jax.sharding import Mesh
from jax.sharding import PartitionSpec as P

NLAG = 768
STEPS = 4
MESH_ID = pl.DeviceIdType.MESH
STA = ("y", "x", "zh")
WIN = ("zl", "c")


def fine_mesh(mesh):
    devs = mesh.devices
    n_sta, n_win = devs.shape
    col = devs[:, 0]
    ny = len({d.coords[1] for d in col})
    nx = len({d.coords[0] for d in col})
    nzh = n_sta // (ny * nx)
    nc = len({d.core_on_chip for d in devs[0, :]})
    nzl = n_win // nc
    return Mesh(devs.reshape(ny, nx, nzh, nzl, nc), STA + WIN)


def whiten(spectra):
    shape = spectra.shape
    blocks = spectra.reshape(shape[0], shape[1], 2, 3, shape[4] // 64, 64)
    power = jnp.mean(blocks * blocks, axis=(2, 3, 5), keepdims=True)
    return (blocks / jnp.sqrt(power + 1e-06)).reshape(shape)


def lag_factors(bins, lags):
    shift = jnp.arange(lags, dtype=jnp.int32) - lags // 2
    hi = jnp.arange(bins // 64, dtype=jnp.int32) * 64 + 360
    lo = jnp.arange(64, dtype=jnp.int32)
    unit = 2.0 * math.pi / 7200.0
    a = jnp.mod(hi[:, None] * shift[None, :], 7200).astype(jnp.float32) * unit
    b = jnp.mod(lo[:, None] * shift[None, :], 7200).astype(jnp.float32) * unit
    return jnp.cos(a), jnp.sin(a), jnp.cos(b), jnp.sin(b)


def corr_kernel(scale, src_ref, rec_ref, ca_ref, sa_ref, cb_ref, sb_ref, out_ref, rows_ref, tab_ref):
    n_win = src_ref.shape[1]
    n_src = src_ref.shape[2]
    n_cmp = src_ref.shape[4]
    n_rows = rec_ref.shape[2]

    @pl.when(pl.program_id(0) == 0)
    def _():
        cb = cb_ref[...]
        sb = sb_ref[...]
        step = cb_ref.shape[0]
        for f1 in range(ca_ref.shape[0]):
            ca = ca_ref[pl.ds(f1, 1), :]
            sa = sa_ref[pl.ds(f1, 1), :]
            rows = pl.ds(f1 * step, step)
            tab_ref[0, rows, :] = ((ca * cb - sa * sb) * scale).astype(jnp.bfloat16)
            tab_ref[1, rows, :] = (-((sa * cb + ca * sb) * scale)).astype(jnp.bfloat16)

    for s in range(n_src):
        for i in range(n_cmp):
            acc_re = None
            acc_im = None
            for w in range(n_win):
                sre = src_ref[0, w, s, 0, pl.ds(i, 1), :]
                sim = src_ref[0, w, s, 1, pl.ds(i, 1), :]
                rre = rec_ref[w, 0]
                rim = rec_ref[w, 1]
                re = sre * rre + sim * rim
                im = sim * rre - sre * rim
                acc_re = re if acc_re is None else acc_re + re
                acc_im = im if acc_im is None else acc_im + im
            row = (s * n_cmp + i) * n_rows
            rows_ref[0, pl.ds(row, n_rows), :] = acc_re.astype(jnp.bfloat16)
            rows_ref[1, pl.ds(row, n_rows), :] = acc_im.astype(jnp.bfloat16)
    out_ref[0] = jnp.dot(rows_ref[0], tab_ref[0], preferred_element_type=jnp.float32) + jnp.dot(
        rows_ref[1], tab_ref[1], preferred_element_type=jnp.float32
    )


def correlate_all(picked_all, rec, factors, windows):
    steps, n_win, n_src, _, n_cmp, bins = picked_all.shape
    n_rows = rec.shape[2]
    lags = NLAG
    m = n_src * n_cmp * n_rows
    scale = 1.0 / math.sqrt(windows * bins)
    whole = lambda t: (0, 0)
    return pl.pallas_call(
        functools.partial(corr_kernel, scale),
        grid=(steps,),
        in_specs=[
            pl.BlockSpec((1, n_win, n_src, 2, n_cmp, bins), lambda t: (t, 0, 0, 0, 0, 0)),
            pl.BlockSpec(rec.shape, lambda t: (0, 0, 0, 0)),
        ]
        + [pl.BlockSpec(f.shape, whole) for f in factors],
        out_specs=pl.BlockSpec((1, m, lags), lambda t: (t, 0, 0)),
        out_shape=jax.ShapeDtypeStruct((steps, m, lags), jnp.float32),
        scratch_shapes=[
            pltpu.VMEM((2, m, bins), jnp.bfloat16),
            pltpu.VMEM((2, bins, lags), jnp.bfloat16),
        ],
    )(picked_all, rec, *factors)


def win_sum_kernel(x_ref, out_ref, a1, a2, r1, r2, r3, send_sem, recv_sem):
    rows = x_ref.shape[0]
    h, q, e = rows // 2, rows // 4, rows // 8
    coords = [lax.axis_index(a) for a in STA + WIN]
    zl, c = coords[3], coords[4]
    b1 = zl % 2
    b2 = zl // 2
    peer_c = tuple(coords[:4]) + (1 - c,)
    peer_1 = tuple(coords[:3]) + (zl + 1 - 2 * b1, c)
    peer_2 = tuple(coords[:3]) + (zl + 2 - 4 * b2, c)

    barrier = pltpu.get_barrier_semaphore()
    for peer in (peer_c, peer_1, peer_2):
        pl.semaphore_signal(barrier, inc=1, device_id=peer, device_id_type=MESH_ID)
    pl.semaphore_wait(barrier, 3)

    def copy(src, dst, k, peer):
        return pltpu.make_async_remote_copy(
            src_ref=src, dst_ref=dst, send_sem=send_sem.at[k], recv_sem=recv_sem.at[k],
            device_id=peer, device_id_type=MESH_ID)

    mine1 = pl.multiple_of(c * h, 8)
    other1 = pl.multiple_of((1 - c) * h, 8)
    mine2 = pl.multiple_of(b1 * q, 8)
    other2 = pl.multiple_of((1 - b1) * q, 8)
    mine3 = pl.multiple_of(b2 * e, 8)
    other3 = pl.multiple_of((1 - b2) * e, 8)
    base_q = pl.multiple_of(mine1 + mine2, 8)
    at_e = pl.multiple_of(base_q + mine3, 8)
    n_chunks = send_sem.shape[0] // 6
    width = x_ref.shape[1] // n_chunks

    def stages(j):
        cols = pl.ds(j * width, width)
        k = 6 * j

        def run(src, dst, i, peer):
            cp = copy(src, dst, k + i, peer)
            cp.start()
            return cp

        cp = run(x_ref.at[pl.ds(other1, h), cols], r1.at[:, cols], 0, peer_c)
        yield
        cp.wait()
        a1[:, cols] = x_ref[pl.ds(mine1, h), cols] + r1[:, cols]
        cp = run(a1.at[pl.ds(other2, q), cols], r2.at[:, cols], 1, peer_1)
        yield
        cp.wait()
        a2[:, cols] = a1[pl.ds(mine2, q), cols] + r2[:, cols]
        cp = run(a2.at[pl.ds(other3, e), cols], r3.at[:, cols], 2, peer_2)
        yield
        cp.wait()
        out_ref[pl.ds(at_e, e), cols] = a2[pl.ds(mine3, e), cols] + r3[:, cols]
        cp = run(out_ref.at[pl.ds(at_e, e), cols], out_ref.at[pl.ds(at_e, e), cols], 3, peer_2)
        yield
        cp.wait()
        cp = run(out_ref.at[pl.ds(base_q, q), cols], out_ref.at[pl.ds(base_q, q), cols], 4, peer_1)
        yield
        cp.wait()
        cp = run(out_ref.at[pl.ds(mine1, h), cols], out_ref.at[pl.ds(mine1, h), cols], 5, peer_c)
        yield
        cp.wait()

    live = [stages(j) for j in range(n_chunks)]
    next(live[0])
    started = 1
    while live:
        if started < len(live):
            next(live[started])
            started += 1
        for g in list(live[:started]):
            try:
                next(g)
            except StopIteration:
                live.remove(g)
                started -= 1


def win_sum(x):
    rows, cols = x.shape
    return pl.pallas_call(
        win_sum_kernel,
        out_shape=jax.ShapeDtypeStruct((rows, cols), jnp.float32),
        in_specs=[pl.BlockSpec(memory_space=pltpu.VMEM)],
        out_specs=pl.BlockSpec(memory_space=pltpu.VMEM),
        scratch_shapes=[
            pltpu.VMEM((rows // 2, cols), jnp.float32),
            pltpu.VMEM((rows // 4, cols), jnp.float32),
            pltpu.VMEM((rows // 2, cols), jnp.float32),
            pltpu.VMEM((rows // 4, cols), jnp.float32),
            pltpu.VMEM((rows // 8, cols), jnp.float32),
            pltpu.SemaphoreType.DMA((18,)),
            pltpu.SemaphoreType.DMA((18,)),
        ],
        compiler_params=pltpu.CompilerParams(collective_id=0, has_side_effects=True),
    )(x)


def bcast_kernel(m_ref, out_ref, rx, s1, ry, piece, zr, sx, rxs, sy, rys, agy_s, agy_r, agx_s, agx_r, zsem):
    nx, ny = m_ref.shape[0], m_ref.shape[1]
    y, x, zh, zl, c = (lax.axis_index(a) for a in STA + WIN)
    xpeer = lambda p: (y, p, zh, zl, c)
    ypeer = lambda p: (p, x, zh, zl, c)
    zpeer = (y, x, 1 - zh, zl, c)

    barrier = pltpu.get_barrier_semaphore()
    for d in range(1, nx):
        pl.semaphore_signal(barrier, inc=1, device_id=xpeer((x + d) % nx), device_id_type=MESH_ID)
    for d in range(1, ny):
        pl.semaphore_signal(barrier, inc=1, device_id=ypeer((y + d) % ny), device_id_type=MESH_ID)
    pl.semaphore_signal(barrier, inc=1, device_id=zpeer, device_id_type=MESH_ID)
    pl.semaphore_wait(barrier, nx + ny - 1)

    def remote(src, dst, ssem, rsem, k, peer):
        cp = pltpu.make_async_remote_copy(
            src_ref=src, dst_ref=dst, send_sem=ssem.at[k], recv_sem=rsem.at[k],
            device_id=peer, device_id_type=MESH_ID)
        cp.start()
        return cp

    order = list(range(1, ny)) + [0]
    rs_x = {}
    for d in order:
        row = (y + d) % ny
        rs_x[d] = [
            remote(m_ref.at[(x + dx) % nx, row], rx.at[x, row], sx, rxs, d * nx + dx, xpeer((x + dx) % nx))
            for dx in range(1, nx)
        ]
    rs_y = []
    for d in order:
        row = (y + d) % ny
        for cp in rs_x[d]:
            cp.wait()
        total = m_ref[x, row]
        for dx in range(1, nx):
            total = total + rx[(x + nx - dx) % nx, row]
        if d == 0:
            part = total
        else:
            s1[row] = total
            rs_y.append(remote(s1.at[row], ry.at[y], sy, rys, d, ypeer(row)))
    for cp in rs_y:
        cp.wait()
    for d in range(1, ny):
        part = part + ry[(y + ny - d) % ny]
    piece[...] = part

    cp = pltpu.make_async_remote_copy(
        src_ref=piece, dst_ref=zr, send_sem=zsem.at[0], recv_sem=zsem.at[1],
        device_id=zpeer, device_id_type=MESH_ID)
    cp.start()
    cp.wait()
    out_ref[x, y] = piece[...] + zr[...]

    ag_y = {d: remote(out_ref.at[x, y], out_ref.at[x, y], agy_s, agy_r, d, ypeer((y + d) % ny)) for d in range(1, ny)}
    ag_x = []
    for d in [0] + list(range(1, ny)):
        if d:
            ag_y[d].wait()
        row = (y + ny - d) % ny
        for dx in range(1, nx):
            ag_x.append(remote(out_ref.at[x, row], out_ref.at[x, row], agx_s, agx_r, d * nx + dx, xpeer((x + dx) % nx)))
    for cp in ag_x:
        cp.wait()


def bcast(masked):
    shape = masked.shape
    nx, ny = shape[0], shape[1]
    return pl.pallas_call(
        bcast_kernel,
        out_shape=jax.ShapeDtypeStruct(shape, jnp.float32),
        in_specs=[pl.BlockSpec(memory_space=pltpu.VMEM)],
        out_specs=pl.BlockSpec(memory_space=pltpu.VMEM),
        scratch_shapes=[
            pltpu.VMEM(shape, jnp.float32),
            pltpu.VMEM(shape[1:], jnp.float32),
            pltpu.VMEM(shape[1:], jnp.float32),
            pltpu.VMEM(shape[2:], jnp.float32),
            pltpu.VMEM(shape[2:], jnp.float32),
            pltpu.SemaphoreType.DMA((nx * ny,)),
            pltpu.SemaphoreType.DMA((nx * ny,)),
            pltpu.SemaphoreType.DMA((ny,)),
            pltpu.SemaphoreType.DMA((ny,)),
            pltpu.SemaphoreType.DMA((ny,)),
            pltpu.SemaphoreType.DMA((ny,)),
            pltpu.SemaphoreType.DMA((nx * ny,)),
            pltpu.SemaphoreType.DMA((nx * ny,)),
            pltpu.SemaphoreType.DMA((2,)),
        ],
        compiler_params=pltpu.CompilerParams(collective_id=1, has_side_effects=True),
    )(masked)


def on_device(spectra, flags, owners, source_slots):
    win_count = spectra.shape[0]
    bins = spectra.shape[4]
    weighted = whiten(spectra) * flags.astype(jnp.float32)[:, :, None, None, None]
    n_win = lax.axis_size(WIN)
    factors = lag_factors(bins, NLAG)
    me = lax.axis_index(STA)
    slots = source_slots[:, None, :, None, None, None]
    picked_all = jnp.zeros((STEPS,) + weighted.shape, weighted.dtype)
    for k in range(weighted.shape[1]):
        picked_all = jnp.where(slots == k, weighted[None, :, k : k + 1], picked_all)
    picked_all = jnp.where((me == owners)[:, None, None, None, None, None], picked_all, 0.0)
    split = (lax.axis_size("x"), lax.axis_size("y"), -1, 128)
    picked_all = bcast(picked_all.reshape(split)).reshape(picked_all.shape)
    shape = weighted.shape
    rec = weighted.transpose(0, 2, 1, 3, 4).reshape(shape[0], 2, shape[1] * shape[3], shape[4])
    stacked = correlate_all(picked_all, rec, factors, win_count * n_win).reshape(
        STEPS, shape[1], shape[3], shape[1], shape[3], NLAG
    )
    return win_sum(stacked.reshape(-1, NLAG)).reshape(stacked.shape)


def solution(mesh):
    fine = fine_mesh(mesh)
    return jax.shard_map(
        on_device,
        mesh=fine,
        in_specs=(P(WIN, STA, None, None, None), P(WIN, STA), P(), P()),
        out_specs=P(None, None, None, STA, None, None),
        check_vma=False,
    )
```

```python
import functools
import math

import jax
import jax.numpy as jnp
from jax import lax
from jax.experimental import pallas as pl
from jax.experimental.pallas import tpu as pltpu
from jax.sharding import Mesh
from jax.sharding import PartitionSpec as P

NLAG = 768
STEPS = 4
MESH_ID = pl.DeviceIdType.MESH
STA = ("y", "x", "zh")
WIN = ("zl", "c")


def fine_mesh(mesh):
    devs = mesh.devices
    n_sta, n_win = devs.shape
    col = devs[:, 0]
    ny = len({d.coords[1] for d in col})
    nx = len({d.coords[0] for d in col})
    nzh = n_sta // (ny * nx)
    nc = len({d.core_on_chip for d in devs[0, :]})
    nzl = n_win // nc
    return Mesh(devs.reshape(ny, nx, nzh, nzl, nc), STA + WIN)


def whiten(spectra):
    shape = spectra.shape
    blocks = spectra.reshape(shape[0], shape[1], 2, 3, shape[4] // 64, 64)
    power = jnp.mean(blocks * blocks, axis=(2, 3, 5), keepdims=True)
    return (blocks / jnp.sqrt(power + 1e-06)).reshape(shape)


def lag_factors(bins, lags):
    shift = jnp.arange(lags, dtype=jnp.int32) - lags // 2
    hi = jnp.arange(bins // 64, dtype=jnp.int32) * 64 + 360
    lo = jnp.arange(64, dtype=jnp.int32)
    unit = 2.0 * math.pi / 7200.0
    a = jnp.mod(hi[:, None] * shift[None, :], 7200).astype(jnp.float32) * unit
    b = jnp.mod(lo[:, None] * shift[None, :], 7200).astype(jnp.float32) * unit
    return jnp.cos(a), jnp.sin(a), jnp.cos(b), jnp.sin(b)


def corr_kernel(scale, src_ref, rec_ref, ca_ref, sa_ref, cb_ref, sb_ref, out_ref, rows_ref, tab_ref):
    n_win = src_ref.shape[1]
    n_src = src_ref.shape[2]
    n_cmp = src_ref.shape[4]
    n_rows = rec_ref.shape[2]

    @pl.when(pl.program_id(0) == 0)
    def _():
        cb = cb_ref[...]
        sb = sb_ref[...]
        step = cb_ref.shape[0]
        for f1 in range(ca_ref.shape[0]):
            ca = ca_ref[pl.ds(f1, 1), :]
            sa = sa_ref[pl.ds(f1, 1), :]
            rows = pl.ds(f1 * step, step)
            tab_ref[0, rows, :] = ((ca * cb - sa * sb) * scale).astype(jnp.bfloat16)
            tab_ref[1, rows, :] = (-((sa * cb + ca * sb) * scale)).astype(jnp.bfloat16)

    for s in range(n_src):
        for i in range(n_cmp):
            acc_re = None
            acc_im = None
            for w in range(n_win):
                sre = src_ref[0, w, s, 0, pl.ds(i, 1), :]
                sim = src_ref[0, w, s, 1, pl.ds(i, 1), :]
                rre = rec_ref[w, 0]
                rim = rec_ref[w, 1]
                re = sre * rre + sim * rim
                im = sim * rre - sre * rim
                acc_re = re if acc_re is None else acc_re + re
                acc_im = im if acc_im is None else acc_im + im
            row = (s * n_cmp + i) * n_rows
            rows_ref[0, pl.ds(row, n_rows), :] = acc_re.astype(jnp.bfloat16)
            rows_ref[1, pl.ds(row, n_rows), :] = acc_im.astype(jnp.bfloat16)
    out_ref[0] = jnp.dot(rows_ref[0], tab_ref[0], preferred_element_type=jnp.float32) + jnp.dot(
        rows_ref[1], tab_ref[1], preferred_element_type=jnp.float32
    )


def correlate_all(picked_all, rec, factors, windows):
    steps, n_win, n_src, _, n_cmp, bins = picked_all.shape
    n_rows = rec.shape[2]
    lags = NLAG
    m = n_src * n_cmp * n_rows
    scale = 1.0 / math.sqrt(windows * bins)
    whole = lambda t: (0, 0)
    return pl.pallas_call(
        functools.partial(corr_kernel, scale),
        grid=(steps,),
        in_specs=[
            pl.BlockSpec((1, n_win, n_src, 2, n_cmp, bins), lambda t: (t, 0, 0, 0, 0, 0)),
            pl.BlockSpec(rec.shape, lambda t: (0, 0, 0, 0)),
        ]
        + [pl.BlockSpec(f.shape, whole) for f in factors],
        out_specs=pl.BlockSpec((1, m, lags), lambda t: (t, 0, 0)),
        out_shape=jax.ShapeDtypeStruct((steps, m, lags), jnp.float32),
        scratch_shapes=[
            pltpu.VMEM((2, m, bins), jnp.bfloat16),
            pltpu.VMEM((2, bins, lags), jnp.bfloat16),
        ],
    )(picked_all, rec, *factors)


def win_sum_kernel(x_ref, out_ref, a1, a2, r1, r2, r3, send_sem, recv_sem):
    rows = x_ref.shape[0]
    h, q, e = rows // 2, rows // 4, rows // 8
    coords = [lax.axis_index(a) for a in STA + WIN]
    zl, c = coords[3], coords[4]
    b1 = zl % 2
    b2 = zl // 2
    peer_c = tuple(coords[:4]) + (1 - c,)
    peer_1 = tuple(coords[:3]) + (zl + 1 - 2 * b1, c)
    peer_2 = tuple(coords[:3]) + (zl + 2 - 4 * b2, c)

    barrier = pltpu.get_barrier_semaphore()
    for peer in (peer_c, peer_1, peer_2):
        pl.semaphore_signal(barrier, inc=1, device_id=peer, device_id_type=MESH_ID)
    pl.semaphore_wait(barrier, 3)

    def copy(src, dst, k, peer):
        return pltpu.make_async_remote_copy(
            src_ref=src, dst_ref=dst, send_sem=send_sem.at[k], recv_sem=recv_sem.at[k],
            device_id=peer, device_id_type=MESH_ID)

    mine1 = pl.multiple_of(c * h, 8)
    other1 = pl.multiple_of((1 - c) * h, 8)
    mine2 = pl.multiple_of(b1 * q, 8)
    other2 = pl.multiple_of((1 - b1) * q, 8)
    mine3 = pl.multiple_of(b2 * e, 8)
    other3 = pl.multiple_of((1 - b2) * e, 8)
    base_q = pl.multiple_of(mine1 + mine2, 8)
    at_e = pl.multiple_of(base_q + mine3, 8)
    n_chunks = send_sem.shape[0] // 6
    width = x_ref.shape[1] // n_chunks

    def stages(j):
        cols = pl.ds(j * width, width)
        k = 6 * j

        def run(src, dst, i, peer):
            cp = copy(src, dst, k + i, peer)
            cp.start()
            return cp

        cp = run(x_ref.at[pl.ds(other1, h), cols], r1.at[:, cols], 0, peer_c)
        yield
        cp.wait()
        a1[:, cols] = x_ref[pl.ds(mine1, h), cols] + r1[:, cols]
        cp = run(a1.at[pl.ds(other2, q), cols], r2.at[:, cols], 1, peer_1)
        yield
        cp.wait()
        a2[:, cols] = a1[pl.ds(mine2, q), cols] + r2[:, cols]
        cp = run(a2.at[pl.ds(other3, e), cols], r3.at[:, cols], 2, peer_2)
        yield
        cp.wait()
        out_ref[pl.ds(at_e, e), cols] = a2[pl.ds(mine3, e), cols] + r3[:, cols]
        cp = run(out_ref.at[pl.ds(at_e, e), cols], out_ref.at[pl.ds(at_e, e), cols], 3, peer_2)
        yield
        cp.wait()
        cp = run(out_ref.at[pl.ds(base_q, q), cols], out_ref.at[pl.ds(base_q, q), cols], 4, peer_1)
        yield
        cp.wait()
        cp = run(out_ref.at[pl.ds(mine1, h), cols], out_ref.at[pl.ds(mine1, h), cols], 5, peer_c)
        yield
        cp.wait()

    live = [stages(j) for j in range(n_chunks)]
    next(live[0])
    started = 1
    while live:
        if started < len(live):
            next(live[started])
            started += 1
        for g in list(live[:started]):
            try:
                next(g)
            except StopIteration:
                live.remove(g)
                started -= 1


def win_sum(x):
    rows, cols = x.shape
    return pl.pallas_call(
        win_sum_kernel,
        out_shape=jax.ShapeDtypeStruct((rows, cols), jnp.float32),
        in_specs=[pl.BlockSpec(memory_space=pltpu.VMEM)],
        out_specs=pl.BlockSpec(memory_space=pltpu.VMEM),
        scratch_shapes=[
            pltpu.VMEM((rows // 2, cols), jnp.float32),
            pltpu.VMEM((rows // 4, cols), jnp.float32),
            pltpu.VMEM((rows // 2, cols), jnp.float32),
            pltpu.VMEM((rows // 4, cols), jnp.float32),
            pltpu.VMEM((rows // 8, cols), jnp.float32),
            pltpu.SemaphoreType.DMA((36,)),
            pltpu.SemaphoreType.DMA((36,)),
        ],
        compiler_params=pltpu.CompilerParams(collective_id=0, has_side_effects=True),
    )(x)


def bcast_kernel(m_ref, out_ref, rx, s1, ry, piece, zr, sx, rxs, sy, rys, agy_s, agy_r, agx_s, agx_r, zsem):
    nx, ny = m_ref.shape[0], m_ref.shape[1]
    y, x, zh, zl, c = (lax.axis_index(a) for a in STA + WIN)
    xpeer = lambda p: (y, p, zh, zl, c)
    ypeer = lambda p: (p, x, zh, zl, c)
    zpeer = (y, x, 1 - zh, zl, c)

    barrier = pltpu.get_barrier_semaphore()
    for d in range(1, nx):
        pl.semaphore_signal(barrier, inc=1, device_id=xpeer((x + d) % nx), device_id_type=MESH_ID)
    for d in range(1, ny):
        pl.semaphore_signal(barrier, inc=1, device_id=ypeer((y + d) % ny), device_id_type=MESH_ID)
    pl.semaphore_signal(barrier, inc=1, device_id=zpeer, device_id_type=MESH_ID)
    pl.semaphore_wait(barrier, nx + ny - 1)

    def remote(src, dst, ssem, rsem, k, peer):
        cp = pltpu.make_async_remote_copy(
            src_ref=src, dst_ref=dst, send_sem=ssem.at[k], recv_sem=rsem.at[k],
            device_id=peer, device_id_type=MESH_ID)
        cp.start()
        return cp

    order = list(range(1, ny)) + [0]
    rs_x = {}
    for d in order:
        row = (y + d) % ny
        rs_x[d] = [
            remote(m_ref.at[(x + dx) % nx, row], rx.at[x, row], sx, rxs, d * nx + dx, xpeer((x + dx) % nx))
            for dx in range(1, nx)
        ]
    rs_y = []
    for d in order:
        row = (y + d) % ny
        for cp in rs_x[d]:
            cp.wait()
        total = m_ref[x, row]
        for dx in range(1, nx):
            total = total + rx[(x + nx - dx) % nx, row]
        if d == 0:
            part = total
        else:
            s1[row] = total
            rs_y.append(remote(s1.at[row], ry.at[y], sy, rys, d, ypeer(row)))
    for cp in rs_y:
        cp.wait()
    for d in range(1, ny):
        part = part + ry[(y + ny - d) % ny]
    piece[...] = part

    cp = pltpu.make_async_remote_copy(
        src_ref=piece, dst_ref=zr, send_sem=zsem.at[0], recv_sem=zsem.at[1],
        device_id=zpeer, device_id_type=MESH_ID)
    cp.start()
    cp.wait()
    out_ref[x, y] = piece[...] + zr[...]

    ag_y = {d: remote(out_ref.at[x, y], out_ref.at[x, y], agy_s, agy_r, d, ypeer((y + d) % ny)) for d in range(1, ny)}
    ag_x = []
    for d in [0] + list(range(1, ny)):
        if d:
            ag_y[d].wait()
        row = (y + ny - d) % ny
        for dx in range(1, nx):
            ag_x.append(remote(out_ref.at[x, row], out_ref.at[x, row], agx_s, agx_r, d * nx + dx, xpeer((x + dx) % nx)))
    for cp in ag_x:
        cp.wait()


def bcast(masked):
    shape = masked.shape
    nx, ny = shape[0], shape[1]
    return pl.pallas_call(
        bcast_kernel,
        out_shape=jax.ShapeDtypeStruct(shape, jnp.float32),
        in_specs=[pl.BlockSpec(memory_space=pltpu.VMEM)],
        out_specs=pl.BlockSpec(memory_space=pltpu.VMEM),
        scratch_shapes=[
            pltpu.VMEM(shape, jnp.float32),
            pltpu.VMEM(shape[1:], jnp.float32),
            pltpu.VMEM(shape[1:], jnp.float32),
            pltpu.VMEM(shape[2:], jnp.float32),
            pltpu.VMEM(shape[2:], jnp.float32),
            pltpu.SemaphoreType.DMA((nx * ny,)),
            pltpu.SemaphoreType.DMA((nx * ny,)),
            pltpu.SemaphoreType.DMA((ny,)),
            pltpu.SemaphoreType.DMA((ny,)),
            pltpu.SemaphoreType.DMA((ny,)),
            pltpu.SemaphoreType.DMA((ny,)),
            pltpu.SemaphoreType.DMA((nx * ny,)),
            pltpu.SemaphoreType.DMA((nx * ny,)),
            pltpu.SemaphoreType.DMA((2,)),
        ],
        compiler_params=pltpu.CompilerParams(collective_id=1, has_side_effects=True),
    )(masked)


def on_device(spectra, flags, owners, source_slots):
    win_count = spectra.shape[0]
    bins = spectra.shape[4]
    weighted = whiten(spectra) * flags.astype(jnp.float32)[:, :, None, None, None]
    n_win = lax.axis_size(WIN)
    factors = lag_factors(bins, NLAG)
    me = lax.axis_index(STA)
    slots = source_slots[:, None, :, None, None, None]
    picked_all = jnp.zeros((STEPS,) + weighted.shape, weighted.dtype)
    for k in range(weighted.shape[1]):
        picked_all = jnp.where(slots == k, weighted[None, :, k : k + 1], picked_all)
    picked_all = jnp.where((me == owners)[:, None, None, None, None, None], picked_all, 0.0)
    split = (lax.axis_size("x"), lax.axis_size("y"), -1, 128)
    picked_all = bcast(picked_all.reshape(split)).reshape(picked_all.shape)
    shape = weighted.shape
    rec = weighted.transpose(0, 2, 1, 3, 4).reshape(shape[0], 2, shape[1] * shape[3], shape[4])
    stacked = correlate_all(picked_all, rec, factors, win_count * n_win).reshape(
        STEPS, shape[1], shape[3], shape[1], shape[3], NLAG
    )
    return win_sum(stacked.reshape(-1, NLAG)).reshape(stacked.shape)


def solution(mesh):
    fine = fine_mesh(mesh)
    return jax.shard_map(
        on_device,
        mesh=fine,
        in_specs=(P(WIN, STA, None, None, None), P(WIN, STA), P(), P()),
        out_specs=P(None, None, None, STA, None, None),
        check_vma=False,
    )
```

```python
import functools
import math

import jax
import jax.numpy as jnp
from jax import lax
from jax.experimental import pallas as pl
from jax.experimental.pallas import tpu as pltpu
from jax.sharding import Mesh
from jax.sharding import PartitionSpec as P

NLAG = 768
STEPS = 4
MESH_ID = pl.DeviceIdType.MESH
STA = ("y", "x", "zh")
WIN = ("zl", "c")


def fine_mesh(mesh):
    devs = mesh.devices
    n_sta, n_win = devs.shape
    col = devs[:, 0]
    ny = len({d.coords[1] for d in col})
    nx = len({d.coords[0] for d in col})
    nzh = n_sta // (ny * nx)
    nc = len({d.core_on_chip for d in devs[0, :]})
    nzl = n_win // nc
    return Mesh(devs.reshape(ny, nx, nzh, nzl, nc), STA + WIN)


def whiten(spectra):
    shape = spectra.shape
    blocks = spectra.reshape(shape[0], shape[1], 2, 3, shape[4] // 64, 64)
    power = jnp.mean(blocks * blocks, axis=(2, 3, 5), keepdims=True)
    return (blocks / jnp.sqrt(power + 1e-06)).reshape(shape)


def lag_factors(bins, lags):
    shift = jnp.arange(lags, dtype=jnp.int32) - lags // 2
    hi = jnp.arange(bins // 64, dtype=jnp.int32) * 64 + 360
    lo = jnp.arange(64, dtype=jnp.int32)
    unit = 2.0 * math.pi / 7200.0
    a = jnp.mod(hi[:, None] * shift[None, :], 7200).astype(jnp.float32) * unit
    b = jnp.mod(lo[:, None] * shift[None, :], 7200).astype(jnp.float32) * unit
    return jnp.cos(a), jnp.sin(a), jnp.cos(b), jnp.sin(b)


def corr_kernel(scale, src_ref, rec_ref, ca_ref, sa_ref, cb_ref, sb_ref, out_ref, rows_ref, tab_ref):
    n_win = src_ref.shape[1]
    n_src = src_ref.shape[2]
    n_cmp = src_ref.shape[4]
    n_rows = rec_ref.shape[2]

    @pl.when(pl.program_id(0) == 0)
    def _():
        cb = cb_ref[...]
        sb = sb_ref[...]
        step = cb_ref.shape[0]
        for f1 in range(ca_ref.shape[0]):
            ca = ca_ref[pl.ds(f1, 1), :]
            sa = sa_ref[pl.ds(f1, 1), :]
            rows = pl.ds(f1 * step, step)
            tab_ref[0, rows, :] = ((ca * cb - sa * sb) * scale).astype(jnp.bfloat16)
            tab_ref[1, rows, :] = (-((sa * cb + ca * sb) * scale)).astype(jnp.bfloat16)

    for s in range(n_src):
        for i in range(n_cmp):
            acc_re = None
            acc_im = None
            for w in range(n_win):
                sre = src_ref[0, w, s, 0, pl.ds(i, 1), :]
                sim = src_ref[0, w, s, 1, pl.ds(i, 1), :]
                rre = rec_ref[w, 0]
                rim = rec_ref[w, 1]
                re = sre * rre + sim * rim
                im = sim * rre - sre * rim
                acc_re = re if acc_re is None else acc_re + re
                acc_im = im if acc_im is None else acc_im + im
            row = (s * n_cmp + i) * n_rows
            rows_ref[0, pl.ds(row, n_rows), :] = acc_re.astype(jnp.bfloat16)
            rows_ref[1, pl.ds(row, n_rows), :] = acc_im.astype(jnp.bfloat16)
    out_ref[0] = jnp.dot(rows_ref[0], tab_ref[0], preferred_element_type=jnp.float32) + jnp.dot(
        rows_ref[1], tab_ref[1], preferred_element_type=jnp.float32
    )


def correlate_all(picked_all, rec, factors, windows):
    steps, n_win, n_src, _, n_cmp, bins = picked_all.shape
    n_rows = rec.shape[2]
    lags = NLAG
    m = n_src * n_cmp * n_rows
    scale = 1.0 / math.sqrt(windows * bins)
    whole = lambda t: (0, 0)
    return pl.pallas_call(
        functools.partial(corr_kernel, scale),
        grid=(steps,),
        in_specs=[
            pl.BlockSpec((1, n_win, n_src, 2, n_cmp, bins), lambda t: (t, 0, 0, 0, 0, 0)),
            pl.BlockSpec(rec.shape, lambda t: (0, 0, 0, 0)),
        ]
        + [pl.BlockSpec(f.shape, whole) for f in factors],
        out_specs=pl.BlockSpec((1, m, lags), lambda t: (t, 0, 0)),
        out_shape=jax.ShapeDtypeStruct((steps, m, lags), jnp.float32),
        scratch_shapes=[
            pltpu.VMEM((2, m, bins), jnp.bfloat16),
            pltpu.VMEM((2, bins, lags), jnp.bfloat16),
        ],
    )(picked_all, rec, *factors)


def win_sum_kernel(x_ref, out_ref, a1, a2, r1, r2, r3, send_sem, recv_sem):
    rows = x_ref.shape[0]
    h, q, e = rows // 2, rows // 4, rows // 8
    coords = [lax.axis_index(a) for a in STA + WIN]
    zl, c = coords[3], coords[4]
    b1 = zl % 2
    b2 = zl // 2
    peer_c = tuple(coords[:4]) + (1 - c,)
    peer_1 = tuple(coords[:3]) + (zl + 1 - 2 * b1, c)
    peer_2 = tuple(coords[:3]) + (zl + 2 - 4 * b2, c)

    barrier = pltpu.get_barrier_semaphore()
    for peer in (peer_c, peer_1, peer_2):
        pl.semaphore_signal(barrier, inc=1, device_id=peer, device_id_type=MESH_ID)
    pl.semaphore_wait(barrier, 3)

    def copy(src, dst, k, peer):
        return pltpu.make_async_remote_copy(
            src_ref=src, dst_ref=dst, send_sem=send_sem.at[k], recv_sem=recv_sem.at[k],
            device_id=peer, device_id_type=MESH_ID)

    mine1 = pl.multiple_of(c * h, 8)
    other1 = pl.multiple_of((1 - c) * h, 8)
    mine2 = pl.multiple_of(b1 * q, 8)
    other2 = pl.multiple_of((1 - b1) * q, 8)
    mine3 = pl.multiple_of(b2 * e, 8)
    other3 = pl.multiple_of((1 - b2) * e, 8)
    base_q = pl.multiple_of(mine1 + mine2, 8)
    at_e = pl.multiple_of(base_q + mine3, 8)
    n_chunks = send_sem.shape[0] // 6
    width = x_ref.shape[1] // n_chunks

    def stages(j):
        cols = pl.ds(j * width, width)
        k = 6 * j

        def run(src, dst, i, peer):
            cp = copy(src, dst, k + i, peer)
            cp.start()
            return cp

        cp = run(x_ref.at[pl.ds(other1, h), cols], r1.at[:, cols], 0, peer_c)
        yield
        cp.wait()
        a1[:, cols] = x_ref[pl.ds(mine1, h), cols] + r1[:, cols]
        cp = run(a1.at[pl.ds(other2, q), cols], r2.at[:, cols], 1, peer_1)
        yield
        cp.wait()
        a2[:, cols] = a1[pl.ds(mine2, q), cols] + r2[:, cols]
        cp = run(a2.at[pl.ds(other3, e), cols], r3.at[:, cols], 2, peer_2)
        yield
        cp.wait()
        out_ref[pl.ds(at_e, e), cols] = a2[pl.ds(mine3, e), cols] + r3[:, cols]
        cp = run(out_ref.at[pl.ds(at_e, e), cols], out_ref.at[pl.ds(at_e, e), cols], 3, peer_2)
        yield
        cp.wait()
        cp = run(out_ref.at[pl.ds(base_q, q), cols], out_ref.at[pl.ds(base_q, q), cols], 4, peer_1)
        yield
        cp.wait()
        cp = run(out_ref.at[pl.ds(mine1, h), cols], out_ref.at[pl.ds(mine1, h), cols], 5, peer_c)
        yield
        cp.wait()

    live = [stages(j) for j in range(n_chunks)]
    next(live[0])
    started = 1
    while live:
        if started < len(live):
            next(live[started])
            started += 1
        for g in list(live[:started]):
            try:
                next(g)
            except StopIteration:
                live.remove(g)
                started -= 1


def win_sum(x):
    rows, cols = x.shape
    return pl.pallas_call(
        win_sum_kernel,
        out_shape=jax.ShapeDtypeStruct((rows, cols), jnp.float32),
        in_specs=[pl.BlockSpec(memory_space=pltpu.VMEM)],
        out_specs=pl.BlockSpec(memory_space=pltpu.VMEM),
        scratch_shapes=[
            pltpu.VMEM((rows // 2, cols), jnp.float32),
            pltpu.VMEM((rows // 4, cols), jnp.float32),
            pltpu.VMEM((rows // 2, cols), jnp.float32),
            pltpu.VMEM((rows // 4, cols), jnp.float32),
            pltpu.VMEM((rows // 8, cols), jnp.float32),
            pltpu.SemaphoreType.DMA((18,)),
            pltpu.SemaphoreType.DMA((18,)),
        ],
        compiler_params=pltpu.CompilerParams(collective_id=0, has_side_effects=True),
    )(x)


def bcast_kernel(m_ref, out_ref, rx, s1, ry, piece, zr, sx, rxs, sy, rys, agy_s, agy_r, agx_s, agx_r, zsem):
    nx, ny = m_ref.shape[0], m_ref.shape[1]
    y, x, zh, zl, c = (lax.axis_index(a) for a in STA + WIN)
    xpeer = lambda p: (y, p, zh, zl, c)
    ypeer = lambda p: (p, x, zh, zl, c)
    zpeer = (y, x, 1 - zh, zl, c)

    barrier = pltpu.get_barrier_semaphore()
    for d in range(1, nx):
        pl.semaphore_signal(barrier, inc=1, device_id=xpeer((x + d) % nx), device_id_type=MESH_ID)
    for d in range(1, ny):
        pl.semaphore_signal(barrier, inc=1, device_id=ypeer((y + d) % ny), device_id_type=MESH_ID)
    pl.semaphore_signal(barrier, inc=1, device_id=zpeer, device_id_type=MESH_ID)
    pl.semaphore_wait(barrier, nx + ny - 1)

    def remote(src, dst, ssem, rsem, k, peer):
        cp = pltpu.make_async_remote_copy(
            src_ref=src, dst_ref=dst, send_sem=ssem.at[k], recv_sem=rsem.at[k],
            device_id=peer, device_id_type=MESH_ID)
        cp.start()
        return cp

    order = list(range(1, ny)) + [0]
    rs_x = {}

    def start_row(i):
        d = order[i]
        row = (y + d) % ny
        rs_x[d] = [
            remote(m_ref.at[(x + dx) % nx, row], rx.at[x, row], sx, rxs, d * nx + dx, xpeer((x + dx) % nx))
            for dx in range(1, nx)
        ]

    ahead = 2
    for i in range(min(ahead, ny)):
        start_row(i)
    rs_y = []
    for i, d in enumerate(order):
        if i + ahead < ny:
            start_row(i + ahead)
        row = (y + d) % ny
        for cp in rs_x[d]:
            cp.wait()
        total = m_ref[x, row]
        for dx in range(1, nx):
            total = total + rx[(x + nx - dx) % nx, row]
        if d == 0:
            part = total
        else:
            s1[row] = total
            rs_y.append(remote(s1.at[row], ry.at[y], sy, rys, d, ypeer(row)))
    for cp in rs_y:
        cp.wait()
    for d in range(1, ny):
        part = part + ry[(y + ny - d) % ny]
    piece[...] = part

    cp = pltpu.make_async_remote_copy(
        src_ref=piece, dst_ref=zr, send_sem=zsem.at[0], recv_sem=zsem.at[1],
        device_id=zpeer, device_id_type=MESH_ID)
    cp.start()
    cp.wait()
    out_ref[x, y] = piece[...] + zr[...]

    ag_y = {d: remote(out_ref.at[x, y], out_ref.at[x, y], agy_s, agy_r, d, ypeer((y + d) % ny)) for d in range(1, ny)}
    ag_x = []
    for d in [0] + list(range(1, ny)):
        if d:
            ag_y[d].wait()
        row = (y + ny - d) % ny
        for dx in range(1, nx):
            ag_x.append(remote(out_ref.at[x, row], out_ref.at[x, row], agx_s, agx_r, d * nx + dx, xpeer((x + dx) % nx)))
    for cp in ag_x:
        cp.wait()


def bcast(masked):
    shape = masked.shape
    nx, ny = shape[0], shape[1]
    return pl.pallas_call(
        bcast_kernel,
        out_shape=jax.ShapeDtypeStruct(shape, jnp.float32),
        in_specs=[pl.BlockSpec(memory_space=pltpu.VMEM)],
        out_specs=pl.BlockSpec(memory_space=pltpu.VMEM),
        scratch_shapes=[
            pltpu.VMEM(shape, jnp.float32),
            pltpu.VMEM(shape[1:], jnp.float32),
            pltpu.VMEM(shape[1:], jnp.float32),
            pltpu.VMEM(shape[2:], jnp.float32),
            pltpu.VMEM(shape[2:], jnp.float32),
            pltpu.SemaphoreType.DMA((nx * ny,)),
            pltpu.SemaphoreType.DMA((nx * ny,)),
            pltpu.SemaphoreType.DMA((ny,)),
            pltpu.SemaphoreType.DMA((ny,)),
            pltpu.SemaphoreType.DMA((ny,)),
            pltpu.SemaphoreType.DMA((ny,)),
            pltpu.SemaphoreType.DMA((nx * ny,)),
            pltpu.SemaphoreType.DMA((nx * ny,)),
            pltpu.SemaphoreType.DMA((2,)),
        ],
        compiler_params=pltpu.CompilerParams(collective_id=1, has_side_effects=True),
    )(masked)


def on_device(spectra, flags, owners, source_slots):
    win_count = spectra.shape[0]
    bins = spectra.shape[4]
    weighted = whiten(spectra) * flags.astype(jnp.float32)[:, :, None, None, None]
    n_win = lax.axis_size(WIN)
    factors = lag_factors(bins, NLAG)
    me = lax.axis_index(STA)
    slots = source_slots[:, None, :, None, None, None]
    picked_all = jnp.zeros((STEPS,) + weighted.shape, weighted.dtype)
    for k in range(weighted.shape[1]):
        picked_all = jnp.where(slots == k, weighted[None, :, k : k + 1], picked_all)
    picked_all = jnp.where((me == owners)[:, None, None, None, None, None], picked_all, 0.0)
    split = (lax.axis_size("x"), lax.axis_size("y"), -1, 128)
    picked_all = bcast(picked_all.reshape(split)).reshape(picked_all.shape)
    shape = weighted.shape
    rec = weighted.transpose(0, 2, 1, 3, 4).reshape(shape[0], 2, shape[1] * shape[3], shape[4])
    stacked = correlate_all(picked_all, rec, factors, win_count * n_win).reshape(
        STEPS, shape[1], shape[3], shape[1], shape[3], NLAG
    )
    return win_sum(stacked.reshape(-1, NLAG)).reshape(stacked.shape)


def solution(mesh):
    fine = fine_mesh(mesh)
    return jax.shard_map(
        on_device,
        mesh=fine,
        in_specs=(P(WIN, STA, None, None, None), P(WIN, STA), P(), P()),
        out_specs=P(None, None, None, STA, None, None),
        check_vma=False,
    )
```

```python
import functools
import math

import jax
import jax.numpy as jnp
from jax import lax
from jax.experimental import pallas as pl
from jax.experimental.pallas import tpu as pltpu
from jax.sharding import Mesh
from jax.sharding import PartitionSpec as P

NLAG = 768
STEPS = 4
MESH_ID = pl.DeviceIdType.MESH
STA = ("y", "x", "zh")
WIN = ("zl", "c")


def fine_mesh(mesh):
    devs = mesh.devices
    n_sta, n_win = devs.shape
    col = devs[:, 0]
    ny = len({d.coords[1] for d in col})
    nx = len({d.coords[0] for d in col})
    nzh = n_sta // (ny * nx)
    nc = len({d.core_on_chip for d in devs[0, :]})
    nzl = n_win // nc
    return Mesh(devs.reshape(ny, nx, nzh, nzl, nc), STA + WIN)


def whiten(spectra):
    shape = spectra.shape
    blocks = spectra.reshape(shape[0], shape[1], 2, 3, shape[4] // 64, 64)
    power = jnp.mean(blocks * blocks, axis=(2, 3, 5), keepdims=True)
    return (blocks / jnp.sqrt(power + 1e-06)).reshape(shape)


def lag_factors(bins, lags):
    shift = jnp.arange(lags, dtype=jnp.int32) - lags // 2
    hi = jnp.arange(bins // 64, dtype=jnp.int32) * 64 + 360
    lo = jnp.arange(64, dtype=jnp.int32)
    unit = 2.0 * math.pi / 7200.0
    a = jnp.mod(hi[:, None] * shift[None, :], 7200).astype(jnp.float32) * unit
    b = jnp.mod(lo[:, None] * shift[None, :], 7200).astype(jnp.float32) * unit
    return jnp.cos(a), jnp.sin(a), jnp.cos(b), jnp.sin(b)


def corr_kernel(scale, src_ref, rec_ref, ca_ref, sa_ref, cb_ref, sb_ref, out_ref, rows_ref, tab_ref):
    n_win = src_ref.shape[1]
    n_src = src_ref.shape[2]
    n_cmp = src_ref.shape[4]
    n_rows = rec_ref.shape[2]

    @pl.when(pl.program_id(0) == 0)
    def _():
        cb = cb_ref[...]
        sb = sb_ref[...]
        step = cb_ref.shape[0]
        for f1 in range(ca_ref.shape[0]):
            ca = ca_ref[pl.ds(f1, 1), :]
            sa = sa_ref[pl.ds(f1, 1), :]
            rows = pl.ds(f1 * step, step)
            tab_ref[0, rows, :] = ((ca * cb - sa * sb) * scale).astype(jnp.bfloat16)
            tab_ref[1, rows, :] = (-((sa * cb + ca * sb) * scale)).astype(jnp.bfloat16)

    for s in range(n_src):
        for i in range(n_cmp):
            acc_re = None
            acc_im = None
            for w in range(n_win):
                sre = src_ref[0, w, s, 0, pl.ds(i, 1), :]
                sim = src_ref[0, w, s, 1, pl.ds(i, 1), :]
                rre = rec_ref[w, 0]
                rim = rec_ref[w, 1]
                re = sre * rre + sim * rim
                im = sim * rre - sre * rim
                acc_re = re if acc_re is None else acc_re + re
                acc_im = im if acc_im is None else acc_im + im
            row = (s * n_cmp + i) * n_rows
            rows_ref[0, pl.ds(row, n_rows), :] = acc_re.astype(jnp.bfloat16)
            rows_ref[1, pl.ds(row, n_rows), :] = acc_im.astype(jnp.bfloat16)
    out_ref[0] = jnp.dot(rows_ref[0], tab_ref[0], preferred_element_type=jnp.float32) + jnp.dot(
        rows_ref[1], tab_ref[1], preferred_element_type=jnp.float32
    )


def correlate_all(picked_all, rec, factors, windows):
    steps, n_win, n_src, _, n_cmp, bins = picked_all.shape
    n_rows = rec.shape[2]
    lags = NLAG
    m = n_src * n_cmp * n_rows
    scale = 1.0 / math.sqrt(windows * bins)
    whole = lambda t: (0, 0)
    return pl.pallas_call(
        functools.partial(corr_kernel, scale),
        grid=(steps,),
        in_specs=[
            pl.BlockSpec((1, n_win, n_src, 2, n_cmp, bins), lambda t: (t, 0, 0, 0, 0, 0)),
            pl.BlockSpec(rec.shape, lambda t: (0, 0, 0, 0)),
        ]
        + [pl.BlockSpec(f.shape, whole) for f in factors],
        out_specs=pl.BlockSpec((1, m, lags), lambda t: (t, 0, 0)),
        out_shape=jax.ShapeDtypeStruct((steps, m, lags), jnp.float32),
        scratch_shapes=[
            pltpu.VMEM((2, m, bins), jnp.bfloat16),
            pltpu.VMEM((2, bins, lags), jnp.bfloat16),
        ],
    )(picked_all, rec, *factors)


def win_sum_kernel(x_ref, out_ref, a1, a2, r1, r2, r3, send_sem, recv_sem):
    rows = x_ref.shape[0]
    h, q, e = rows // 2, rows // 4, rows // 8
    coords = [lax.axis_index(a) for a in STA + WIN]
    zl, c = coords[3], coords[4]
    b1 = zl % 2
    b2 = zl // 2
    peer_c = tuple(coords[:4]) + (1 - c,)
    peer_1 = tuple(coords[:3]) + (zl + 1 - 2 * b1, c)
    peer_2 = tuple(coords[:3]) + (zl + 2 - 4 * b2, c)

    barrier = pltpu.get_barrier_semaphore()
    for peer in (peer_c, peer_1, peer_2):
        pl.semaphore_signal(barrier, inc=1, device_id=peer, device_id_type=MESH_ID)
    pl.semaphore_wait(barrier, 3)

    def copy(src, dst, k, peer):
        return pltpu.make_async_remote_copy(
            src_ref=src, dst_ref=dst, send_sem=send_sem.at[k], recv_sem=recv_sem.at[k],
            device_id=peer, device_id_type=MESH_ID)

    mine1 = pl.multiple_of(c * h, 8)
    other1 = pl.multiple_of((1 - c) * h, 8)
    mine2 = pl.multiple_of(b1 * q, 8)
    other2 = pl.multiple_of((1 - b1) * q, 8)
    mine3 = pl.multiple_of(b2 * e, 8)
    other3 = pl.multiple_of((1 - b2) * e, 8)
    base_q = pl.multiple_of(mine1 + mine2, 8)
    at_e = pl.multiple_of(base_q + mine3, 8)
    n_chunks = send_sem.shape[0] // 6
    width = x_ref.shape[1] // n_chunks

    def stages(j):
        cols = pl.ds(j * width, width)
        k = 6 * j

        def run(src, dst, i, peer):
            cp = copy(src, dst, k + i, peer)
            cp.start()
            return cp

        cp = run(x_ref.at[pl.ds(other1, h), cols], r1.at[:, cols], 0, peer_c)
        yield
        cp.wait()
        a1[:, cols] = x_ref[pl.ds(mine1, h), cols] + r1[:, cols]
        cp = run(a1.at[pl.ds(other2, q), cols], r2.at[:, cols], 1, peer_1)
        yield
        cp.wait()
        a2[:, cols] = a1[pl.ds(mine2, q), cols] + r2[:, cols]
        cp = run(a2.at[pl.ds(other3, e), cols], r3.at[:, cols], 2, peer_2)
        yield
        cp.wait()
        out_ref[pl.ds(at_e, e), cols] = a2[pl.ds(mine3, e), cols] + r3[:, cols]
        cp = run(out_ref.at[pl.ds(at_e, e), cols], out_ref.at[pl.ds(at_e, e), cols], 3, peer_2)
        yield
        cp.wait()
        cp = run(out_ref.at[pl.ds(base_q, q), cols], out_ref.at[pl.ds(base_q, q), cols], 4, peer_1)
        yield
        cp.wait()
        cp = run(out_ref.at[pl.ds(mine1, h), cols], out_ref.at[pl.ds(mine1, h), cols], 5, peer_c)
        yield
        cp.wait()

    live = [stages(j) for j in range(n_chunks)]
    next(live[0])
    started = 1
    while live:
        if started < len(live):
            next(live[started])
            started += 1
        for g in list(live[:started]):
            try:
                next(g)
            except StopIteration:
                live.remove(g)
                started -= 1


def win_sum(x):
    rows, cols = x.shape
    return pl.pallas_call(
        win_sum_kernel,
        out_shape=jax.ShapeDtypeStruct((rows, cols), jnp.float32),
        in_specs=[pl.BlockSpec(memory_space=pltpu.VMEM)],
        out_specs=pl.BlockSpec(memory_space=pltpu.VMEM),
        scratch_shapes=[
            pltpu.VMEM((rows // 2, cols), jnp.float32),
            pltpu.VMEM((rows // 4, cols), jnp.float32),
            pltpu.VMEM((rows // 2, cols), jnp.float32),
            pltpu.VMEM((rows // 4, cols), jnp.float32),
            pltpu.VMEM((rows // 8, cols), jnp.float32),
            pltpu.SemaphoreType.DMA((18,)),
            pltpu.SemaphoreType.DMA((18,)),
        ],
        compiler_params=pltpu.CompilerParams(collective_id=0, has_side_effects=True),
    )(x)


def bcast_kernel(m_ref, out_ref, rx, s1, ry, piece, zr, sx, rxs, sy, rys, agy_s, agy_r, agx_s, agx_r, zsem):
    nx, ny = m_ref.shape[0], m_ref.shape[1]
    y, x, zh, zl, c = (lax.axis_index(a) for a in STA + WIN)
    xpeer = lambda p: (y, p, zh, zl, c)
    ypeer = lambda p: (p, x, zh, zl, c)
    zpeer = (y, x, 1 - zh, zl, c)

    barrier = pltpu.get_barrier_semaphore()
    for d in range(1, nx):
        pl.semaphore_signal(barrier, inc=1, device_id=xpeer((x + d) % nx), device_id_type=MESH_ID)
    for d in range(1, ny):
        pl.semaphore_signal(barrier, inc=1, device_id=ypeer((y + d) % ny), device_id_type=MESH_ID)
    pl.semaphore_signal(barrier, inc=1, device_id=zpeer, device_id_type=MESH_ID)
    pl.semaphore_wait(barrier, nx + ny - 1)

    def remote(src, dst, ssem, rsem, k, peer):
        cp = pltpu.make_async_remote_copy(
            src_ref=src, dst_ref=dst, send_sem=ssem.at[k], recv_sem=rsem.at[k],
            device_id=peer, device_id_type=MESH_ID)
        cp.start()
        return cp

    order = list(range(1, ny)) + [0]
    rs_x = {}

    def start_row(i):
        d = order[i]
        row = (y + d) % ny
        rs_x[d] = [
            remote(m_ref.at[(x + dx) % nx, row], rx.at[x, row], sx, rxs, d * nx + dx, xpeer((x + dx) % nx))
            for dx in range(1, nx)
        ]

    ahead = 1
    for i in range(min(ahead, ny)):
        start_row(i)
    rs_y = []
    for i, d in enumerate(order):
        if i + ahead < ny:
            start_row(i + ahead)
        row = (y + d) % ny
        for cp in rs_x[d]:
            cp.wait()
        total = m_ref[x, row]
        for dx in range(1, nx):
            total = total + rx[(x + nx - dx) % nx, row]
        if d == 0:
            part = total
        else:
            s1[row] = total
            rs_y.append(remote(s1.at[row], ry.at[y], sy, rys, d, ypeer(row)))
    for cp in rs_y:
        cp.wait()
    for d in range(1, ny):
        part = part + ry[(y + ny - d) % ny]
    piece[...] = part

    cp = pltpu.make_async_remote_copy(
        src_ref=piece, dst_ref=zr, send_sem=zsem.at[0], recv_sem=zsem.at[1],
        device_id=zpeer, device_id_type=MESH_ID)
    cp.start()
    cp.wait()
    out_ref[x, y] = piece[...] + zr[...]

    ag_y = {d: remote(out_ref.at[x, y], out_ref.at[x, y], agy_s, agy_r, d, ypeer((y + d) % ny)) for d in range(1, ny)}
    ag_x = []
    for d in [0] + list(range(1, ny)):
        if d:
            ag_y[d].wait()
        row = (y + ny - d) % ny
        for dx in range(1, nx):
            ag_x.append(remote(out_ref.at[x, row], out_ref.at[x, row], agx_s, agx_r, d * nx + dx, xpeer((x + dx) % nx)))
    for cp in ag_x:
        cp.wait()


def bcast(masked):
    shape = masked.shape
    nx, ny = shape[0], shape[1]
    return pl.pallas_call(
        bcast_kernel,
        out_shape=jax.ShapeDtypeStruct(shape, jnp.float32),
        in_specs=[pl.BlockSpec(memory_space=pltpu.VMEM)],
        out_specs=pl.BlockSpec(memory_space=pltpu.VMEM),
        scratch_shapes=[
            pltpu.VMEM(shape, jnp.float32),
            pltpu.VMEM(shape[1:], jnp.float32),
            pltpu.VMEM(shape[1:], jnp.float32),
            pltpu.VMEM(shape[2:], jnp.float32),
            pltpu.VMEM(shape[2:], jnp.float32),
            pltpu.SemaphoreType.DMA((nx * ny,)),
            pltpu.SemaphoreType.DMA((nx * ny,)),
            pltpu.SemaphoreType.DMA((ny,)),
            pltpu.SemaphoreType.DMA((ny,)),
            pltpu.SemaphoreType.DMA((ny,)),
            pltpu.SemaphoreType.DMA((ny,)),
            pltpu.SemaphoreType.DMA((nx * ny,)),
            pltpu.SemaphoreType.DMA((nx * ny,)),
            pltpu.SemaphoreType.DMA((2,)),
        ],
        compiler_params=pltpu.CompilerParams(collective_id=1, has_side_effects=True),
    )(masked)


def on_device(spectra, flags, owners, source_slots):
    win_count = spectra.shape[0]
    bins = spectra.shape[4]
    weighted = whiten(spectra) * flags.astype(jnp.float32)[:, :, None, None, None]
    n_win = lax.axis_size(WIN)
    factors = lag_factors(bins, NLAG)
    me = lax.axis_index(STA)
    slots = source_slots[:, None, :, None, None, None]
    picked_all = jnp.zeros((STEPS,) + weighted.shape, weighted.dtype)
    for k in range(weighted.shape[1]):
        picked_all = jnp.where(slots == k, weighted[None, :, k : k + 1], picked_all)
    picked_all = jnp.where((me == owners)[:, None, None, None, None, None], picked_all, 0.0)
    split = (lax.axis_size("x"), lax.axis_size("y"), -1, 128)
    picked_all = bcast(picked_all.reshape(split)).reshape(picked_all.shape)
    shape = weighted.shape
    rec = weighted.transpose(0, 2, 1, 3, 4).reshape(shape[0], 2, shape[1] * shape[3], shape[4])
    stacked = correlate_all(picked_all, rec, factors, win_count * n_win).reshape(
        STEPS, shape[1], shape[3], shape[1], shape[3], NLAG
    )
    return win_sum(stacked.reshape(-1, NLAG)).reshape(stacked.shape)


def solution(mesh):
    fine = fine_mesh(mesh)
    return jax.shard_map(
        on_device,
        mesh=fine,
        in_specs=(P(WIN, STA, None, None, None), P(WIN, STA), P(), P()),
        out_specs=P(None, None, None, STA, None, None),
        check_vma=False,
    )
```
